512 devices in a mesh: layer: 32 (over z, y_hi, core), prow: 4 (over x), pcol: 4 (over y_lo).
Axes of the slice: x: 4, y: 8 (y_hi: 2, y_lo: 4; y = y_hi * 4 + y_lo), z: 8, core: 2. Of those that a mesh axis runs over, the one named last changes fastest.
Arguments:
- subtree_right_hand: bfloat16 [32, 6144, 512], P('layer', ('prow', 'pcol')), may hold values from -6 to 6
- root_rhs: bfloat16 [2048, 512], P(('prow', 'pcol')), may hold values from -6 to 6
- blocks: bfloat16 [32, 6, 4, 4, 4, 4, 128, 128], P('layer', None, 'prow', 'pcol'), may hold values from -0.1875 to 0.1875
- pattern: int32 [32, 6, 4, 4, 4, 4], P('layer', None, 'prow', 'pcol'), may hold values 0 or 1
- forest_inverse: float32 [32, 3, 4, 4, 128, 128], P('layer', None, 'prow', 'pcol'), may hold values from -0.5 to 0.5
- root_inverse: float32 [4, 4, 128, 128], P('prow', 'pcol'), may hold values from -0.5 to 0.5
Outputs:
- forest_solution: bfloat16 [32, 6144, 512], P('layer', ('prow', 'pcol'))
- root_solution: bfloat16 [2048, 512], P(('prow', 'pcol'))
The draws below stay inside these ranges and needn't reach their ends.
All inputs are finite; a program needn't handle non-finite values. No bound on the sum of `pattern` on one device may be relied on, other than what follows from the above.
Results may differ from the reference program's by a relative error of at most 0.0057.
Values may be sent and summed in bfloat16 or wider, within the bound.
A program may use at most 64 MiB of HBM per device.

```python
import jax
import jax.numpy as jnp
from jax import lax

SUPER = 128
RHS = 512
PAIRS = 6
GRID = 4
SUBTREE_UNKNOWNS = 6144
ROOT_ROWS = 2048
N_LAYER = 32


def place_ends(drawn, stream_key, low, largest):
    spot = [jax.random.randint(jax.random.fold_in(stream_key, axis), (), 0, length) for axis, length in enumerate(drawn.shape)]
    longest = drawn.shape.index(max(drawn.shape))
    beside = spot[:longest] + [(spot[longest] + 1) % drawn.shape[longest]] + spot[longest + 1:]
    return drawn.at[tuple(spot)].set(low).at[tuple(beside)].set(largest)


def raised(values, key, source, target, shards_of, factor):
    owner, partner = [(jnp.arange(values.shape[position]) // (values.shape[position] // shards_of)).reshape([-1 if axis == position else 1 for axis in range(values.ndim)]) for position in (source, target)]
    chosen = jax.random.permutation(key, shards_of)[partner]
    strong = (owner == chosen) | (owner == (partner + shards_of // 2) % shards_of)
    return jnp.where(strong, factor * values, values)


def block_levels(stream_key, dims, pieces, low, high):
    def one(dim, parts):
        steps = jax.random.uniform(jax.random.fold_in(jax.random.fold_in(stream_key, 6), dim), (parts,), jnp.float32, low / len(pieces), high / len(pieces))
        return jnp.repeat(jnp.exp(steps), dims[dim] // parts).reshape((-1,) + (1,) * (len(dims) - dim - 1))

    factor_of = one(*pieces[0])
    for cut in pieces[1:]:
        factor_of = factor_of * one(*cut)
    return factor_of


def normal_values(stream_key, dims, width, most, shards=(), held_as=jnp.bfloat16):
    level = block_levels(stream_key, dims, shards, -0.22, 0.18) if shards else 1.0
    values = jax.random.normal(stream_key, dims, jnp.float32) * width * level
    return jnp.minimum(jnp.maximum(values, -most), most).astype(held_as)


def heavy_noise(own_key, extent, spread, most, cuts, heavy, held_as=jnp.bfloat16):
    values = spread * jax.random.normal(own_key, extent, jnp.float32)
    if cuts:
        values = values * block_levels(own_key, extent, cuts, -0.22, 0.18)
    return jnp.clip(raised(values, jax.random.fold_in(own_key, 3), *heavy), -most, most).astype(held_as)


def setup_inputs(seed: int = 0) -> dict:
    key_list = jax.random.split(jax.random.key(seed), 7)
    subtree_right_hand = normal_values(key_list[0], (N_LAYER, SUBTREE_UNKNOWNS, RHS), 1.0, 6.0, ((0, 32), (1, 16)))
    root_rhs = normal_values(key_list[1], (ROOT_ROWS, RHS), 1.0, 6.0, ((0, 16),))
    blocks = heavy_noise(key_list[2], (N_LAYER, PAIRS, GRID, GRID, GRID, GRID, SUPER, SUPER), (GRID * GRID * SUPER) ** -0.5, 0.1875, ((0, 32), (2, 4), (3, 4)), (3, 4, 4, 2.0))
    pattern = place_ends((jax.random.randint(key_list[3], (N_LAYER, PAIRS, GRID, GRID, GRID, GRID), 0, 2) < 1).astype(jnp.int32), jax.random.fold_in(key_list[3], 1), 0, 1)
    forest_inverse = normal_values(key_list[4], (N_LAYER, 3, GRID, GRID, SUPER, SUPER), SUPER ** -0.5, 0.5, ((0, 32), (2, 4), (3, 4)), jnp.float32)
    root_inverse = normal_values(key_list[5], (GRID, GRID, SUPER, SUPER), SUPER ** -0.5, 0.5, ((0, 4), (1, 4)), jnp.float32)
    return {"subtree_right_hand": subtree_right_hand, "root_rhs": root_rhs, "blocks": blocks, "pattern": pattern, "forest_inverse": forest_inverse, "root_inverse": root_inverse}


def pair_slot(source, target):
    return (0, 3, 5)[source] + target - source - 1


def to_supernodes(flat_rows, levels):
    shaped = flat_rows.reshape(GRID, GRID, levels, GRID, SUPER // GRID, RHS)
    return shaped.transpose(2, 3, 0, 1, 4, 5).reshape(levels, GRID, GRID, SUPER, RHS)


def flatten_blocks(supernodes, levels):
    shaped = supernodes.reshape(levels, GRID, GRID, GRID, SUPER // GRID, RHS)
    return shaped.transpose(2, 3, 0, 1, 4, 5).reshape(GRID * GRID * levels * SUPER, RHS)


def contribution(block_entries, block_mask, solution):
    factor_weights = block_entries.astype(jnp.float32) * block_mask.astype(jnp.float32)[..., None, None]
    return jnp.einsum("acbdxy,dcyr->abxr", factor_weights, solution.astype(jnp.float32), precision=lax.Precision.HIGHEST)


def solve_blocks(inverse, right_hand_side):
    product = jnp.einsum("abxy,abyr->abxr", inverse, right_hand_side, precision=lax.Precision.HIGHEST)
    return product.astype(jnp.bfloat16)


def reference(subtree_right_hand, root_rhs, blocks, pattern, forest_inverse, root_inverse):
    forest_out = []
    root_terms = jnp.zeros((GRID, GRID, SUPER, RHS), jnp.float32)
    for layer_index in range(N_LAYER):
        right_blocks = to_supernodes(subtree_right_hand[layer_index], 3)
        solved = []
        for target in range(3):
            incoming = jnp.zeros((GRID, GRID, SUPER, RHS), jnp.float32)
            for source in range(target):
                slot = pair_slot(source, target)
                incoming = incoming + contribution(blocks[layer_index, slot], pattern[layer_index, slot], solved[source])
            right_hand_side = right_blocks[target].astype(jnp.float32) - incoming
            solved.append(solve_blocks(forest_inverse[layer_index, target], right_hand_side))
        layer_terms = jnp.zeros((GRID, GRID, SUPER, RHS), jnp.float32)
        for source in range(3):
            slot = pair_slot(source, 3)
            layer_terms = layer_terms + contribution(blocks[layer_index, slot], pattern[layer_index, slot], solved[source])
        root_terms = root_terms + layer_terms
        forest_out.append(flatten_blocks(jnp.stack(solved), 3))
    root_blocks = to_supernodes(root_rhs, 1)
    root_solved = solve_blocks(root_inverse, root_blocks[0].astype(jnp.float32) - root_terms)
    return jnp.stack(forest_out), flatten_blocks(root_solved[None], 1)
```

```python
import jax
import jax.numpy as jnp
from jax import lax
from jax.experimental import pallas as pl
from jax.experimental.pallas import tpu as pltpu
from jax.sharding import PartitionSpec as P

MESH = pl.DeviceIdType.MESH
VMEM_SPEC = pl.BlockSpec(memory_space=pltpu.VMEM)


def pair_slot(source, target):
    return (0, 3, 5)[source] + target - source - 1


def _barrier(axis, n, me):
    barrier = pltpu.get_barrier_semaphore()
    for d in range(1, n):
        pl.semaphore_signal(barrier, 1, device_id={axis: (me + d) % n}, device_id_type=MESH)
    pl.semaphore_wait(barrier, n - 1)


def _params(cid):
    return pltpu.CompilerParams(collective_id=cid, has_side_effects=True)


def reduce_scatter(x, axis, cid):
    n = x.shape[0]

    def kernel(x_ref, o_ref, recv, ssem, rsem):
        me = lax.axis_index(axis)
        _barrier(axis, n, me)
        copies = []
        for d in range(1, n):
            peer = (me + d) % n
            copy = pltpu.make_async_remote_copy(
                x_ref.at[peer], recv.at[d - 1], ssem.at[d - 1], rsem.at[d - 1],
                device_id={axis: peer}, device_id_type=MESH)
            copy.start()
            copies.append(copy)
        for copy in copies:
            copy.wait()
        total = x_ref[me]
        for d in range(n - 1):
            total = total + recv[d]
        o_ref[...] = total

    return pl.pallas_call(
        kernel,
        out_shape=jax.ShapeDtypeStruct(x.shape[1:], x.dtype),
        in_specs=[VMEM_SPEC],
        out_specs=VMEM_SPEC,
        scratch_shapes=[
            pltpu.VMEM((n - 1,) + x.shape[1:], x.dtype),
            pltpu.SemaphoreType.DMA((n - 1,)),
            pltpu.SemaphoreType.DMA((n - 1,)),
        ],
        compiler_params=_params(cid),
    )(x)


def all_gather(x, axis, n, cid):
    def kernel(x_ref, o_ref, ssem, rsem):
        me = lax.axis_index(axis)
        _barrier(axis, n, me)
        copies = []
        for d in range(1, n):
            peer = (me + d) % n
            copy = pltpu.make_async_remote_copy(
                x_ref, o_ref.at[me], ssem.at[d - 1], rsem.at[d - 1],
                device_id={axis: peer}, device_id_type=MESH)
            copy.start()
            copies.append(copy)
        o_ref[me] = x_ref[...]
        for copy in copies:
            copy.wait()

    return pl.pallas_call(
        kernel,
        out_shape=jax.ShapeDtypeStruct((n,) + x.shape, x.dtype),
        in_specs=[VMEM_SPEC],
        out_specs=VMEM_SPEC,
        scratch_shapes=[
            pltpu.SemaphoreType.DMA((n - 1,)),
            pltpu.SemaphoreType.DMA((n - 1,)),
        ],
        compiler_params=_params(cid),
    )(x)


def all_reduce(x, axis, cid):
    n = x.shape[0]

    def kernel(x_ref, o_ref, recv, part, ssem, rsem, gsem, hsem):
        me = lax.axis_index(axis)
        _barrier(axis, n, me)
        copies = []
        for d in range(1, n):
            peer = (me + d) % n
            copy = pltpu.make_async_remote_copy(
                x_ref.at[peer], recv.at[d - 1], ssem.at[d - 1], rsem.at[d - 1],
                device_id={axis: peer}, device_id_type=MESH)
            copy.start()
            copies.append(copy)
        for copy in copies:
            copy.wait()
        total = x_ref[me]
        for d in range(n - 1):
            total = total + recv[d]
        part[...] = total
        o_ref[me] = total
        copies = []
        for d in range(1, n):
            peer = (me + d) % n
            copy = pltpu.make_async_remote_copy(
                part, o_ref.at[me], gsem.at[d - 1], hsem.at[d - 1],
                device_id={axis: peer}, device_id_type=MESH)
            copy.start()
            copies.append(copy)
        for copy in copies:
            copy.wait()

    return pl.pallas_call(
        kernel,
        out_shape=jax.ShapeDtypeStruct(x.shape, x.dtype),
        in_specs=[VMEM_SPEC],
        out_specs=VMEM_SPEC,
        scratch_shapes=[
            pltpu.VMEM((n - 1,) + x.shape[1:], x.dtype),
            pltpu.VMEM(x.shape[1:], x.dtype),
            pltpu.SemaphoreType.DMA((n - 1,)),
            pltpu.SemaphoreType.DMA((n - 1,)),
            pltpu.SemaphoreType.DMA((n - 1,)),
            pltpu.SemaphoreType.DMA((n - 1,)),
        ],
        compiler_params=_params(cid),
    )(x)


def shards(subtree_right_hand, root_rhs, blocks, pattern, forest_inverse, root_inverse):
    grid_size = lax.axis_size("prow")
    n_layer = lax.axis_size("layer")
    super_rows = blocks.shape[-1]
    rhs_cols = subtree_right_hand.shape[-1]
    slice_rows = super_rows // grid_size
    local_forest = subtree_right_hand.reshape(3, grid_size, slice_rows, rhs_cols)
    local_root = root_rhs.reshape(1, grid_size, slice_rows, rhs_cols)
    joined = jnp.concatenate([local_forest, local_root], axis=0)
    placed = lax.all_to_all(
        lax.all_to_all(joined, "prow", split_axis=1, concat_axis=1, tiled=True),
        "pcol",
        split_axis=1,
        concat_axis=1,
        tiled=True,
    )
    placed = placed.reshape(4, super_rows, rhs_cols)
    block_mask = pattern.reshape(6, grid_size, grid_size).astype(jnp.bfloat16)
    masked = (
        blocks.reshape(6, grid_size, grid_size, super_rows, super_rows)
        * block_mask[..., None, None]
    )
    inverses = forest_inverse.reshape(3, super_rows, super_rows)
    solved = []
    empty_rows = jnp.zeros((grid_size, super_rows, rhs_cols), jnp.float32)
    totals = (empty_rows, empty_rows, empty_rows, empty_rows)
    for tier_index in range(3):
        right_hand_side = placed[tier_index].astype(jnp.float32)
        if tier_index > 0:
            reduced = reduce_scatter(totals[tier_index], "pcol", 10 + tier_index)
            right_hand_side = right_hand_side - reduced
        answer = jnp.dot(
            inverses[tier_index],
            right_hand_side,
            precision=lax.Precision.HIGHEST,
            preferred_element_type=jnp.float32,
        ).astype(jnp.bfloat16)
        solved.append(answer)
        block_pieces = all_gather(answer, "prow", grid_size, 20 + tier_index)
        updated_rows = []
        for target in range(4):
            if target > tier_index:
                factor_weights = masked[pair_slot(tier_index, target)]
                term = jnp.einsum(
                    "jznv,zvs->jns",
                    factor_weights,
                    block_pieces,
                    preferred_element_type=jnp.float32,
                )
                updated_rows.append(totals[target] + term)
            else:
                updated_rows.append(totals[target])
        totals = tuple(updated_rows)
    row_share = reduce_scatter(totals[3], "pcol", 13)
    chunks = row_share.reshape(n_layer, -1, 128)
    reduced_root = all_reduce(chunks, "layer", 30).reshape(super_rows, rhs_cols)
    root_side = placed[3].astype(jnp.float32) - reduced_root
    root_answer = jnp.dot(
        root_inverse.reshape(super_rows, super_rows),
        root_side,
        precision=lax.Precision.HIGHEST,
        preferred_element_type=jnp.float32,
    ).astype(jnp.bfloat16)
    stacked = jnp.stack(solved + [root_answer]).reshape(4, grid_size, slice_rows, rhs_cols)
    returned = lax.all_to_all(
        lax.all_to_all(stacked, "pcol", split_axis=1, concat_axis=1, tiled=True),
        "prow",
        split_axis=1,
        concat_axis=1,
        tiled=True,
    )
    forest_out = returned[:3].reshape(1, 3 * super_rows, rhs_cols)
    root_out = returned[3].reshape(super_rows, rhs_cols)
    return (forest_out, root_out)


def solution(mesh):
    placed = (
        P("layer", ("prow", "pcol"), None),
        P(("prow", "pcol"), None),
        P("layer", None, "prow", "pcol", None, None, None, None),
        P("layer", None, "prow", "pcol", None, None),
        P("layer", None, "prow", "pcol", None, None),
        P("prow", "pcol", None, None),
    )
    return jax.shard_map(
        shards,
        mesh=mesh,
        in_specs=placed,
        out_specs=(P("layer", ("prow", "pcol"), None), P(("prow", "pcol"), None)),
        check_vma=False,
    )
```

```python
import jax
import jax.numpy as jnp
from jax import lax
from jax.experimental import pallas as pl
from jax.experimental.pallas import tpu as pltpu
from jax.sharding import PartitionSpec as P

MESH = pl.DeviceIdType.MESH
VMEM_SPEC = pl.BlockSpec(memory_space=pltpu.VMEM)


def pair_slot(source, target):
    return (0, 3, 5)[source] + target - source - 1


def _barrier(axis, n, me):
    barrier = pltpu.get_barrier_semaphore()
    for d in range(1, n):
        pl.semaphore_signal(barrier, 1, device_id={axis: (me + d) % n}, device_id_type=MESH)
    pl.semaphore_wait(barrier, n - 1)


def _params(cid):
    return pltpu.CompilerParams(collective_id=cid, has_side_effects=True)


def reduce_scatter(x, axis, cid):
    n = x.shape[0]

    def kernel(x_ref, o_ref, recv, ssem, rsem):
        me = lax.axis_index(axis)
        _barrier(axis, n, me)
        copies = []
        for d in range(1, n):
            peer = (me + d) % n
            copy = pltpu.make_async_remote_copy(
                x_ref.at[peer], recv.at[d - 1], ssem.at[d - 1], rsem.at[d - 1],
                device_id={axis: peer}, device_id_type=MESH)
            copy.start()
            copies.append(copy)
        for copy in copies:
            copy.wait()
        total = x_ref[me]
        for d in range(n - 1):
            total = total + recv[d]
        o_ref[...] = total

    return pl.pallas_call(
        kernel,
        out_shape=jax.ShapeDtypeStruct(x.shape[1:], x.dtype),
        in_specs=[VMEM_SPEC],
        out_specs=VMEM_SPEC,
        scratch_shapes=[
            pltpu.VMEM((n - 1,) + x.shape[1:], x.dtype),
            pltpu.SemaphoreType.DMA((n - 1,)),
            pltpu.SemaphoreType.DMA((n - 1,)),
        ],
        compiler_params=_params(cid),
    )(x)


def all_gather(x, axis, n, cid):
    def kernel(x_ref, o_ref, ssem, rsem):
        me = lax.axis_index(axis)
        _barrier(axis, n, me)
        copies = []
        for d in range(1, n):
            peer = (me + d) % n
            copy = pltpu.make_async_remote_copy(
                x_ref, o_ref.at[me], ssem.at[d - 1], rsem.at[d - 1],
                device_id={axis: peer}, device_id_type=MESH)
            copy.start()
            copies.append(copy)
        o_ref[me] = x_ref[...]
        for copy in copies:
            copy.wait()

    return pl.pallas_call(
        kernel,
        out_shape=jax.ShapeDtypeStruct((n,) + x.shape, x.dtype),
        in_specs=[VMEM_SPEC],
        out_specs=VMEM_SPEC,
        scratch_shapes=[
            pltpu.SemaphoreType.DMA((n - 1,)),
            pltpu.SemaphoreType.DMA((n - 1,)),
        ],
        compiler_params=_params(cid),
    )(x)


def all_reduce(x, axis, cid):
    n = x.shape[0]

    def kernel(x_ref, o_ref, recv, part, ssem, rsem, gsem, hsem):
        me = lax.axis_index(axis)
        _barrier(axis, n, me)
        copies = []
        for d in range(1, n):
            peer = (me + d) % n
            copy = pltpu.make_async_remote_copy(
                x_ref.at[peer], recv.at[d - 1], ssem.at[d - 1], rsem.at[d - 1],
                device_id={axis: peer}, device_id_type=MESH)
            copy.start()
            copies.append(copy)
        for copy in copies:
            copy.wait()
        total = x_ref[me]
        for d in range(n - 1):
            total = total + recv[d]
        part[...] = total
        o_ref[me] = total
        copies = []
        for d in range(1, n):
            peer = (me + d) % n
            copy = pltpu.make_async_remote_copy(
                part, o_ref.at[me], gsem.at[d - 1], hsem.at[d - 1],
                device_id={axis: peer}, device_id_type=MESH)
            copy.start()
            copies.append(copy)
        for copy in copies:
            copy.wait()

    return pl.pallas_call(
        kernel,
        out_shape=jax.ShapeDtypeStruct(x.shape, x.dtype),
        in_specs=[VMEM_SPEC],
        out_specs=VMEM_SPEC,
        scratch_shapes=[
            pltpu.VMEM((n - 1,) + x.shape[1:], x.dtype),
            pltpu.VMEM(x.shape[1:], x.dtype),
            pltpu.SemaphoreType.DMA((n - 1,)),
            pltpu.SemaphoreType.DMA((n - 1,)),
            pltpu.SemaphoreType.DMA((n - 1,)),
            pltpu.SemaphoreType.DMA((n - 1,)),
        ],
        compiler_params=_params(cid),
    )(x)


def permute_rows(x, forward, cid):
    g = x.shape[1]

    def kernel(x_ref, o_ref, ssem, rsem, lsem):
        p = lax.axis_index("prow")
        q = lax.axis_index("pcol")
        barrier = pltpu.get_barrier_semaphore()
        for dp in range(g):
            for dq in range(g):
                if dp or dq:
                    pl.semaphore_signal(
                        barrier, 1, device_id={"prow": (p + dp) % g, "pcol": (q + dq) % g},
                        device_id_type=MESH)
        pl.semaphore_wait(barrier, g * g - 1)
        own = p == q
        slot = q if forward else p
        sends = []
        for dj in range(g):
            j = (p + dj) % g
            dest = {"prow": j, "pcol": p} if forward else {"prow": q, "pcol": j}
            copy = pltpu.make_async_remote_copy(
                x_ref.at[:, j], o_ref.at[:, slot], ssem.at[dj], rsem.at[slot],
                device_id=dest, device_id_type=MESH)
            if dj == 0:
                local = pltpu.make_async_copy(x_ref.at[:, j], o_ref.at[:, j], lsem)

                @pl.when(own)
                def _():
                    local.start()

                @pl.when(jnp.logical_not(own))
                def _():
                    copy.start()
            else:
                copy.start()
            sends.append(copy)
        for dj in range(g):
            s = (p + dj) % g
            arrival = pltpu.make_async_copy(x_ref.at[:, s], o_ref.at[:, s], rsem.at[s])
            if dj == 0:
                @pl.when(own)
                def _():
                    local.wait()

                @pl.when(jnp.logical_not(own))
                def _():
                    sends[0].wait_send()
                    arrival.wait()
            else:
                sends[dj].wait_send()
                arrival.wait()

    return pl.pallas_call(
        kernel,
        out_shape=jax.ShapeDtypeStruct(x.shape, x.dtype),
        in_specs=[VMEM_SPEC],
        out_specs=VMEM_SPEC,
        scratch_shapes=[
            pltpu.SemaphoreType.DMA((g,)),
            pltpu.SemaphoreType.DMA((g,)),
            pltpu.SemaphoreType.DMA(()),
        ],
        compiler_params=_params(cid),
    )(x)


def shards(subtree_right_hand, root_rhs, blocks, pattern, forest_inverse, root_inverse):
    grid_size = lax.axis_size("prow")
    n_layer = lax.axis_size("layer")
    super_rows = blocks.shape[-1]
    rhs_cols = subtree_right_hand.shape[-1]
    slice_rows = super_rows // grid_size
    local_forest = subtree_right_hand.reshape(3, grid_size, slice_rows, rhs_cols)
    local_root = root_rhs.reshape(1, grid_size, slice_rows, rhs_cols)
    joined = jnp.concatenate([local_forest, local_root], axis=0)
    placed = permute_rows(joined, True, 40)
    placed = placed.reshape(4, super_rows, rhs_cols)
    block_mask = pattern.reshape(6, grid_size, grid_size).astype(jnp.bfloat16)
    masked = (
        blocks.reshape(6, grid_size, grid_size, super_rows, super_rows)
        * block_mask[..., None, None]
    )
    inverses = forest_inverse.reshape(3, super_rows, super_rows)
    solved = []
    empty_rows = jnp.zeros((grid_size, super_rows, rhs_cols), jnp.float32)
    totals = (empty_rows, empty_rows, empty_rows, empty_rows)
    for tier_index in range(3):
        right_hand_side = placed[tier_index].astype(jnp.float32)
        if tier_index > 0:
            reduced = reduce_scatter(totals[tier_index], "pcol", 10 + tier_index)
            right_hand_side = right_hand_side - reduced
        answer = jnp.dot(
            inverses[tier_index],
            right_hand_side,
            precision=lax.Precision.HIGHEST,
            preferred_element_type=jnp.float32,
        ).astype(jnp.bfloat16)
        solved.append(answer)
        block_pieces = all_gather(answer, "prow", grid_size, 20 + tier_index)
        updated_rows = []
        for target in range(4):
            if target > tier_index:
                factor_weights = masked[pair_slot(tier_index, target)]
                term = jnp.einsum(
                    "jznv,zvs->jns",
                    factor_weights,
                    block_pieces,
                    preferred_element_type=jnp.float32,
                )
                updated_rows.append(totals[target] + term)
            else:
                updated_rows.append(totals[target])
        totals = tuple(updated_rows)
    row_share = reduce_scatter(totals[3], "pcol", 13)
    chunks = row_share.reshape(n_layer, -1, 128)
    reduced_root = all_reduce(chunks, "layer", 30).reshape(super_rows, rhs_cols)
    root_side = placed[3].astype(jnp.float32) - reduced_root
    root_answer = jnp.dot(
        root_inverse.reshape(super_rows, super_rows),
        root_side,
        precision=lax.Precision.HIGHEST,
        preferred_element_type=jnp.float32,
    ).astype(jnp.bfloat16)
    stacked = jnp.stack(solved + [root_answer]).reshape(4, grid_size, slice_rows, rhs_cols)
    returned = permute_rows(stacked, False, 41)
    forest_out = returned[:3].reshape(1, 3 * super_rows, rhs_cols)
    root_out = returned[3].reshape(super_rows, rhs_cols)
    return (forest_out, root_out)


def solution(mesh):
    placed = (
        P("layer", ("prow", "pcol"), None),
        P(("prow", "pcol"), None),
        P("layer", None, "prow", "pcol", None, None, None, None),
        P("layer", None, "prow", "pcol", None, None),
        P("layer", None, "prow", "pcol", None, None),
        P("prow", "pcol", None, None),
    )
    return jax.shard_map(
        shards,
        mesh=mesh,
        in_specs=placed,
        out_specs=(P("layer", ("prow", "pcol"), None), P(("prow", "pcol"), None)),
        check_vma=False,
    )
```

```python
import jax
import jax.numpy as jnp
from jax import lax
from jax.experimental import pallas as pl
from jax.experimental.pallas import tpu as pltpu
from jax.sharding import PartitionSpec as P

MESH = pl.DeviceIdType.MESH
VMEM_SPEC = pl.BlockSpec(memory_space=pltpu.VMEM)


def pair_slot(source, target):
    return (0, 3, 5)[source] + target - source - 1


def _barrier(axis, n, me):
    barrier = pltpu.get_barrier_semaphore()
    for d in range(1, n):
        pl.semaphore_signal(barrier, 1, device_id={axis: (me + d) % n}, device_id_type=MESH)
    pl.semaphore_wait(barrier, n - 1)


def _params(cid):
    return pltpu.CompilerParams(collective_id=cid, has_side_effects=True)


def reduce_scatter(x, own_part, axis, cid, wire):
    n = x.shape[0]

    def kernel(x_ref, own_ref, o_ref, recv, ssem, rsem):
        me = lax.axis_index(axis)
        _barrier(axis, n, me)
        copies = []
        for d in range(1, n):
            peer = (me + d) % n
            copy = pltpu.make_async_remote_copy(
                x_ref.at[peer], recv.at[d - 1], ssem.at[d - 1], rsem.at[d - 1],
                device_id={axis: peer}, device_id_type=MESH)
            copy.start()
            copies.append(copy)
        for copy in copies:
            copy.wait()
        total = own_ref[...]
        for d in range(n - 1):
            total = total + recv[d].astype(jnp.float32)
        o_ref[...] = total

    return pl.pallas_call(
        kernel,
        out_shape=jax.ShapeDtypeStruct(x.shape[1:], jnp.float32),
        in_specs=[VMEM_SPEC, VMEM_SPEC],
        out_specs=VMEM_SPEC,
        scratch_shapes=[
            pltpu.VMEM((n - 1,) + x.shape[1:], wire),
            pltpu.SemaphoreType.DMA((n - 1,)),
            pltpu.SemaphoreType.DMA((n - 1,)),
        ],
        compiler_params=_params(cid),
    )(x, own_part)


def all_gather(x, axis, n, cid):
    def kernel(x_ref, o_ref, ssem, rsem):
        me = lax.axis_index(axis)
        _barrier(axis, n, me)
        copies = []
        for d in range(1, n):
            peer = (me + d) % n
            copy = pltpu.make_async_remote_copy(
                x_ref, o_ref.at[me], ssem.at[d - 1], rsem.at[d - 1],
                device_id={axis: peer}, device_id_type=MESH)
            copy.start()
            copies.append(copy)
        o_ref[me] = x_ref[...]
        for copy in copies:
            copy.wait()

    return pl.pallas_call(
        kernel,
        out_shape=jax.ShapeDtypeStruct((n,) + x.shape, x.dtype),
        in_specs=[VMEM_SPEC],
        out_specs=VMEM_SPEC,
        scratch_shapes=[
            pltpu.SemaphoreType.DMA((n - 1,)),
            pltpu.SemaphoreType.DMA((n - 1,)),
        ],
        compiler_params=_params(cid),
    )(x)


def all_reduce(x, axis, cid):
    n = x.shape[0]

    def kernel(x_ref, o_ref, recv, part, ssem, rsem, gsem, hsem):
        me = lax.axis_index(axis)
        _barrier(axis, n, me)
        copies = []
        for d in range(1, n):
            peer = (me + d) % n
            copy = pltpu.make_async_remote_copy(
                x_ref.at[peer], recv.at[d - 1], ssem.at[d - 1], rsem.at[d - 1],
                device_id={axis: peer}, device_id_type=MESH)
            copy.start()
            copies.append(copy)
        for copy in copies:
            copy.wait()
        total = x_ref[me]
        for d in range(n - 1):
            total = total + recv[d]
        part[...] = total
        o_ref[me] = total
        copies = []
        for d in range(1, n):
            peer = (me + d) % n
            copy = pltpu.make_async_remote_copy(
                part, o_ref.at[me], gsem.at[d - 1], hsem.at[d - 1],
                device_id={axis: peer}, device_id_type=MESH)
            copy.start()
            copies.append(copy)
        for copy in copies:
            copy.wait()

    return pl.pallas_call(
        kernel,
        out_shape=jax.ShapeDtypeStruct(x.shape, x.dtype),
        in_specs=[VMEM_SPEC],
        out_specs=VMEM_SPEC,
        scratch_shapes=[
            pltpu.VMEM((n - 1,) + x.shape[1:], x.dtype),
            pltpu.VMEM(x.shape[1:], x.dtype),
            pltpu.SemaphoreType.DMA((n - 1,)),
            pltpu.SemaphoreType.DMA((n - 1,)),
            pltpu.SemaphoreType.DMA((n - 1,)),
            pltpu.SemaphoreType.DMA((n - 1,)),
        ],
        compiler_params=_params(cid),
    )(x)


def permute_rows(x, forward, cid):
    g = x.shape[1]

    def kernel(x_ref, o_ref, ssem, rsem, lsem):
        p = lax.axis_index("prow")
        q = lax.axis_index("pcol")
        barrier = pltpu.get_barrier_semaphore()
        for dp in range(g):
            for dq in range(g):
                if dp or dq:
                    pl.semaphore_signal(
                        barrier, 1, device_id={"prow": (p + dp) % g, "pcol": (q + dq) % g},
                        device_id_type=MESH)
        pl.semaphore_wait(barrier, g * g - 1)
        own = p == q
        slot = q if forward else p
        sends = []
        for dj in range(g):
            j = (p + dj) % g
            dest = {"prow": j, "pcol": p} if forward else {"prow": q, "pcol": j}
            copy = pltpu.make_async_remote_copy(
                x_ref.at[:, j], o_ref.at[:, slot], ssem.at[dj], rsem.at[slot],
                device_id=dest, device_id_type=MESH)
            if dj == 0:
                local = pltpu.make_async_copy(x_ref.at[:, j], o_ref.at[:, j], lsem)

                @pl.when(own)
                def _():
                    local.start()

                @pl.when(jnp.logical_not(own))
                def _():
                    copy.start()
            else:
                copy.start()
            sends.append(copy)
        for dj in range(g):
            s = (p + dj) % g
            arrival = pltpu.make_async_copy(x_ref.at[:, s], o_ref.at[:, s], rsem.at[s])
            if dj == 0:
                @pl.when(own)
                def _():
                    local.wait()

                @pl.when(jnp.logical_not(own))
                def _():
                    sends[0].wait_send()
                    arrival.wait()
            else:
                sends[dj].wait_send()
                arrival.wait()

    return pl.pallas_call(
        kernel,
        out_shape=jax.ShapeDtypeStruct(x.shape, x.dtype),
        in_specs=[VMEM_SPEC],
        out_specs=VMEM_SPEC,
        scratch_shapes=[
            pltpu.SemaphoreType.DMA((g,)),
            pltpu.SemaphoreType.DMA((g,)),
            pltpu.SemaphoreType.DMA(()),
        ],
        compiler_params=_params(cid),
    )(x)


def shards(subtree_right_hand, root_rhs, blocks, pattern, forest_inverse, root_inverse):
    grid_size = lax.axis_size("prow")
    n_layer = lax.axis_size("layer")
    super_rows = blocks.shape[-1]
    rhs_cols = subtree_right_hand.shape[-1]
    slice_rows = super_rows // grid_size
    local_forest = subtree_right_hand.reshape(3, grid_size, slice_rows, rhs_cols)
    local_root = root_rhs.reshape(1, grid_size, slice_rows, rhs_cols)
    joined = jnp.concatenate([local_forest, local_root], axis=0)
    placed = permute_rows(joined, True, 40)
    placed = placed.reshape(4, super_rows, rhs_cols)
    block_mask = pattern.reshape(6, grid_size, grid_size).astype(jnp.bfloat16)
    masked = (
        blocks.reshape(6, grid_size, grid_size, super_rows, super_rows)
        * block_mask[..., None, None]
    )
    inverses = forest_inverse.reshape(3, super_rows, super_rows)
    solved = []
    empty_rows = jnp.zeros((grid_size, super_rows, rhs_cols), jnp.float32)
    totals = (empty_rows, empty_rows, empty_rows, empty_rows)
    for tier_index in range(3):
        right_hand_side = placed[tier_index].astype(jnp.float32)
        if tier_index > 0:
            rows = totals[tier_index]
            own_rows = rows[lax.axis_index("pcol")]
            reduced = reduce_scatter(rows.astype(jnp.bfloat16), own_rows, "pcol", 10 + tier_index, jnp.bfloat16)
            right_hand_side = right_hand_side - reduced
        answer = jnp.dot(
            inverses[tier_index],
            right_hand_side,
            precision=lax.Precision.HIGHEST,
            preferred_element_type=jnp.float32,
        ).astype(jnp.bfloat16)
        solved.append(answer)
        block_pieces = all_gather(answer, "prow", grid_size, 20 + tier_index)
        updated_rows = []
        for target in range(4):
            if target > tier_index:
                factor_weights = masked[pair_slot(tier_index, target)]
                term = jnp.einsum(
                    "jznv,zvs->jns",
                    factor_weights,
                    block_pieces,
                    preferred_element_type=jnp.float32,
                )
                updated_rows.append(totals[target] + term)
            else:
                updated_rows.append(totals[target])
        totals = tuple(updated_rows)
    row_share = reduce_scatter(totals[3], totals[3][lax.axis_index("pcol")], "pcol", 13, jnp.float32)
    chunks = row_share.reshape(n_layer, -1, 128)
    reduced_root = all_reduce(chunks, "layer", 30).reshape(super_rows, rhs_cols)
    root_side = placed[3].astype(jnp.float32) - reduced_root
    root_answer = jnp.dot(
        root_inverse.reshape(super_rows, super_rows),
        root_side,
        precision=lax.Precision.HIGHEST,
        preferred_element_type=jnp.float32,
    ).astype(jnp.bfloat16)
    stacked = jnp.stack(solved + [root_answer]).reshape(4, grid_size, slice_rows, rhs_cols)
    returned = permute_rows(stacked, False, 41)
    forest_out = returned[:3].reshape(1, 3 * super_rows, rhs_cols)
    root_out = returned[3].reshape(super_rows, rhs_cols)
    return (forest_out, root_out)


def solution(mesh):
    placed = (
        P("layer", ("prow", "pcol"), None),
        P(("prow", "pcol"), None),
        P("layer", None, "prow", "pcol", None, None, None, None),
        P("layer", None, "prow", "pcol", None, None),
        P("layer", None, "prow", "pcol", None, None),
        P("prow", "pcol", None, None),
    )
    return jax.shard_map(
        shards,
        mesh=mesh,
        in_specs=placed,
        out_specs=(P("layer", ("prow", "pcol"), None), P(("prow", "pcol"), None)),
        check_vma=False,
    )
```

```python
import jax
import jax.numpy as jnp
from jax import lax
from jax.experimental import pallas as pl
from jax.experimental.pallas import tpu as pltpu
from jax.sharding import PartitionSpec as P

MESH = pl.DeviceIdType.MESH
VMEM_SPEC = pl.BlockSpec(memory_space=pltpu.VMEM)


def pair_slot(source, target):
    return (0, 3, 5)[source] + target - source - 1


def _barrier(axis, n, me):
    barrier = pltpu.get_barrier_semaphore()
    for d in range(1, n):
        pl.semaphore_signal(barrier, 1, device_id={axis: (me + d) % n}, device_id_type=MESH)
    pl.semaphore_wait(barrier, n - 1)


def _params(cid):
    return pltpu.CompilerParams(collective_id=cid, has_side_effects=True)


def reduce_scatter(x, own_part, axis, cid, wire):
    n = x.shape[0]

    def kernel(x_ref, own_ref, o_ref, recv, ssem, rsem):
        me = lax.axis_index(axis)
        _barrier(axis, n, me)
        copies = []
        for d in range(1, n):
            peer = (me + d) % n
            copy = pltpu.make_async_remote_copy(
                x_ref.at[peer], recv.at[d - 1], ssem.at[d - 1], rsem.at[d - 1],
                device_id={axis: peer}, device_id_type=MESH)
            copy.start()
            copies.append(copy)
        for copy in copies:
            copy.wait()
        total = own_ref[...]
        for d in range(n - 1):
            total = total + recv[d].astype(jnp.float32)
        o_ref[...] = total

    return pl.pallas_call(
        kernel,
        out_shape=jax.ShapeDtypeStruct(x.shape[1:], jnp.float32),
        in_specs=[VMEM_SPEC, VMEM_SPEC],
        out_specs=VMEM_SPEC,
        scratch_shapes=[
            pltpu.VMEM((n - 1,) + x.shape[1:], wire),
            pltpu.SemaphoreType.DMA((n - 1,)),
            pltpu.SemaphoreType.DMA((n - 1,)),
        ],
        compiler_params=_params(cid),
    )(x, own_part)


def all_gather(x, axis, n, cid):
    def kernel(x_ref, o_ref, ssem, rsem):
        me = lax.axis_index(axis)
        _barrier(axis, n, me)
        copies = []
        for d in range(1, n):
            peer = (me + d) % n
            copy = pltpu.make_async_remote_copy(
                x_ref, o_ref.at[me], ssem.at[d - 1], rsem.at[d - 1],
                device_id={axis: peer}, device_id_type=MESH)
            copy.start()
            copies.append(copy)
        o_ref[me] = x_ref[...]
        for copy in copies:
            copy.wait()

    return pl.pallas_call(
        kernel,
        out_shape=jax.ShapeDtypeStruct((n,) + x.shape, x.dtype),
        in_specs=[VMEM_SPEC],
        out_specs=VMEM_SPEC,
        scratch_shapes=[
            pltpu.SemaphoreType.DMA((n - 1,)),
            pltpu.SemaphoreType.DMA((n - 1,)),
        ],
        compiler_params=_params(cid),
    )(x)


def all_reduce(x, axis, cid):
    n = x.shape[0]

    def kernel(x_ref, o_ref, recv, part, ssem, rsem, gsem, hsem):
        me = lax.axis_index(axis)
        _barrier(axis, n, me)
        copies = []
        for d in range(1, n):
            peer = (me + d) % n
            copy = pltpu.make_async_remote_copy(
                x_ref.at[peer], recv.at[d - 1], ssem.at[d - 1], rsem.at[d - 1],
                device_id={axis: peer}, device_id_type=MESH)
            copy.start()
            copies.append(copy)
        for copy in copies:
            copy.wait()
        total = x_ref[me]
        for d in range(n - 1):
            total = total + recv[d]
        part[...] = total
        o_ref[me] = total
        copies = []
        for d in range(1, n):
            peer = (me + d) % n
            copy = pltpu.make_async_remote_copy(
                part, o_ref.at[me], gsem.at[d - 1], hsem.at[d - 1],
                device_id={axis: peer}, device_id_type=MESH)
            copy.start()
            copies.append(copy)
        for copy in copies:
            copy.wait()

    return pl.pallas_call(
        kernel,
        out_shape=jax.ShapeDtypeStruct(x.shape, x.dtype),
        in_specs=[VMEM_SPEC],
        out_specs=VMEM_SPEC,
        scratch_shapes=[
            pltpu.VMEM((n - 1,) + x.shape[1:], x.dtype),
            pltpu.VMEM(x.shape[1:], x.dtype),
            pltpu.SemaphoreType.DMA((n - 1,)),
            pltpu.SemaphoreType.DMA((n - 1,)),
            pltpu.SemaphoreType.DMA((n - 1,)),
            pltpu.SemaphoreType.DMA((n - 1,)),
        ],
        compiler_params=_params(cid),
    )(x)


def _grid_barrier_signals(barrier, g, p, q):
    for dp in range(g):
        for dq in range(g):
            if dp or dq:
                pl.semaphore_signal(
                    barrier, 1, device_id={"prow": (p + dp) % g, "pcol": (q + dq) % g},
                    device_id_type=MESH)


def _permute_start(x_ref, o_ref, forward, ssem, rsem, lsem):
    g = x_ref.shape[1]
    p = lax.axis_index("prow")
    q = lax.axis_index("pcol")
    own = p == q
    slot = q if forward else p
    sends = []
    local = pltpu.make_async_copy(x_ref.at[:, p], o_ref.at[:, p], lsem)
    for dj in range(g):
        j = (p + dj) % g
        dest = {"prow": j, "pcol": p} if forward else {"prow": q, "pcol": j}
        copy = pltpu.make_async_remote_copy(
            x_ref.at[:, j], o_ref.at[:, slot], ssem.at[dj], rsem.at[slot],
            device_id=dest, device_id_type=MESH)
        if dj == 0:
            @pl.when(own)
            def _():
                local.start()

            @pl.when(jnp.logical_not(own))
            def _():
                copy.start()
        else:
            copy.start()
        sends.append(copy)

    def wait():
        for dj in range(g):
            s = (p + dj) % g
            arrival = pltpu.make_async_copy(x_ref.at[:, s], o_ref.at[:, s], rsem.at[s])
            if dj == 0:
                @pl.when(own)
                def _():
                    local.wait()

                @pl.when(jnp.logical_not(own))
                def _():
                    sends[0].wait_send()
                    arrival.wait()
            else:
                sends[dj].wait_send()
                arrival.wait()

    return wait


def _permute_scratch(g):
    return [pltpu.SemaphoreType.DMA((g,)), pltpu.SemaphoreType.DMA((g,)), pltpu.SemaphoreType.DMA(())]


def permute_rows(x, forward, cid):
    g = x.shape[1]

    def kernel(x_ref, o_ref, ssem, rsem, lsem):
        p = lax.axis_index("prow")
        q = lax.axis_index("pcol")
        barrier = pltpu.get_barrier_semaphore()
        _grid_barrier_signals(barrier, g, p, q)
        pl.semaphore_wait(barrier, g * g - 1)
        _permute_start(x_ref, o_ref, forward, ssem, rsem, lsem)()

    return pl.pallas_call(
        kernel,
        out_shape=jax.ShapeDtypeStruct(x.shape, x.dtype),
        in_specs=[VMEM_SPEC],
        out_specs=VMEM_SPEC,
        scratch_shapes=_permute_scratch(g),
        compiler_params=_params(cid),
    )(x)


def root_exchange(chunks, forest, root_in, cid):
    n = chunks.shape[0]
    g = forest.shape[1]
    axis = "layer"

    def kernel(x_ref, f_ref, r_ref, o_ref, fo_ref, ro_ref, recv, part,
               ssem, rsem, gsem, hsem, fs, fr, fl, rs, rr, rl):
        me = lax.axis_index(axis)
        p = lax.axis_index("prow")
        q = lax.axis_index("pcol")
        barrier = pltpu.get_barrier_semaphore()
        for d in range(1, n):
            pl.semaphore_signal(barrier, 1, device_id={axis: (me + d) % n}, device_id_type=MESH)
        _grid_barrier_signals(barrier, g, p, q)
        pl.semaphore_wait(barrier, n - 1 + g * g - 1)
        root_wait = _permute_start(r_ref, ro_ref, True, rs, rr, rl)
        forest_wait = _permute_start(f_ref, fo_ref, False, fs, fr, fl)
        copies = []
        for d in range(1, n):
            peer = (me + d) % n
            copy = pltpu.make_async_remote_copy(
                x_ref.at[peer], recv.at[d - 1], ssem.at[d - 1], rsem.at[d - 1],
                device_id={axis: peer}, device_id_type=MESH)
            copy.start()
            copies.append(copy)
        for copy in copies:
            copy.wait()
        total = x_ref[me]
        for d in range(n - 1):
            total = total + recv[d]
        part[...] = total
        o_ref[me] = total
        copies = []
        for d in range(1, n):
            peer = (me + d) % n
            copy = pltpu.make_async_remote_copy(
                part, o_ref.at[me], gsem.at[d - 1], hsem.at[d - 1],
                device_id={axis: peer}, device_id_type=MESH)
            copy.start()
            copies.append(copy)
        for copy in copies:
            copy.wait()
        root_wait()
        forest_wait()

    return pl.pallas_call(
        kernel,
        out_shape=(
            jax.ShapeDtypeStruct(chunks.shape, chunks.dtype),
            jax.ShapeDtypeStruct(forest.shape, forest.dtype),
            jax.ShapeDtypeStruct(root_in.shape, root_in.dtype),
        ),
        in_specs=[VMEM_SPEC] * 3,
        out_specs=(VMEM_SPEC,) * 3,
        scratch_shapes=[
            pltpu.VMEM((n - 1,) + chunks.shape[1:], chunks.dtype),
            pltpu.VMEM(chunks.shape[1:], chunks.dtype),
            pltpu.SemaphoreType.DMA((n - 1,)),
            pltpu.SemaphoreType.DMA((n - 1,)),
            pltpu.SemaphoreType.DMA((n - 1,)),
            pltpu.SemaphoreType.DMA((n - 1,)),
        ] + _permute_scratch(g) + _permute_scratch(g),
        compiler_params=_params(cid),
    )(chunks, forest, root_in)


def shards(subtree_right_hand, root_rhs, blocks, pattern, forest_inverse, root_inverse):
    grid_size = lax.axis_size("prow")
    n_layer = lax.axis_size("layer")
    super_rows = blocks.shape[-1]
    rhs_cols = subtree_right_hand.shape[-1]
    slice_rows = super_rows // grid_size
    local_forest = subtree_right_hand.reshape(3, grid_size, slice_rows, rhs_cols)
    local_root = root_rhs.reshape(1, grid_size, slice_rows, rhs_cols)
    placed = permute_rows(local_forest, True, 40)
    placed = placed.reshape(3, super_rows, rhs_cols)
    block_mask = pattern.reshape(6, grid_size, grid_size).astype(jnp.bfloat16)
    masked = (
        blocks.reshape(6, grid_size, grid_size, super_rows, super_rows)
        * block_mask[..., None, None]
    )
    inverses = forest_inverse.reshape(3, super_rows, super_rows)
    solved = []
    empty_rows = jnp.zeros((grid_size, super_rows, rhs_cols), jnp.float32)
    totals = (empty_rows, empty_rows, empty_rows, empty_rows)
    for tier_index in range(3):
        right_hand_side = placed[tier_index].astype(jnp.float32)
        if tier_index > 0:
            rows = totals[tier_index]
            own_rows = rows[lax.axis_index("pcol")]
            reduced = reduce_scatter(rows.astype(jnp.bfloat16), own_rows, "pcol", 10 + tier_index, jnp.bfloat16)
            right_hand_side = right_hand_side - reduced
        answer = jnp.dot(
            inverses[tier_index],
            right_hand_side,
            precision=lax.Precision.HIGHEST,
            preferred_element_type=jnp.float32,
        ).astype(jnp.bfloat16)
        solved.append(answer)
        block_pieces = all_gather(answer, "prow", grid_size, 20 + tier_index)
        updated_rows = []
        for target in range(4):
            if target > tier_index:
                factor_weights = masked[pair_slot(tier_index, target)]
                term = jnp.einsum(
                    "jznv,zvs->jns",
                    factor_weights,
                    block_pieces,
                    preferred_element_type=jnp.float32,
                )
                updated_rows.append(totals[target] + term)
            else:
                updated_rows.append(totals[target])
        totals = tuple(updated_rows)
    row_share = reduce_scatter(totals[3], totals[3][lax.axis_index("pcol")], "pcol", 13, jnp.float32)
    chunks = row_share.reshape(n_layer, -1, 128)
    forest_solved = jnp.stack(solved).reshape(3, grid_size, slice_rows, rhs_cols)
    reduced_root, forest_back, root_placed = root_exchange(chunks, forest_solved, local_root, 30)
    reduced_root = reduced_root.reshape(super_rows, rhs_cols)
    root_side = root_placed.reshape(super_rows, rhs_cols).astype(jnp.float32) - reduced_root
    root_answer = jnp.dot(
        root_inverse.reshape(super_rows, super_rows),
        root_side,
        precision=lax.Precision.HIGHEST,
        preferred_element_type=jnp.float32,
    ).astype(jnp.bfloat16)
    root_back = permute_rows(root_answer.reshape(1, grid_size, slice_rows, rhs_cols), False, 41)
    forest_out = forest_back.reshape(1, 3 * super_rows, rhs_cols)
    root_out = root_back.reshape(super_rows, rhs_cols)
    return (forest_out, root_out)


def solution(mesh):
    placed = (
        P("layer", ("prow", "pcol"), None),
        P(("prow", "pcol"), None),
        P("layer", None, "prow", "pcol", None, None, None, None),
        P("layer", None, "prow", "pcol", None, None),
        P("layer", None, "prow", "pcol", None, None),
        P("prow", "pcol", None, None),
    )
    return jax.shard_map(
        shards,
        mesh=mesh,
        in_specs=placed,
        out_specs=(P("layer", ("prow", "pcol"), None), P(("prow", "pcol"), None)),
        check_vma=False,
    )
```

```python
import jax
import jax.numpy as jnp
from jax import lax
from jax.experimental import pallas as pl
from jax.experimental.pallas import tpu as pltpu
from jax.sharding import PartitionSpec as P

MESH = pl.DeviceIdType.MESH
VMEM_SPEC = pl.BlockSpec(memory_space=pltpu.VMEM)


def pair_slot(source, target):
    return (0, 3, 5)[source] + target - source - 1


def _barrier(axis, n, me):
    barrier = pltpu.get_barrier_semaphore()
    for d in range(1, n):
        pl.semaphore_signal(barrier, 1, device_id={axis: (me + d) % n}, device_id_type=MESH)
    pl.semaphore_wait(barrier, n - 1)


def _params(cid):
    return pltpu.CompilerParams(collective_id=cid, has_side_effects=True)


def reduce_scatter(x, own_part, axis, cid, wire):
    n = x.shape[0]

    def kernel(x_ref, own_ref, o_ref, recv, ssem, rsem):
        me = lax.axis_index(axis)
        _barrier(axis, n, me)
        copies = []
        for d in range(1, n):
            peer = (me + d) % n
            copy = pltpu.make_async_remote_copy(
                x_ref.at[peer], recv.at[d - 1], ssem.at[d - 1], rsem.at[d - 1],
                device_id={axis: peer}, device_id_type=MESH)
            copy.start()
            copies.append(copy)
        for copy in copies:
            copy.wait()
        total = own_ref[...]
        for d in range(n - 1):
            total = total + recv[d].astype(jnp.float32)
        o_ref[...] = total

    return pl.pallas_call(
        kernel,
        out_shape=jax.ShapeDtypeStruct(x.shape[1:], jnp.float32),
        in_specs=[VMEM_SPEC, VMEM_SPEC],
        out_specs=VMEM_SPEC,
        scratch_shapes=[
            pltpu.VMEM((n - 1,) + x.shape[1:], wire),
            pltpu.SemaphoreType.DMA((n - 1,)),
            pltpu.SemaphoreType.DMA((n - 1,)),
        ],
        compiler_params=_params(cid),
    )(x, own_part)


def all_gather(x, axis, n, cid):
    def kernel(x_ref, o_ref, ssem, rsem):
        me = lax.axis_index(axis)
        _barrier(axis, n, me)
        copies = []
        for d in range(1, n):
            peer = (me + d) % n
            copy = pltpu.make_async_remote_copy(
                x_ref, o_ref.at[me], ssem.at[d - 1], rsem.at[d - 1],
                device_id={axis: peer}, device_id_type=MESH)
            copy.start()
            copies.append(copy)
        o_ref[me] = x_ref[...]
        for copy in copies:
            copy.wait()

    return pl.pallas_call(
        kernel,
        out_shape=jax.ShapeDtypeStruct((n,) + x.shape, x.dtype),
        in_specs=[VMEM_SPEC],
        out_specs=VMEM_SPEC,
        scratch_shapes=[
            pltpu.SemaphoreType.DMA((n - 1,)),
            pltpu.SemaphoreType.DMA((n - 1,)),
        ],
        compiler_params=_params(cid),
    )(x)


def all_reduce(x, axis, cid):
    n = x.shape[0]

    def kernel(x_ref, o_ref, recv, part, ssem, rsem, gsem, hsem):
        me = lax.axis_index(axis)
        _barrier(axis, n, me)
        copies = []
        for d in range(1, n):
            peer = (me + d) % n
            copy = pltpu.make_async_remote_copy(
                x_ref.at[peer], recv.at[d - 1], ssem.at[d - 1], rsem.at[d - 1],
                device_id={axis: peer}, device_id_type=MESH)
            copy.start()
            copies.append(copy)
        for copy in copies:
            copy.wait()
        total = x_ref[me]
        for d in range(n - 1):
            total = total + recv[d]
        part[...] = total
        o_ref[me] = total
        copies = []
        for d in range(1, n):
            peer = (me + d) % n
            copy = pltpu.make_async_remote_copy(
                part, o_ref.at[me], gsem.at[d - 1], hsem.at[d - 1],
                device_id={axis: peer}, device_id_type=MESH)
            copy.start()
            copies.append(copy)
        for copy in copies:
            copy.wait()

    return pl.pallas_call(
        kernel,
        out_shape=jax.ShapeDtypeStruct(x.shape, x.dtype),
        in_specs=[VMEM_SPEC],
        out_specs=VMEM_SPEC,
        scratch_shapes=[
            pltpu.VMEM((n - 1,) + x.shape[1:], x.dtype),
            pltpu.VMEM(x.shape[1:], x.dtype),
            pltpu.SemaphoreType.DMA((n - 1,)),
            pltpu.SemaphoreType.DMA((n - 1,)),
            pltpu.SemaphoreType.DMA((n - 1,)),
            pltpu.SemaphoreType.DMA((n - 1,)),
        ],
        compiler_params=_params(cid),
    )(x)


def _grid_barrier_signals(barrier, g, p, q):
    for dp in range(g):
        for dq in range(g):
            if dp or dq:
                pl.semaphore_signal(
                    barrier, 1, device_id={"prow": (p + dp) % g, "pcol": (q + dq) % g},
                    device_id_type=MESH)


def _permute_start(x_ref, o_ref, forward, ssem, rsem, lsem):
    g = x_ref.shape[1]
    p = lax.axis_index("prow")
    q = lax.axis_index("pcol")
    own = p == q
    slot = q if forward else p
    sends = []
    local = pltpu.make_async_copy(x_ref.at[:, p], o_ref.at[:, p], lsem)
    for dj in range(g):
        j = (p + dj) % g
        dest = {"prow": j, "pcol": p} if forward else {"prow": q, "pcol": j}
        copy = pltpu.make_async_remote_copy(
            x_ref.at[:, j], o_ref.at[:, slot], ssem.at[dj], rsem.at[slot],
            device_id=dest, device_id_type=MESH)
        if dj == 0:
            @pl.when(own)
            def _():
                local.start()

            @pl.when(jnp.logical_not(own))
            def _():
                copy.start()
        else:
            copy.start()
        sends.append(copy)

    def wait():
        for dj in range(g):
            s = (p + dj) % g
            arrival = pltpu.make_async_copy(x_ref.at[:, s], o_ref.at[:, s], rsem.at[s])
            if dj == 0:
                @pl.when(own)
                def _():
                    local.wait()

                @pl.when(jnp.logical_not(own))
                def _():
                    sends[0].wait_send()
                    arrival.wait()
            else:
                sends[dj].wait_send()
                arrival.wait()

    return wait


def _permute_scratch(g):
    return [pltpu.SemaphoreType.DMA((g,)), pltpu.SemaphoreType.DMA((g,)), pltpu.SemaphoreType.DMA(())]


def permute_rows(x, forward, cid):
    g = x.shape[1]

    def kernel(x_ref, o_ref, ssem, rsem, lsem):
        p = lax.axis_index("prow")
        q = lax.axis_index("pcol")
        barrier = pltpu.get_barrier_semaphore()
        _grid_barrier_signals(barrier, g, p, q)
        pl.semaphore_wait(barrier, g * g - 1)
        _permute_start(x_ref, o_ref, forward, ssem, rsem, lsem)()

    return pl.pallas_call(
        kernel,
        out_shape=jax.ShapeDtypeStruct(x.shape, x.dtype),
        in_specs=[VMEM_SPEC],
        out_specs=VMEM_SPEC,
        scratch_shapes=_permute_scratch(g),
        compiler_params=_params(cid),
    )(x)


def root_exchange(chunks, forest, root_in, cid):
    n = chunks.shape[0]
    g = forest.shape[1]
    axis = "layer"

    def kernel(x_ref, f_ref, r_ref, o_ref, fo_ref, ro_ref, recv, part,
               ssem, rsem, gsem, hsem, fs, fr, fl, rs, rr, rl):
        me = lax.axis_index(axis)
        p = lax.axis_index("prow")
        q = lax.axis_index("pcol")
        barrier = pltpu.get_barrier_semaphore()
        for d in range(1, n):
            pl.semaphore_signal(barrier, 1, device_id={axis: (me + d) % n}, device_id_type=MESH)
        _grid_barrier_signals(barrier, g, p, q)
        pl.semaphore_wait(barrier, n - 1 + g * g - 1)
        root_wait = _permute_start(r_ref, ro_ref, True, rs, rr, rl)
        forest_wait = _permute_start(f_ref, fo_ref, False, fs, fr, fl)
        copies = []
        for d in range(1, n):
            peer = (me + d) % n
            copy = pltpu.make_async_remote_copy(
                x_ref.at[peer], recv.at[d - 1], ssem.at[d - 1], rsem.at[d - 1],
                device_id={axis: peer}, device_id_type=MESH)
            copy.start()
            copies.append(copy)
        for copy in copies:
            copy.wait()
        total = x_ref[me]
        for d in range(n - 1):
            total = total + recv[d]
        part[...] = total
        o_ref[me] = total
        copies = []
        for d in range(1, n):
            peer = (me + d) % n
            copy = pltpu.make_async_remote_copy(
                part, o_ref.at[me], gsem.at[d - 1], hsem.at[d - 1],
                device_id={axis: peer}, device_id_type=MESH)
            copy.start()
            copies.append(copy)
        for copy in copies:
            copy.wait()
        root_wait()
        forest_wait()

    return pl.pallas_call(
        kernel,
        out_shape=(
            jax.ShapeDtypeStruct(chunks.shape, chunks.dtype),
            jax.ShapeDtypeStruct(forest.shape, forest.dtype),
            jax.ShapeDtypeStruct(root_in.shape, root_in.dtype),
        ),
        in_specs=[VMEM_SPEC] * 3,
        out_specs=(VMEM_SPEC,) * 3,
        scratch_shapes=[
            pltpu.VMEM((n - 1,) + chunks.shape[1:], chunks.dtype),
            pltpu.VMEM(chunks.shape[1:], chunks.dtype),
            pltpu.SemaphoreType.DMA((n - 1,)),
            pltpu.SemaphoreType.DMA((n - 1,)),
            pltpu.SemaphoreType.DMA((n - 1,)),
            pltpu.SemaphoreType.DMA((n - 1,)),
        ] + _permute_scratch(g) + _permute_scratch(g),
        compiler_params=_params(cid),
    )(chunks, forest, root_in)


def forest_solve(local_forest, masked, inverses, cid):
    levels, g, slice_rows, cols = local_forest.shape
    rows = g * slice_rows
    f32, bf16 = jnp.float32, jnp.bfloat16

    def kernel(f_ref, w_ref, inv_ref, sol_ref, share_ref,
               placed, gath, tot, sb, rrecv, rootrecv,
               ps, pr, plsem, gs, gr, rs_s, rs_r):
        p = lax.axis_index("prow")
        q = lax.axis_index("pcol")
        barrier = pltpu.get_barrier_semaphore()
        _grid_barrier_signals(barrier, g, p, q)
        pl.semaphore_wait(barrier, g * g - 1)
        _permute_start(f_ref, placed, True, ps, pr, plsem)()
        tot[...] = jnp.zeros(tot.shape, f32)
        pending = []
        for t in range(levels):
            rhs = placed[t].reshape(rows, cols).astype(f32)
            if t > 0:
                for copy in pending:
                    copy.wait()
                red = tot[t - 1, q]
                for d in range(g - 1):
                    red = red + rrecv[t - 1, d].astype(f32)
                rhs = rhs - red
            ans = jnp.dot(inv_ref[t], rhs, precision=lax.Precision.HIGHEST,
                          preferred_element_type=f32).astype(bf16)
            sol_ref[t] = ans.reshape(g, slice_rows, cols)
            gath[t, p] = ans
            copies = []
            for d in range(1, g):
                copy = pltpu.make_async_remote_copy(
                    gath.at[t, p], gath.at[t, p], gs.at[t, d - 1], gr.at[t, d - 1],
                    device_id={"prow": (p + d) % g}, device_id_type=MESH)
                copy.start()
                copies.append(copy)
            for copy in copies:
                copy.wait()
            for target in range(t + 1, levels + 1):
                pair = pair_slot(t, target)

                def body(j, carry, t=t, target=target, pair=pair):
                    acc = tot[target - 1, j]
                    for z in range(g):
                        acc = acc + jnp.dot(w_ref[pair, j, z], gath[t, z],
                                            preferred_element_type=f32)
                    tot[target - 1, j] = acc
                    return carry

                lax.fori_loop(0, g, body, 0)
            pending = []
            if t + 1 < levels:
                sb[t] = tot[t].astype(bf16)
                src, dst = sb.at[t], rrecv.at[t]
            else:
                src, dst = tot.at[t], rootrecv
            for d in range(1, g):
                peer = (q + d) % g
                copy = pltpu.make_async_remote_copy(
                    src.at[peer], dst.at[d - 1], rs_s.at[t, d - 1], rs_r.at[t, d - 1],
                    device_id={"pcol": peer}, device_id_type=MESH)
                copy.start()
                pending.append(copy)
        for copy in pending:
            copy.wait()
        share = tot[levels - 1, q]
        for d in range(g - 1):
            share = share + rootrecv[d]
        share_ref[...] = share

    return pl.pallas_call(
        kernel,
        out_shape=(
            jax.ShapeDtypeStruct(local_forest.shape, bf16),
            jax.ShapeDtypeStruct((rows, cols), f32),
        ),
        in_specs=[VMEM_SPEC] * 3,
        out_specs=(VMEM_SPEC,) * 2,
        scratch_shapes=[
            pltpu.VMEM(local_forest.shape, bf16),
            pltpu.VMEM((levels, g, rows, cols), bf16),
            pltpu.VMEM((levels, g, rows, cols), f32),
            pltpu.VMEM((levels - 1, g, rows, cols), bf16),
            pltpu.VMEM((levels - 1, g - 1, rows, cols), bf16),
            pltpu.VMEM((g - 1, rows, cols), f32),
        ] + _permute_scratch(g) + [
            pltpu.SemaphoreType.DMA((levels, g - 1)),
            pltpu.SemaphoreType.DMA((levels, g - 1)),
            pltpu.SemaphoreType.DMA((levels, g - 1)),
            pltpu.SemaphoreType.DMA((levels, g - 1)),
        ],
        compiler_params=pltpu.CompilerParams(
            collective_id=cid, has_side_effects=True, vmem_limit_bytes=48 * 1024 * 1024),
    )(local_forest, masked, inverses)


def shards(subtree_right_hand, root_rhs, blocks, pattern, forest_inverse, root_inverse):
    grid_size = lax.axis_size("prow")
    n_layer = lax.axis_size("layer")
    super_rows = blocks.shape[-1]
    rhs_cols = subtree_right_hand.shape[-1]
    slice_rows = super_rows // grid_size
    local_forest = subtree_right_hand.reshape(3, grid_size, slice_rows, rhs_cols)
    local_root = root_rhs.reshape(1, grid_size, slice_rows, rhs_cols)
    block_mask = pattern.reshape(6, grid_size, grid_size).astype(jnp.bfloat16)
    masked = (
        blocks.reshape(6, grid_size, grid_size, super_rows, super_rows)
        * block_mask[..., None, None]
    )
    inverses = forest_inverse.reshape(3, super_rows, super_rows)
    forest_solved, row_share = forest_solve(local_forest, masked, inverses, 10)
    chunks = row_share.reshape(n_layer, -1, 128)
    reduced_root, forest_back, root_placed = root_exchange(chunks, forest_solved, local_root, 30)
    reduced_root = reduced_root.reshape(super_rows, rhs_cols)
    root_side = root_placed.reshape(super_rows, rhs_cols).astype(jnp.float32) - reduced_root
    root_answer = jnp.dot(
        root_inverse.reshape(super_rows, super_rows),
        root_side,
        precision=lax.Precision.HIGHEST,
        preferred_element_type=jnp.float32,
    ).astype(jnp.bfloat16)
    root_back = permute_rows(root_answer.reshape(1, grid_size, slice_rows, rhs_cols), False, 41)
    forest_out = forest_back.reshape(1, 3 * super_rows, rhs_cols)
    root_out = root_back.reshape(super_rows, rhs_cols)
    return (forest_out, root_out)


def solution(mesh):
    placed = (
        P("layer", ("prow", "pcol"), None),
        P(("prow", "pcol"), None),
        P("layer", None, "prow", "pcol", None, None, None, None),
        P("layer", None, "prow", "pcol", None, None),
        P("layer", None, "prow", "pcol", None, None),
        P("prow", "pcol", None, None),
    )
    return jax.shard_map(
        shards,
        mesh=mesh,
        in_specs=placed,
        out_specs=(P("layer", ("prow", "pcol"), None), P(("prow", "pcol"), None)),
        check_vma=False,
    )
```

```python
import jax
import jax.numpy as jnp
from jax import lax
from jax.experimental import pallas as pl
from jax.experimental.pallas import tpu as pltpu
from jax.sharding import PartitionSpec as P

MESH = pl.DeviceIdType.MESH
VMEM_SPEC = pl.BlockSpec(memory_space=pltpu.VMEM)


def pair_slot(source, target):
    return (0, 3, 5)[source] + target - source - 1


def _barrier(axis, n, me):
    barrier = pltpu.get_barrier_semaphore()
    for d in range(1, n):
        pl.semaphore_signal(barrier, 1, device_id={axis: (me + d) % n}, device_id_type=MESH)
    pl.semaphore_wait(barrier, n - 1)


def _params(cid):
    return pltpu.CompilerParams(collective_id=cid, has_side_effects=True)


def reduce_scatter(x, own_part, axis, cid, wire):
    n = x.shape[0]

    def kernel(x_ref, own_ref, o_ref, recv, ssem, rsem):
        me = lax.axis_index(axis)
        _barrier(axis, n, me)
        copies = []
        for d in range(1, n):
            peer = (me + d) % n
            copy = pltpu.make_async_remote_copy(
                x_ref.at[peer], recv.at[d - 1], ssem.at[d - 1], rsem.at[d - 1],
                device_id={axis: peer}, device_id_type=MESH)
            copy.start()
            copies.append(copy)
        for copy in copies:
            copy.wait()
        total = own_ref[...]
        for d in range(n - 1):
            total = total + recv[d].astype(jnp.float32)
        o_ref[...] = total

    return pl.pallas_call(
        kernel,
        out_shape=jax.ShapeDtypeStruct(x.shape[1:], jnp.float32),
        in_specs=[VMEM_SPEC, VMEM_SPEC],
        out_specs=VMEM_SPEC,
        scratch_shapes=[
            pltpu.VMEM((n - 1,) + x.shape[1:], wire),
            pltpu.SemaphoreType.DMA((n - 1,)),
            pltpu.SemaphoreType.DMA((n - 1,)),
        ],
        compiler_params=_params(cid),
    )(x, own_part)


def all_gather(x, axis, n, cid):
    def kernel(x_ref, o_ref, ssem, rsem):
        me = lax.axis_index(axis)
        _barrier(axis, n, me)
        copies = []
        for d in range(1, n):
            peer = (me + d) % n
            copy = pltpu.make_async_remote_copy(
                x_ref, o_ref.at[me], ssem.at[d - 1], rsem.at[d - 1],
                device_id={axis: peer}, device_id_type=MESH)
            copy.start()
            copies.append(copy)
        o_ref[me] = x_ref[...]
        for copy in copies:
            copy.wait()

    return pl.pallas_call(
        kernel,
        out_shape=jax.ShapeDtypeStruct((n,) + x.shape, x.dtype),
        in_specs=[VMEM_SPEC],
        out_specs=VMEM_SPEC,
        scratch_shapes=[
            pltpu.SemaphoreType.DMA((n - 1,)),
            pltpu.SemaphoreType.DMA((n - 1,)),
        ],
        compiler_params=_params(cid),
    )(x)


def all_reduce(x, axis, cid):
    n = x.shape[0]

    def kernel(x_ref, o_ref, recv, part, ssem, rsem, gsem, hsem):
        me = lax.axis_index(axis)
        _barrier(axis, n, me)
        copies = []
        for d in range(1, n):
            peer = (me + d) % n
            copy = pltpu.make_async_remote_copy(
                x_ref.at[peer], recv.at[d - 1], ssem.at[d - 1], rsem.at[d - 1],
                device_id={axis: peer}, device_id_type=MESH)
            copy.start()
            copies.append(copy)
        for copy in copies:
            copy.wait()
        total = x_ref[me]
        for d in range(n - 1):
            total = total + recv[d]
        part[...] = total
        o_ref[me] = total
        copies = []
        for d in range(1, n):
            peer = (me + d) % n
            copy = pltpu.make_async_remote_copy(
                part, o_ref.at[me], gsem.at[d - 1], hsem.at[d - 1],
                device_id={axis: peer}, device_id_type=MESH)
            copy.start()
            copies.append(copy)
        for copy in copies:
            copy.wait()

    return pl.pallas_call(
        kernel,
        out_shape=jax.ShapeDtypeStruct(x.shape, x.dtype),
        in_specs=[VMEM_SPEC],
        out_specs=VMEM_SPEC,
        scratch_shapes=[
            pltpu.VMEM((n - 1,) + x.shape[1:], x.dtype),
            pltpu.VMEM(x.shape[1:], x.dtype),
            pltpu.SemaphoreType.DMA((n - 1,)),
            pltpu.SemaphoreType.DMA((n - 1,)),
            pltpu.SemaphoreType.DMA((n - 1,)),
            pltpu.SemaphoreType.DMA((n - 1,)),
        ],
        compiler_params=_params(cid),
    )(x)


def _grid_barrier_signals(barrier, g, p, q):
    for dp in range(g):
        for dq in range(g):
            if dp or dq:
                pl.semaphore_signal(
                    barrier, 1, device_id={"prow": (p + dp) % g, "pcol": (q + dq) % g},
                    device_id_type=MESH)


def _permute_start(x_ref, o_ref, forward, ssem, rsem, lsem):
    g = x_ref.shape[1]
    p = lax.axis_index("prow")
    q = lax.axis_index("pcol")
    own = p == q
    slot = q if forward else p
    sends = []
    local = pltpu.make_async_copy(x_ref.at[:, p], o_ref.at[:, p], lsem)
    for dj in range(g):
        j = (p + dj) % g
        dest = {"prow": j, "pcol": p} if forward else {"prow": q, "pcol": j}
        copy = pltpu.make_async_remote_copy(
            x_ref.at[:, j], o_ref.at[:, slot], ssem.at[dj], rsem.at[slot],
            device_id=dest, device_id_type=MESH)
        if dj == 0:
            @pl.when(own)
            def _():
                local.start()

            @pl.when(jnp.logical_not(own))
            def _():
                copy.start()
        else:
            copy.start()
        sends.append(copy)

    def wait():
        for dj in range(g):
            s = (p + dj) % g
            arrival = pltpu.make_async_copy(x_ref.at[:, s], o_ref.at[:, s], rsem.at[s])
            if dj == 0:
                @pl.when(own)
                def _():
                    local.wait()

                @pl.when(jnp.logical_not(own))
                def _():
                    sends[0].wait_send()
                    arrival.wait()
            else:
                sends[dj].wait_send()
                arrival.wait()

    return wait


def _permute_scratch(g):
    return [pltpu.SemaphoreType.DMA((g,)), pltpu.SemaphoreType.DMA((g,)), pltpu.SemaphoreType.DMA(())]


def permute_rows(x, forward, cid):
    g = x.shape[1]

    def kernel(x_ref, o_ref, ssem, rsem, lsem):
        p = lax.axis_index("prow")
        q = lax.axis_index("pcol")
        barrier = pltpu.get_barrier_semaphore()
        _grid_barrier_signals(barrier, g, p, q)
        pl.semaphore_wait(barrier, g * g - 1)
        _permute_start(x_ref, o_ref, forward, ssem, rsem, lsem)()

    return pl.pallas_call(
        kernel,
        out_shape=jax.ShapeDtypeStruct(x.shape, x.dtype),
        in_specs=[VMEM_SPEC],
        out_specs=VMEM_SPEC,
        scratch_shapes=_permute_scratch(g),
        compiler_params=_params(cid),
    )(x)


def root_exchange(chunks, forest, root_in, cid):
    n = chunks.shape[0]
    g = forest.shape[1]
    axis = "layer"

    def kernel(x_ref, f_ref, r_ref, o_ref, fo_ref, ro_ref, recv, part,
               ssem, rsem, gsem, hsem, fs, fr, fl, rs, rr, rl):
        me = lax.axis_index(axis)
        p = lax.axis_index("prow")
        q = lax.axis_index("pcol")
        barrier = pltpu.get_barrier_semaphore()
        for d in range(1, n):
            pl.semaphore_signal(barrier, 1, device_id={axis: (me + d) % n}, device_id_type=MESH)
        _grid_barrier_signals(barrier, g, p, q)
        pl.semaphore_wait(barrier, n - 1 + g * g - 1)
        root_wait = _permute_start(r_ref, ro_ref, True, rs, rr, rl)
        forest_wait = _permute_start(f_ref, fo_ref, False, fs, fr, fl)
        copies = []
        for d in range(1, n):
            peer = (me + d) % n
            copy = pltpu.make_async_remote_copy(
                x_ref.at[peer], recv.at[d - 1], ssem.at[d - 1], rsem.at[d - 1],
                device_id={axis: peer}, device_id_type=MESH)
            copy.start()
            copies.append(copy)
        for copy in copies:
            copy.wait()
        total = x_ref[me]
        for d in range(n - 1):
            total = total + recv[d]
        part[...] = total
        o_ref[me] = total
        copies = []
        for d in range(1, n):
            peer = (me + d) % n
            copy = pltpu.make_async_remote_copy(
                part, o_ref.at[me], gsem.at[d - 1], hsem.at[d - 1],
                device_id={axis: peer}, device_id_type=MESH)
            copy.start()
            copies.append(copy)
        for copy in copies:
            copy.wait()
        root_wait()
        forest_wait()

    return pl.pallas_call(
        kernel,
        out_shape=(
            jax.ShapeDtypeStruct(chunks.shape, chunks.dtype),
            jax.ShapeDtypeStruct(forest.shape, forest.dtype),
            jax.ShapeDtypeStruct(root_in.shape, root_in.dtype),
        ),
        in_specs=[VMEM_SPEC] * 3,
        out_specs=(VMEM_SPEC,) * 3,
        scratch_shapes=[
            pltpu.VMEM((n - 1,) + chunks.shape[1:], chunks.dtype),
            pltpu.VMEM(chunks.shape[1:], chunks.dtype),
            pltpu.SemaphoreType.DMA((n - 1,)),
            pltpu.SemaphoreType.DMA((n - 1,)),
            pltpu.SemaphoreType.DMA((n - 1,)),
            pltpu.SemaphoreType.DMA((n - 1,)),
        ] + _permute_scratch(g) + _permute_scratch(g),
        compiler_params=_params(cid),
    )(chunks, forest, root_in)


def solve_all(local_forest, local_root, masked, inverses, root_inverse, n_layer, cid):
    levels, g, slice_rows, cols = local_forest.shape
    rows = g * slice_rows
    f32, bf16 = jnp.float32, jnp.bfloat16
    row_blocks = rows // 8
    col_parts = n_layer // row_blocks
    chunk_cols = cols // col_parts

    def chunk(ref, c):
        r0 = pl.multiple_of((c // col_parts) * 8, 8)
        c0 = pl.multiple_of((c % col_parts) * chunk_cols, chunk_cols)
        return ref.at[pl.ds(r0, 8), pl.ds(c0, chunk_cols)]

    def kernel(f_ref, r_ref, w_ref, inv_ref, rinv_ref, fo_ref, ro_ref,
               placed, placed_root, sol, root_sol, gath, tot, sb, rrecv, rootrecv,
               share_buf, recv_layer, part, full,
               gs, gr, rs_s, rs_r, ls, lr, hs, hr, *perm_sems):
        p = lax.axis_index("prow")
        q = lax.axis_index("pcol")
        me = lax.axis_index("layer")
        perm = [perm_sems[3 * i:3 * i + 3] for i in range(levels + 3)]
        barrier = pltpu.get_barrier_semaphore()
        _grid_barrier_signals(barrier, g, p, q)
        for d in range(1, n_layer):
            pl.semaphore_signal(barrier, 1, device_id={"layer": (me + d) % n_layer},
                                device_id_type=MESH)
        pl.semaphore_wait(barrier, g * g - 1 + n_layer - 1)
        forest_in = _permute_start(f_ref, placed, True, *perm[0])
        root_in = _permute_start(r_ref, placed_root, True, *perm[1])
        forest_in()
        tot[...] = jnp.zeros(tot.shape, f32)
        pending = []
        outs = []
        for t in range(levels):
            rhs = placed[t].reshape(rows, cols).astype(f32)
            if t > 0:
                for copy in pending:
                    copy.wait()
                red = tot[t - 1, q]
                for d in range(g - 1):
                    red = red + rrecv[t - 1, d].astype(f32)
                rhs = rhs - red
            ans = jnp.dot(inv_ref[t], rhs, precision=lax.Precision.HIGHEST,
                          preferred_element_type=f32).astype(bf16)
            sol[t] = ans.reshape(g, slice_rows, cols)
            gath[t, p] = ans
            copies = []
            for d in range(1, g):
                copy = pltpu.make_async_remote_copy(
                    gath.at[t, p], gath.at[t, p], gs.at[t, d - 1], gr.at[t, d - 1],
                    device_id={"prow": (p + d) % g}, device_id_type=MESH)
                copy.start()
                copies.append(copy)
            outs.append(_permute_start(sol.at[pl.ds(t, 1)], fo_ref.at[pl.ds(t, 1)], False,
                                       *perm[3 + t]))
            for copy in copies:
                copy.wait()
            for target in range(t + 1, levels + 1):
                pair = pair_slot(t, target)

                def body(j, carry, t=t, target=target, pair=pair):
                    acc = tot[target - 1, j]
                    for z in range(g):
                        acc = acc + jnp.dot(w_ref[pair, j, z], gath[t, z],
                                            preferred_element_type=f32)
                    tot[target - 1, j] = acc
                    return carry

                lax.fori_loop(0, g, body, 0)
            pending = []
            if t + 1 < levels:
                sb[t] = tot[t].astype(bf16)
                src, dst = sb.at[t], rrecv.at[t]
            else:
                src, dst = tot.at[t], rootrecv
            for d in range(1, g):
                peer = (q + d) % g
                copy = pltpu.make_async_remote_copy(
                    src.at[peer], dst.at[d - 1], rs_s.at[t, d - 1], rs_r.at[t, d - 1],
                    device_id={"pcol": peer}, device_id_type=MESH)
                copy.start()
                pending.append(copy)
        for copy in pending:
            copy.wait()
        share = tot[levels - 1, q]
        for d in range(g - 1):
            share = share + rootrecv[d]
        share_buf[...] = share
        copies = []
        for d in range(1, n_layer):
            peer = (me + d) % n_layer
            copy = pltpu.make_async_remote_copy(
                chunk(share_buf, peer), recv_layer.at[d - 1], ls.at[d - 1], lr.at[d - 1],
                device_id={"layer": peer}, device_id_type=MESH)
            copy.start()
            copies.append(copy)
        for copy in copies:
            copy.wait()
        r0 = pl.multiple_of((me // col_parts) * 8, 8)
        c0 = pl.multiple_of((me % col_parts) * chunk_cols, chunk_cols)
        total = share_buf[pl.ds(r0, 8), pl.ds(c0, chunk_cols)]
        for d in range(n_layer - 1):
            total = total + recv_layer[d]
        part[...] = total
        full[pl.ds(r0, 8), pl.ds(c0, chunk_cols)] = total
        copies = []
        for d in range(1, n_layer):
            peer = (me + d) % n_layer
            copy = pltpu.make_async_remote_copy(
                part, chunk(full, me), hs.at[d - 1], hr.at[d - 1],
                device_id={"layer": peer}, device_id_type=MESH)
            copy.start()
            copies.append(copy)
        for copy in copies:
            copy.wait()
        root_in()
        side = placed_root[0].reshape(rows, cols).astype(f32) - full[...]
        answer = jnp.dot(rinv_ref[...], side, precision=lax.Precision.HIGHEST,
                         preferred_element_type=f32).astype(bf16)
        root_sol[0] = answer.reshape(g, slice_rows, cols)
        root_out = _permute_start(root_sol, ro_ref, False, *perm[2])
        for wait in outs:
            wait()
        root_out()

    return pl.pallas_call(
        kernel,
        out_shape=(
            jax.ShapeDtypeStruct(local_forest.shape, bf16),
            jax.ShapeDtypeStruct(local_root.shape, bf16),
        ),
        in_specs=[VMEM_SPEC] * 5,
        out_specs=(VMEM_SPEC,) * 2,
        scratch_shapes=[
            pltpu.VMEM(local_forest.shape, bf16),
            pltpu.VMEM(local_root.shape, bf16),
            pltpu.VMEM(local_forest.shape, bf16),
            pltpu.VMEM(local_root.shape, bf16),
            pltpu.VMEM((levels, g, rows, cols), bf16),
            pltpu.VMEM((levels, g, rows, cols), f32),
            pltpu.VMEM((levels - 1, g, rows, cols), bf16),
            pltpu.VMEM((levels - 1, g - 1, rows, cols), bf16),
            pltpu.VMEM((g - 1, rows, cols), f32),
            pltpu.VMEM((rows, cols), f32),
            pltpu.VMEM((n_layer - 1, 8, chunk_cols), f32),
            pltpu.VMEM((8, chunk_cols), f32),
            pltpu.VMEM((rows, cols), f32),
            pltpu.SemaphoreType.DMA((levels, g - 1)),
            pltpu.SemaphoreType.DMA((levels, g - 1)),
            pltpu.SemaphoreType.DMA((levels, g - 1)),
            pltpu.SemaphoreType.DMA((levels, g - 1)),
            pltpu.SemaphoreType.DMA((n_layer - 1,)),
            pltpu.SemaphoreType.DMA((n_layer - 1,)),
            pltpu.SemaphoreType.DMA((n_layer - 1,)),
            pltpu.SemaphoreType.DMA((n_layer - 1,)),
        ] + _permute_scratch(g) * (levels + 3),
        compiler_params=pltpu.CompilerParams(
            collective_id=cid, has_side_effects=True, vmem_limit_bytes=48 * 1024 * 1024),
    )(local_forest, local_root, masked, inverses, root_inverse)


def shards(subtree_right_hand, root_rhs, blocks, pattern, forest_inverse, root_inverse):
    grid_size = lax.axis_size("prow")
    n_layer = lax.axis_size("layer")
    super_rows = blocks.shape[-1]
    rhs_cols = subtree_right_hand.shape[-1]
    slice_rows = super_rows // grid_size
    local_forest = subtree_right_hand.reshape(3, grid_size, slice_rows, rhs_cols)
    local_root = root_rhs.reshape(1, grid_size, slice_rows, rhs_cols)
    block_mask = pattern.reshape(6, grid_size, grid_size).astype(jnp.bfloat16)
    masked = (
        blocks.reshape(6, grid_size, grid_size, super_rows, super_rows)
        * block_mask[..., None, None]
    )
    inverses = forest_inverse.reshape(3, super_rows, super_rows)
    forest_back, root_back = solve_all(
        local_forest, local_root, masked, inverses,
        root_inverse.reshape(super_rows, super_rows), n_layer, 10)
    forest_out = forest_back.reshape(1, 3 * super_rows, rhs_cols)
    root_out = root_back.reshape(super_rows, rhs_cols)
    return (forest_out, root_out)


def solution(mesh):
    placed = (
        P("layer", ("prow", "pcol"), None),
        P(("prow", "pcol"), None),
        P("layer", None, "prow", "pcol", None, None, None, None),
        P("layer", None, "prow", "pcol", None, None),
        P("layer", None, "prow", "pcol", None, None),
        P("prow", "pcol", None, None),
    )
    return jax.shard_map(
        shards,
        mesh=mesh,
        in_specs=placed,
        out_specs=(P("layer", ("prow", "pcol"), None), P(("prow", "pcol"), None)),
        check_vma=False,
    )
```

```python
import jax
import jax.numpy as jnp
from jax import lax
from jax.experimental import pallas as pl
from jax.experimental.pallas import tpu as pltpu
from jax.sharding import PartitionSpec as P

MESH = pl.DeviceIdType.MESH
VMEM_SPEC = pl.BlockSpec(memory_space=pltpu.VMEM)


def pair_slot(source, target):
    return (0, 3, 5)[source] + target - source - 1


def _barrier(axis, n, me):
    barrier = pltpu.get_barrier_semaphore()
    for d in range(1, n):
        pl.semaphore_signal(barrier, 1, device_id={axis: (me + d) % n}, device_id_type=MESH)
    pl.semaphore_wait(barrier, n - 1)


def _params(cid):
    return pltpu.CompilerParams(collective_id=cid, has_side_effects=True)


def reduce_scatter(x, own_part, axis, cid, wire):
    n = x.shape[0]

    def kernel(x_ref, own_ref, o_ref, recv, ssem, rsem):
        me = lax.axis_index(axis)
        _barrier(axis, n, me)
        copies = []
        for d in range(1, n):
            peer = (me + d) % n
            copy = pltpu.make_async_remote_copy(
                x_ref.at[peer], recv.at[d - 1], ssem.at[d - 1], rsem.at[d - 1],
                device_id={axis: peer}, device_id_type=MESH)
            copy.start()
            copies.append(copy)
        for copy in copies:
            copy.wait()
        total = own_ref[...]
        for d in range(n - 1):
            total = total + recv[d].astype(jnp.float32)
        o_ref[...] = total

    return pl.pallas_call(
        kernel,
        out_shape=jax.ShapeDtypeStruct(x.shape[1:], jnp.float32),
        in_specs=[VMEM_SPEC, VMEM_SPEC],
        out_specs=VMEM_SPEC,
        scratch_shapes=[
            pltpu.VMEM((n - 1,) + x.shape[1:], wire),
            pltpu.SemaphoreType.DMA((n - 1,)),
            pltpu.SemaphoreType.DMA((n - 1,)),
        ],
        compiler_params=_params(cid),
    )(x, own_part)


def all_gather(x, axis, n, cid):
    def kernel(x_ref, o_ref, ssem, rsem):
        me = lax.axis_index(axis)
        _barrier(axis, n, me)
        copies = []
        for d in range(1, n):
            peer = (me + d) % n
            copy = pltpu.make_async_remote_copy(
                x_ref, o_ref.at[me], ssem.at[d - 1], rsem.at[d - 1],
                device_id={axis: peer}, device_id_type=MESH)
            copy.start()
            copies.append(copy)
        o_ref[me] = x_ref[...]
        for copy in copies:
            copy.wait()

    return pl.pallas_call(
        kernel,
        out_shape=jax.ShapeDtypeStruct((n,) + x.shape, x.dtype),
        in_specs=[VMEM_SPEC],
        out_specs=VMEM_SPEC,
        scratch_shapes=[
            pltpu.SemaphoreType.DMA((n - 1,)),
            pltpu.SemaphoreType.DMA((n - 1,)),
        ],
        compiler_params=_params(cid),
    )(x)


def all_reduce(x, axis, cid):
    n = x.shape[0]

    def kernel(x_ref, o_ref, recv, part, ssem, rsem, gsem, hsem):
        me = lax.axis_index(axis)
        _barrier(axis, n, me)
        copies = []
        for d in range(1, n):
            peer = (me + d) % n
            copy = pltpu.make_async_remote_copy(
                x_ref.at[peer], recv.at[d - 1], ssem.at[d - 1], rsem.at[d - 1],
                device_id={axis: peer}, device_id_type=MESH)
            copy.start()
            copies.append(copy)
        for copy in copies:
            copy.wait()
        total = x_ref[me]
        for d in range(n - 1):
            total = total + recv[d]
        part[...] = total
        o_ref[me] = total
        copies = []
        for d in range(1, n):
            peer = (me + d) % n
            copy = pltpu.make_async_remote_copy(
                part, o_ref.at[me], gsem.at[d - 1], hsem.at[d - 1],
                device_id={axis: peer}, device_id_type=MESH)
            copy.start()
            copies.append(copy)
        for copy in copies:
            copy.wait()

    return pl.pallas_call(
        kernel,
        out_shape=jax.ShapeDtypeStruct(x.shape, x.dtype),
        in_specs=[VMEM_SPEC],
        out_specs=VMEM_SPEC,
        scratch_shapes=[
            pltpu.VMEM((n - 1,) + x.shape[1:], x.dtype),
            pltpu.VMEM(x.shape[1:], x.dtype),
            pltpu.SemaphoreType.DMA((n - 1,)),
            pltpu.SemaphoreType.DMA((n - 1,)),
            pltpu.SemaphoreType.DMA((n - 1,)),
            pltpu.SemaphoreType.DMA((n - 1,)),
        ],
        compiler_params=_params(cid),
    )(x)


def _grid_barrier_signals(barrier, g, p, q):
    for dp in range(g):
        for dq in range(g):
            if dp or dq:
                pl.semaphore_signal(
                    barrier, 1, device_id={"prow": (p + dp) % g, "pcol": (q + dq) % g},
                    device_id_type=MESH)


def _permute_start(x_ref, o_ref, forward, ssem, rsem, lsem):
    g = x_ref.shape[1]
    p = lax.axis_index("prow")
    q = lax.axis_index("pcol")
    own = p == q
    slot = q if forward else p
    sends = []
    local = pltpu.make_async_copy(x_ref.at[:, p], o_ref.at[:, p], lsem)
    for dj in range(g):
        j = (p + dj) % g
        dest = {"prow": j, "pcol": p} if forward else {"prow": q, "pcol": j}
        copy = pltpu.make_async_remote_copy(
            x_ref.at[:, j], o_ref.at[:, slot], ssem.at[dj], rsem.at[slot],
            device_id=dest, device_id_type=MESH)
        if dj == 0:
            @pl.when(own)
            def _():
                local.start()

            @pl.when(jnp.logical_not(own))
            def _():
                copy.start()
        else:
            copy.start()
        sends.append(copy)

    def wait():
        for dj in range(g):
            s = (p + dj) % g
            arrival = pltpu.make_async_copy(x_ref.at[:, s], o_ref.at[:, s], rsem.at[s])
            if dj == 0:
                @pl.when(own)
                def _():
                    local.wait()

                @pl.when(jnp.logical_not(own))
                def _():
                    sends[0].wait_send()
                    arrival.wait()
            else:
                sends[dj].wait_send()
                arrival.wait()

    return wait


def _permute_scratch(g):
    return [pltpu.SemaphoreType.DMA((g,)), pltpu.SemaphoreType.DMA((g,)), pltpu.SemaphoreType.DMA(())]


def permute_rows(x, forward, cid):
    g = x.shape[1]

    def kernel(x_ref, o_ref, ssem, rsem, lsem):
        p = lax.axis_index("prow")
        q = lax.axis_index("pcol")
        barrier = pltpu.get_barrier_semaphore()
        _grid_barrier_signals(barrier, g, p, q)
        pl.semaphore_wait(barrier, g * g - 1)
        _permute_start(x_ref, o_ref, forward, ssem, rsem, lsem)()

    return pl.pallas_call(
        kernel,
        out_shape=jax.ShapeDtypeStruct(x.shape, x.dtype),
        in_specs=[VMEM_SPEC],
        out_specs=VMEM_SPEC,
        scratch_shapes=_permute_scratch(g),
        compiler_params=_params(cid),
    )(x)


def root_exchange(chunks, forest, root_in, cid):
    n = chunks.shape[0]
    g = forest.shape[1]
    axis = "layer"

    def kernel(x_ref, f_ref, r_ref, o_ref, fo_ref, ro_ref, recv, part,
               ssem, rsem, gsem, hsem, fs, fr, fl, rs, rr, rl):
        me = lax.axis_index(axis)
        p = lax.axis_index("prow")
        q = lax.axis_index("pcol")
        barrier = pltpu.get_barrier_semaphore()
        for d in range(1, n):
            pl.semaphore_signal(barrier, 1, device_id={axis: (me + d) % n}, device_id_type=MESH)
        _grid_barrier_signals(barrier, g, p, q)
        pl.semaphore_wait(barrier, n - 1 + g * g - 1)
        root_wait = _permute_start(r_ref, ro_ref, True, rs, rr, rl)
        forest_wait = _permute_start(f_ref, fo_ref, False, fs, fr, fl)
        copies = []
        for d in range(1, n):
            peer = (me + d) % n
            copy = pltpu.make_async_remote_copy(
                x_ref.at[peer], recv.at[d - 1], ssem.at[d - 1], rsem.at[d - 1],
                device_id={axis: peer}, device_id_type=MESH)
            copy.start()
            copies.append(copy)
        for copy in copies:
            copy.wait()
        total = x_ref[me]
        for d in range(n - 1):
            total = total + recv[d]
        part[...] = total
        o_ref[me] = total
        copies = []
        for d in range(1, n):
            peer = (me + d) % n
            copy = pltpu.make_async_remote_copy(
                part, o_ref.at[me], gsem.at[d - 1], hsem.at[d - 1],
                device_id={axis: peer}, device_id_type=MESH)
            copy.start()
            copies.append(copy)
        for copy in copies:
            copy.wait()
        root_wait()
        forest_wait()

    return pl.pallas_call(
        kernel,
        out_shape=(
            jax.ShapeDtypeStruct(chunks.shape, chunks.dtype),
            jax.ShapeDtypeStruct(forest.shape, forest.dtype),
            jax.ShapeDtypeStruct(root_in.shape, root_in.dtype),
        ),
        in_specs=[VMEM_SPEC] * 3,
        out_specs=(VMEM_SPEC,) * 3,
        scratch_shapes=[
            pltpu.VMEM((n - 1,) + chunks.shape[1:], chunks.dtype),
            pltpu.VMEM(chunks.shape[1:], chunks.dtype),
            pltpu.SemaphoreType.DMA((n - 1,)),
            pltpu.SemaphoreType.DMA((n - 1,)),
            pltpu.SemaphoreType.DMA((n - 1,)),
            pltpu.SemaphoreType.DMA((n - 1,)),
        ] + _permute_scratch(g) + _permute_scratch(g),
        compiler_params=_params(cid),
    )(chunks, forest, root_in)


def solve_all(local_forest, local_root, factors, pattern, inverses, root_inverse, n_layer, cid):
    levels, g, slice_rows, cols = local_forest.shape
    rows = g * slice_rows
    f32, bf16 = jnp.float32, jnp.bfloat16
    row_blocks = rows // 8
    col_parts = n_layer // row_blocks
    chunk_cols = cols // col_parts

    def chunk(ref, c):
        r0 = pl.multiple_of((c // col_parts) * 8, 8)
        c0 = pl.multiple_of((c % col_parts) * chunk_cols, chunk_cols)
        return ref.at[pl.ds(r0, 8), pl.ds(c0, chunk_cols)]

    def kernel(f_ref, r_ref, w_ref, pat_ref, inv_ref, rinv_ref, fo_ref, ro_ref,
               placed, placed_root, sol, root_sol, gath, tot, sb, rrecv, rootrecv,
               share_buf, recv_layer, part, full,
               gs, gr, rs_s, rs_r, ls, lr, hs, hr, *perm_sems):
        p = lax.axis_index("prow")
        q = lax.axis_index("pcol")
        me = lax.axis_index("layer")
        perm = [perm_sems[3 * i:3 * i + 3] for i in range(levels + 3)]
        barrier = pltpu.get_barrier_semaphore()
        _grid_barrier_signals(barrier, g, p, q)
        for d in range(1, n_layer):
            pl.semaphore_signal(barrier, 1, device_id={"layer": (me + d) % n_layer},
                                device_id_type=MESH)
        pl.semaphore_wait(barrier, g * g - 1 + n_layer - 1)
        forest_in = _permute_start(f_ref, placed, True, *perm[0])
        root_in = _permute_start(r_ref, placed_root, True, *perm[1])
        tot[...] = jnp.zeros(tot.shape, f32)
        forest_in()
        pending = []
        outs = []
        for t in range(levels):
            rhs = placed[t].reshape(rows, cols).astype(f32)
            if t > 0:
                for copy in pending:
                    copy.wait()
                red = tot[t - 1, q]
                for d in range(g - 1):
                    red = red + rrecv[t - 1, d].astype(f32)
                rhs = rhs - red
            ans = jnp.dot(inv_ref[t], rhs, precision=lax.Precision.HIGHEST,
                          preferred_element_type=f32).astype(bf16)
            sol[t] = ans.reshape(g, slice_rows, cols)
            gath[t, p] = ans
            copies = []
            for d in range(1, g):
                copy = pltpu.make_async_remote_copy(
                    gath.at[t, p], gath.at[t, p], gs.at[t, d - 1], gr.at[t, d - 1],
                    device_id={"prow": (p + d) % g}, device_id_type=MESH)
                copy.start()
                copies.append(copy)
            outs.append(_permute_start(sol.at[pl.ds(t, 1)], fo_ref.at[pl.ds(t, 1)], False,
                                       *perm[3 + t]))
            for copy in copies:
                copy.wait()
            for target in range(t + 1, levels + 1):
                pair = pair_slot(t, target)

                def body(j, carry, t=t, target=target, pair=pair):
                    acc = tot[target - 1, j]
                    for z in range(g):
                        present = pat_ref[pair, j, z].astype(f32).astype(bf16)
                        acc = acc + jnp.dot(w_ref[pair, j, z] * present, gath[t, z],
                                            preferred_element_type=f32)
                    tot[target - 1, j] = acc
                    return carry

                lax.fori_loop(0, g, body, 0)
            pending = []
            if t + 1 < levels:
                sb[t] = tot[t].astype(bf16)
                src, dst = sb.at[t], rrecv.at[t]
            else:
                src, dst = tot.at[t], rootrecv
            for d in range(1, g):
                peer = (q + d) % g
                copy = pltpu.make_async_remote_copy(
                    src.at[peer], dst.at[d - 1], rs_s.at[t, d - 1], rs_r.at[t, d - 1],
                    device_id={"pcol": peer}, device_id_type=MESH)
                copy.start()
                pending.append(copy)
        for copy in pending:
            copy.wait()
        share = tot[levels - 1, q]
        for d in range(g - 1):
            share = share + rootrecv[d]
        share_buf[...] = share
        copies = []
        for d in range(1, n_layer):
            peer = (me + d) % n_layer
            copy = pltpu.make_async_remote_copy(
                chunk(share_buf, peer), recv_layer.at[d - 1], ls.at[d - 1], lr.at[d - 1],
                device_id={"layer": peer}, device_id_type=MESH)
            copy.start()
            copies.append(copy)
        for copy in copies:
            copy.wait()
        r0 = pl.multiple_of((me // col_parts) * 8, 8)
        c0 = pl.multiple_of((me % col_parts) * chunk_cols, chunk_cols)
        total = share_buf[pl.ds(r0, 8), pl.ds(c0, chunk_cols)]
        for d in range(n_layer - 1):
            total = total + recv_layer[d]
        part[...] = total
        full[pl.ds(r0, 8), pl.ds(c0, chunk_cols)] = total
        copies = []
        for d in range(1, n_layer):
            peer = (me + d) % n_layer
            copy = pltpu.make_async_remote_copy(
                part, chunk(full, me), hs.at[d - 1], hr.at[d - 1],
                device_id={"layer": peer}, device_id_type=MESH)
            copy.start()
            copies.append(copy)
        for copy in copies:
            copy.wait()
        root_in()
        side = placed_root[0].reshape(rows, cols).astype(f32) - full[...]
        answer = jnp.dot(rinv_ref[...], side, precision=lax.Precision.HIGHEST,
                         preferred_element_type=f32).astype(bf16)
        root_sol[0] = answer.reshape(g, slice_rows, cols)
        root_out = _permute_start(root_sol, ro_ref, False, *perm[2])
        for wait in outs:
            wait()
        root_out()

    return pl.pallas_call(
        kernel,
        out_shape=(
            jax.ShapeDtypeStruct(local_forest.shape, bf16),
            jax.ShapeDtypeStruct(local_root.shape, bf16),
        ),
        in_specs=[VMEM_SPEC, VMEM_SPEC, VMEM_SPEC,
                  pl.BlockSpec(memory_space=pltpu.SMEM), VMEM_SPEC, VMEM_SPEC],
        out_specs=(VMEM_SPEC,) * 2,
        scratch_shapes=[
            pltpu.VMEM(local_forest.shape, bf16),
            pltpu.VMEM(local_root.shape, bf16),
            pltpu.VMEM(local_forest.shape, bf16),
            pltpu.VMEM(local_root.shape, bf16),
            pltpu.VMEM((levels, g, rows, cols), bf16),
            pltpu.VMEM((levels, g, rows, cols), f32),
            pltpu.VMEM((levels - 1, g, rows, cols), bf16),
            pltpu.VMEM((levels - 1, g - 1, rows, cols), bf16),
            pltpu.VMEM((g - 1, rows, cols), f32),
            pltpu.VMEM((rows, cols), f32),
            pltpu.VMEM((n_layer - 1, 8, chunk_cols), f32),
            pltpu.VMEM((8, chunk_cols), f32),
            pltpu.VMEM((rows, cols), f32),
            pltpu.SemaphoreType.DMA((levels, g - 1)),
            pltpu.SemaphoreType.DMA((levels, g - 1)),
            pltpu.SemaphoreType.DMA((levels, g - 1)),
            pltpu.SemaphoreType.DMA((levels, g - 1)),
            pltpu.SemaphoreType.DMA((n_layer - 1,)),
            pltpu.SemaphoreType.DMA((n_layer - 1,)),
            pltpu.SemaphoreType.DMA((n_layer - 1,)),
            pltpu.SemaphoreType.DMA((n_layer - 1,)),
        ] + _permute_scratch(g) * (levels + 3),
        compiler_params=pltpu.CompilerParams(
            collective_id=cid, has_side_effects=True, vmem_limit_bytes=48 * 1024 * 1024),
    )(local_forest, local_root, factors, pattern, inverses, root_inverse)


def shards(subtree_right_hand, root_rhs, blocks, pattern, forest_inverse, root_inverse):
    grid_size = lax.axis_size("prow")
    n_layer = lax.axis_size("layer")
    super_rows = blocks.shape[-1]
    rhs_cols = subtree_right_hand.shape[-1]
    slice_rows = super_rows // grid_size
    local_forest = subtree_right_hand.reshape(3, grid_size, slice_rows, rhs_cols)
    local_root = root_rhs.reshape(1, grid_size, slice_rows, rhs_cols)
    factors = blocks.reshape(6, grid_size, grid_size, super_rows, super_rows)
    present = pattern.reshape(6, grid_size, grid_size)
    inverses = forest_inverse.reshape(3, super_rows, super_rows)
    forest_back, root_back = solve_all(
        local_forest, local_root, factors, present, inverses,
        root_inverse.reshape(super_rows, super_rows), n_layer, 10)
    forest_out = forest_back.reshape(1, 3 * super_rows, rhs_cols)
    root_out = root_back.reshape(super_rows, rhs_cols)
    return (forest_out, root_out)


def solution(mesh):
    placed = (
        P("layer", ("prow", "pcol"), None),
        P(("prow", "pcol"), None),
        P("layer", None, "prow", "pcol", None, None, None, None),
        P("layer", None, "prow", "pcol", None, None),
        P("layer", None, "prow", "pcol", None, None),
        P("prow", "pcol", None, None),
    )
    return jax.shard_map(
        shards,
        mesh=mesh,
        in_specs=placed,
        out_specs=(P("layer", ("prow", "pcol"), None), P(("prow", "pcol"), None)),
        check_vma=False,
    )
```

```python
import jax
import jax.numpy as jnp
from jax import lax
from jax.experimental import pallas as pl
from jax.experimental.pallas import tpu as pltpu
from jax.sharding import PartitionSpec as P

MESH = pl.DeviceIdType.MESH
VMEM_SPEC = pl.BlockSpec(memory_space=pltpu.VMEM)
ANY_SPEC = pl.BlockSpec(memory_space=pl.ANY)


def pair_slot(source, target):
    return (0, 3, 5)[source] + target - source - 1


def _barrier(axis, n, me):
    barrier = pltpu.get_barrier_semaphore()
    for d in range(1, n):
        pl.semaphore_signal(barrier, 1, device_id={axis: (me + d) % n}, device_id_type=MESH)
    pl.semaphore_wait(barrier, n - 1)


def _params(cid):
    return pltpu.CompilerParams(collective_id=cid, has_side_effects=True)


def reduce_scatter(x, own_part, axis, cid, wire):
    n = x.shape[0]

    def kernel(x_ref, own_ref, o_ref, recv, ssem, rsem):
        me = lax.axis_index(axis)
        _barrier(axis, n, me)
        copies = []
        for d in range(1, n):
            peer = (me + d) % n
            copy = pltpu.make_async_remote_copy(
                x_ref.at[peer], recv.at[d - 1], ssem.at[d - 1], rsem.at[d - 1],
                device_id={axis: peer}, device_id_type=MESH)
            copy.start()
            copies.append(copy)
        for copy in copies:
            copy.wait()
        total = own_ref[...]
        for d in range(n - 1):
            total = total + recv[d].astype(jnp.float32)
        o_ref[...] = total

    return pl.pallas_call(
        kernel,
        out_shape=jax.ShapeDtypeStruct(x.shape[1:], jnp.float32),
        in_specs=[VMEM_SPEC, VMEM_SPEC],
        out_specs=VMEM_SPEC,
        scratch_shapes=[
            pltpu.VMEM((n - 1,) + x.shape[1:], wire),
            pltpu.SemaphoreType.DMA((n - 1,)),
            pltpu.SemaphoreType.DMA((n - 1,)),
        ],
        compiler_params=_params(cid),
    )(x, own_part)


def all_gather(x, axis, n, cid):
    def kernel(x_ref, o_ref, ssem, rsem):
        me = lax.axis_index(axis)
        _barrier(axis, n, me)
        copies = []
        for d in range(1, n):
            peer = (me + d) % n
            copy = pltpu.make_async_remote_copy(
                x_ref, o_ref.at[me], ssem.at[d - 1], rsem.at[d - 1],
                device_id={axis: peer}, device_id_type=MESH)
            copy.start()
            copies.append(copy)
        o_ref[me] = x_ref[...]
        for copy in copies:
            copy.wait()

    return pl.pallas_call(
        kernel,
        out_shape=jax.ShapeDtypeStruct((n,) + x.shape, x.dtype),
        in_specs=[VMEM_SPEC],
        out_specs=VMEM_SPEC,
        scratch_shapes=[
            pltpu.SemaphoreType.DMA((n - 1,)),
            pltpu.SemaphoreType.DMA((n - 1,)),
        ],
        compiler_params=_params(cid),
    )(x)


def all_reduce(x, axis, cid):
    n = x.shape[0]

    def kernel(x_ref, o_ref, recv, part, ssem, rsem, gsem, hsem):
        me = lax.axis_index(axis)
        _barrier(axis, n, me)
        copies = []
        for d in range(1, n):
            peer = (me + d) % n
            copy = pltpu.make_async_remote_copy(
                x_ref.at[peer], recv.at[d - 1], ssem.at[d - 1], rsem.at[d - 1],
                device_id={axis: peer}, device_id_type=MESH)
            copy.start()
            copies.append(copy)
        for copy in copies:
            copy.wait()
        total = x_ref[me]
        for d in range(n - 1):
            total = total + recv[d]
        part[...] = total
        o_ref[me] = total
        copies = []
        for d in range(1, n):
            peer = (me + d) % n
            copy = pltpu.make_async_remote_copy(
                part, o_ref.at[me], gsem.at[d - 1], hsem.at[d - 1],
                device_id={axis: peer}, device_id_type=MESH)
            copy.start()
            copies.append(copy)
        for copy in copies:
            copy.wait()

    return pl.pallas_call(
        kernel,
        out_shape=jax.ShapeDtypeStruct(x.shape, x.dtype),
        in_specs=[VMEM_SPEC],
        out_specs=VMEM_SPEC,
        scratch_shapes=[
            pltpu.VMEM((n - 1,) + x.shape[1:], x.dtype),
            pltpu.VMEM(x.shape[1:], x.dtype),
            pltpu.SemaphoreType.DMA((n - 1,)),
            pltpu.SemaphoreType.DMA((n - 1,)),
            pltpu.SemaphoreType.DMA((n - 1,)),
            pltpu.SemaphoreType.DMA((n - 1,)),
        ],
        compiler_params=_params(cid),
    )(x)


def _grid_barrier_signals(barrier, g, p, q):
    for dp in range(g):
        for dq in range(g):
            if dp or dq:
                pl.semaphore_signal(
                    barrier, 1, device_id={"prow": (p + dp) % g, "pcol": (q + dq) % g},
                    device_id_type=MESH)


def _permute_start(x_ref, o_ref, forward, ssem, rsem, lsem):
    g = x_ref.shape[1]
    p = lax.axis_index("prow")
    q = lax.axis_index("pcol")
    own = p == q
    slot = q if forward else p
    sends = []
    local = pltpu.make_async_copy(x_ref.at[:, p], o_ref.at[:, p], lsem)
    for dj in range(g):
        j = (p + dj) % g
        dest = {"prow": j, "pcol": p} if forward else {"prow": q, "pcol": j}
        copy = pltpu.make_async_remote_copy(
            x_ref.at[:, j], o_ref.at[:, slot], ssem.at[dj], rsem.at[slot],
            device_id=dest, device_id_type=MESH)
        if dj == 0:
            @pl.when(own)
            def _():
                local.start()

            @pl.when(jnp.logical_not(own))
            def _():
                copy.start()
        else:
            copy.start()
        sends.append(copy)

    def wait():
        for dj in range(g):
            s = (p + dj) % g
            arrival = pltpu.make_async_copy(x_ref.at[:, s], o_ref.at[:, s], rsem.at[s])
            if dj == 0:
                @pl.when(own)
                def _():
                    local.wait()

                @pl.when(jnp.logical_not(own))
                def _():
                    sends[0].wait_send()
                    arrival.wait()
            else:
                sends[dj].wait_send()
                arrival.wait()

    return wait


def _permute_scratch(g):
    return [pltpu.SemaphoreType.DMA((g,)), pltpu.SemaphoreType.DMA((g,)), pltpu.SemaphoreType.DMA(())]


def permute_rows(x, forward, cid):
    g = x.shape[1]

    def kernel(x_ref, o_ref, ssem, rsem, lsem):
        p = lax.axis_index("prow")
        q = lax.axis_index("pcol")
        barrier = pltpu.get_barrier_semaphore()
        _grid_barrier_signals(barrier, g, p, q)
        pl.semaphore_wait(barrier, g * g - 1)
        _permute_start(x_ref, o_ref, forward, ssem, rsem, lsem)()

    return pl.pallas_call(
        kernel,
        out_shape=jax.ShapeDtypeStruct(x.shape, x.dtype),
        in_specs=[VMEM_SPEC],
        out_specs=VMEM_SPEC,
        scratch_shapes=_permute_scratch(g),
        compiler_params=_params(cid),
    )(x)


def root_exchange(chunks, forest, root_in, cid):
    n = chunks.shape[0]
    g = forest.shape[1]
    axis = "layer"

    def kernel(x_ref, f_ref, r_ref, o_ref, fo_ref, ro_ref, recv, part,
               ssem, rsem, gsem, hsem, fs, fr, fl, rs, rr, rl):
        me = lax.axis_index(axis)
        p = lax.axis_index("prow")
        q = lax.axis_index("pcol")
        barrier = pltpu.get_barrier_semaphore()
        for d in range(1, n):
            pl.semaphore_signal(barrier, 1, device_id={axis: (me + d) % n}, device_id_type=MESH)
        _grid_barrier_signals(barrier, g, p, q)
        pl.semaphore_wait(barrier, n - 1 + g * g - 1)
        root_wait = _permute_start(r_ref, ro_ref, True, rs, rr, rl)
        forest_wait = _permute_start(f_ref, fo_ref, False, fs, fr, fl)
        copies = []
        for d in range(1, n):
            peer = (me + d) % n
            copy = pltpu.make_async_remote_copy(
                x_ref.at[peer], recv.at[d - 1], ssem.at[d - 1], rsem.at[d - 1],
                device_id={axis: peer}, device_id_type=MESH)
            copy.start()
            copies.append(copy)
        for copy in copies:
            copy.wait()
        total = x_ref[me]
        for d in range(n - 1):
            total = total + recv[d]
        part[...] = total
        o_ref[me] = total
        copies = []
        for d in range(1, n):
            peer = (me + d) % n
            copy = pltpu.make_async_remote_copy(
                part, o_ref.at[me], gsem.at[d - 1], hsem.at[d - 1],
                device_id={axis: peer}, device_id_type=MESH)
            copy.start()
            copies.append(copy)
        for copy in copies:
            copy.wait()
        root_wait()
        forest_wait()

    return pl.pallas_call(
        kernel,
        out_shape=(
            jax.ShapeDtypeStruct(chunks.shape, chunks.dtype),
            jax.ShapeDtypeStruct(forest.shape, forest.dtype),
            jax.ShapeDtypeStruct(root_in.shape, root_in.dtype),
        ),
        in_specs=[VMEM_SPEC] * 3,
        out_specs=(VMEM_SPEC,) * 3,
        scratch_shapes=[
            pltpu.VMEM((n - 1,) + chunks.shape[1:], chunks.dtype),
            pltpu.VMEM(chunks.shape[1:], chunks.dtype),
            pltpu.SemaphoreType.DMA((n - 1,)),
            pltpu.SemaphoreType.DMA((n - 1,)),
            pltpu.SemaphoreType.DMA((n - 1,)),
            pltpu.SemaphoreType.DMA((n - 1,)),
        ] + _permute_scratch(g) + _permute_scratch(g),
        compiler_params=_params(cid),
    )(chunks, forest, root_in)


def solve_all(local_forest, local_root, factors, pattern, inverses, root_inverse, n_layer, cid):
    levels, g, slice_rows, cols = local_forest.shape
    rows = g * slice_rows
    f32, bf16 = jnp.float32, jnp.bfloat16
    row_blocks = rows // 8
    col_parts = n_layer // row_blocks
    chunk_cols = cols // col_parts

    def chunk(ref, c):
        r0 = pl.multiple_of((c // col_parts) * 8, 8)
        c0 = pl.multiple_of((c % col_parts) * chunk_cols, chunk_cols)
        return ref.at[pl.ds(r0, 8), pl.ds(c0, chunk_cols)]

    def kernel(f_ref, r_ref, w_hbm, pat_ref, inv_hbm, rinv_hbm, fo_ref, ro_ref,
               placed, placed_root, sol, root_sol, gath, tot, sb, rrecv, rootrecv,
               share_buf, recv_layer, part, full, w_ref, inv_ref, rinv_ref, load_sems,
               gs, gr, rs_s, rs_r, ls, lr, hs, hr, *perm_sems):
        p = lax.axis_index("prow")
        q = lax.axis_index("pcol")
        me = lax.axis_index("layer")
        perm = [perm_sems[3 * i:3 * i + 3] for i in range(levels + 3)]
        loads = [pltpu.make_async_copy(src, dst, load_sems.at[i]) for i, (src, dst) in
                 enumerate(((inv_hbm, inv_ref), (w_hbm, w_ref), (rinv_hbm, rinv_ref)))]
        for load in loads:
            load.start()
        barrier = pltpu.get_barrier_semaphore()
        _grid_barrier_signals(barrier, g, p, q)
        for d in range(1, n_layer):
            pl.semaphore_signal(barrier, 1, device_id={"layer": (me + d) % n_layer},
                                device_id_type=MESH)
        pl.semaphore_wait(barrier, g * g - 1 + n_layer - 1)
        forest_in = _permute_start(f_ref, placed, True, *perm[0])
        root_in = _permute_start(r_ref, placed_root, True, *perm[1])
        tot[...] = jnp.zeros(tot.shape, f32)
        forest_in()
        pending = []
        outs = []
        loads[0].wait()
        for t in range(levels):
            rhs = placed[t].reshape(rows, cols).astype(f32)
            if t > 0:
                for copy in pending:
                    copy.wait()
                red = tot[t - 1, q]
                for d in range(g - 1):
                    red = red + rrecv[t - 1, d].astype(f32)
                rhs = rhs - red
            ans = jnp.dot(inv_ref[t], rhs, precision=lax.Precision.HIGHEST,
                          preferred_element_type=f32).astype(bf16)
            sol[t] = ans.reshape(g, slice_rows, cols)
            gath[t, p] = ans
            copies = []
            for d in range(1, g):
                copy = pltpu.make_async_remote_copy(
                    gath.at[t, p], gath.at[t, p], gs.at[t, d - 1], gr.at[t, d - 1],
                    device_id={"prow": (p + d) % g}, device_id_type=MESH)
                copy.start()
                copies.append(copy)
            outs.append(_permute_start(sol.at[pl.ds(t, 1)], fo_ref.at[pl.ds(t, 1)], False,
                                       *perm[3 + t]))
            for copy in copies:
                copy.wait()
            if t == 0:
                loads[1].wait()
            for target in range(t + 1, levels + 1):
                pair = pair_slot(t, target)

                def body(j, carry, t=t, target=target, pair=pair):
                    acc = tot[target - 1, j]
                    for z in range(g):
                        present = pat_ref[pair, j, z].astype(f32).astype(bf16)
                        acc = acc + jnp.dot(w_ref[pair, j, z] * present, gath[t, z],
                                            preferred_element_type=f32)
                    tot[target - 1, j] = acc
                    return carry

                lax.fori_loop(0, g, body, 0)
            pending = []
            if t + 1 < levels:
                sb[t] = tot[t].astype(bf16)
                src, dst = sb.at[t], rrecv.at[t]
            else:
                src, dst = tot.at[t], rootrecv
            for d in range(1, g):
                peer = (q + d) % g
                copy = pltpu.make_async_remote_copy(
                    src.at[peer], dst.at[d - 1], rs_s.at[t, d - 1], rs_r.at[t, d - 1],
                    device_id={"pcol": peer}, device_id_type=MESH)
                copy.start()
                pending.append(copy)
        for copy in pending:
            copy.wait()
        share = tot[levels - 1, q]
        for d in range(g - 1):
            share = share + rootrecv[d]
        share_buf[...] = share
        copies = []
        for d in range(1, n_layer):
            peer = (me + d) % n_layer
            copy = pltpu.make_async_remote_copy(
                chunk(share_buf, peer), recv_layer.at[d - 1], ls.at[d - 1], lr.at[d - 1],
                device_id={"layer": peer}, device_id_type=MESH)
            copy.start()
            copies.append(copy)
        for copy in copies:
            copy.wait()
        r0 = pl.multiple_of((me // col_parts) * 8, 8)
        c0 = pl.multiple_of((me % col_parts) * chunk_cols, chunk_cols)
        total = share_buf[pl.ds(r0, 8), pl.ds(c0, chunk_cols)]
        for d in range(n_layer - 1):
            total = total + recv_layer[d]
        part[...] = total
        full[pl.ds(r0, 8), pl.ds(c0, chunk_cols)] = total
        copies = []
        for d in range(1, n_layer):
            peer = (me + d) % n_layer
            copy = pltpu.make_async_remote_copy(
                part, chunk(full, me), hs.at[d - 1], hr.at[d - 1],
                device_id={"layer": peer}, device_id_type=MESH)
            copy.start()
            copies.append(copy)
        for copy in copies:
            copy.wait()
        root_in()
        loads[2].wait()
        side = placed_root[0].reshape(rows, cols).astype(f32) - full[...]
        answer = jnp.dot(rinv_ref[...], side, precision=lax.Precision.HIGHEST,
                         preferred_element_type=f32).astype(bf16)
        root_sol[0] = answer.reshape(g, slice_rows, cols)
        root_out = _permute_start(root_sol, ro_ref, False, *perm[2])
        for wait in outs:
            wait()
        root_out()

    return pl.pallas_call(
        kernel,
        out_shape=(
            jax.ShapeDtypeStruct(local_forest.shape, bf16),
            jax.ShapeDtypeStruct(local_root.shape, bf16),
        ),
        in_specs=[ANY_SPEC, ANY_SPEC, ANY_SPEC,
                  pl.BlockSpec(memory_space=pltpu.SMEM), ANY_SPEC, ANY_SPEC],
        out_specs=(VMEM_SPEC,) * 2,
        scratch_shapes=[
            pltpu.VMEM(local_forest.shape, bf16),
            pltpu.VMEM(local_root.shape, bf16),
            pltpu.VMEM(local_forest.shape, bf16),
            pltpu.VMEM(local_root.shape, bf16),
            pltpu.VMEM((levels, g, rows, cols), bf16),
            pltpu.VMEM((levels, g, rows, cols), f32),
            pltpu.VMEM((levels - 1, g, rows, cols), bf16),
            pltpu.VMEM((levels - 1, g - 1, rows, cols), bf16),
            pltpu.VMEM((g - 1, rows, cols), f32),
            pltpu.VMEM((rows, cols), f32),
            pltpu.VMEM((n_layer - 1, 8, chunk_cols), f32),
            pltpu.VMEM((8, chunk_cols), f32),
            pltpu.VMEM((rows, cols), f32),
            pltpu.VMEM(factors.shape, factors.dtype),
            pltpu.VMEM(inverses.shape, f32),
            pltpu.VMEM(root_inverse.shape, f32),
            pltpu.SemaphoreType.DMA((3,)),
            pltpu.SemaphoreType.DMA((levels, g - 1)),
            pltpu.SemaphoreType.DMA((levels, g - 1)),
            pltpu.SemaphoreType.DMA((levels, g - 1)),
            pltpu.SemaphoreType.DMA((levels, g - 1)),
            pltpu.SemaphoreType.DMA((n_layer - 1,)),
            pltpu.SemaphoreType.DMA((n_layer - 1,)),
            pltpu.SemaphoreType.DMA((n_layer - 1,)),
            pltpu.SemaphoreType.DMA((n_layer - 1,)),
        ] + _permute_scratch(g) * (levels + 3),
        compiler_params=_params(cid),
    )(local_forest, local_root, factors, pattern, inverses, root_inverse)


def shards(subtree_right_hand, root_rhs, blocks, pattern, forest_inverse, root_inverse):
    grid_size = lax.axis_size("prow")
    n_layer = lax.axis_size("layer")
    super_rows = blocks.shape[-1]
    rhs_cols = subtree_right_hand.shape[-1]
    slice_rows = super_rows // grid_size
    local_forest = subtree_right_hand.reshape(3, grid_size, slice_rows, rhs_cols)
    local_root = root_rhs.reshape(1, grid_size, slice_rows, rhs_cols)
    factors = blocks.reshape(6, grid_size, grid_size, super_rows, super_rows)
    present = pattern.reshape(6, grid_size, grid_size)
    inverses = forest_inverse.reshape(3, super_rows, super_rows)
    forest_back, root_back = solve_all(
        local_forest, local_root, factors, present, inverses,
        root_inverse.reshape(super_rows, super_rows), n_layer, 10)
    forest_out = forest_back.reshape(1, 3 * super_rows, rhs_cols)
    root_out = root_back.reshape(super_rows, rhs_cols)
    return (forest_out, root_out)


def solution(mesh):
    placed = (
        P("layer", ("prow", "pcol"), None),
        P(("prow", "pcol"), None),
        P("layer", None, "prow", "pcol", None, None, None, None),
        P("layer", None, "prow", "pcol", None, None),
        P("layer", None, "prow", "pcol", None, None),
        P("prow", "pcol", None, None),
    )
    return jax.shard_map(
        shards,
        mesh=mesh,
        in_specs=placed,
        out_specs=(P("layer", ("prow", "pcol"), None), P(("prow", "pcol"), None)),
        check_vma=False,
    )
```

```python
import jax
import jax.numpy as jnp
from jax import lax
from jax.experimental import pallas as pl
from jax.experimental.pallas import tpu as pltpu
from jax.sharding import PartitionSpec as P

MESH = pl.DeviceIdType.MESH
VMEM_SPEC = pl.BlockSpec(memory_space=pltpu.VMEM)
ANY_SPEC = pl.BlockSpec(memory_space=pl.ANY)


def pair_slot(source, target):
    return (0, 3, 5)[source] + target - source - 1


def _barrier(axis, n, me):
    barrier = pltpu.get_barrier_semaphore()
    for d in range(1, n):
        pl.semaphore_signal(barrier, 1, device_id={axis: (me + d) % n}, device_id_type=MESH)
    pl.semaphore_wait(barrier, n - 1)


def _params(cid):
    return pltpu.CompilerParams(collective_id=cid, has_side_effects=True)


def reduce_scatter(x, own_part, axis, cid, wire):
    n = x.shape[0]

    def kernel(x_ref, own_ref, o_ref, recv, ssem, rsem):
        me = lax.axis_index(axis)
        _barrier(axis, n, me)
        copies = []
        for d in range(1, n):
            peer = (me + d) % n
            copy = pltpu.make_async_remote_copy(
                x_ref.at[peer], recv.at[d - 1], ssem.at[d - 1], rsem.at[d - 1],
                device_id={axis: peer}, device_id_type=MESH)
            copy.start()
            copies.append(copy)
        for copy in copies:
            copy.wait()
        total = own_ref[...]
        for d in range(n - 1):
            total = total + recv[d].astype(jnp.float32)
        o_ref[...] = total

    return pl.pallas_call(
        kernel,
        out_shape=jax.ShapeDtypeStruct(x.shape[1:], jnp.float32),
        in_specs=[VMEM_SPEC, VMEM_SPEC],
        out_specs=VMEM_SPEC,
        scratch_shapes=[
            pltpu.VMEM((n - 1,) + x.shape[1:], wire),
            pltpu.SemaphoreType.DMA((n - 1,)),
            pltpu.SemaphoreType.DMA((n - 1,)),
        ],
        compiler_params=_params(cid),
    )(x, own_part)


def all_gather(x, axis, n, cid):
    def kernel(x_ref, o_ref, ssem, rsem):
        me = lax.axis_index(axis)
        _barrier(axis, n, me)
        copies = []
        for d in range(1, n):
            peer = (me + d) % n
            copy = pltpu.make_async_remote_copy(
                x_ref, o_ref.at[me], ssem.at[d - 1], rsem.at[d - 1],
                device_id={axis: peer}, device_id_type=MESH)
            copy.start()
            copies.append(copy)
        o_ref[me] = x_ref[...]
        for copy in copies:
            copy.wait()

    return pl.pallas_call(
        kernel,
        out_shape=jax.ShapeDtypeStruct((n,) + x.shape, x.dtype),
        in_specs=[VMEM_SPEC],
        out_specs=VMEM_SPEC,
        scratch_shapes=[
            pltpu.SemaphoreType.DMA((n - 1,)),
            pltpu.SemaphoreType.DMA((n - 1,)),
        ],
        compiler_params=_params(cid),
    )(x)


def all_reduce(x, axis, cid):
    n = x.shape[0]

    def kernel(x_ref, o_ref, recv, part, ssem, rsem, gsem, hsem):
        me = lax.axis_index(axis)
        _barrier(axis, n, me)
        copies = []
        for d in range(1, n):
            peer = (me + d) % n
            copy = pltpu.make_async_remote_copy(
                x_ref.at[peer], recv.at[d - 1], ssem.at[d - 1], rsem.at[d - 1],
                device_id={axis: peer}, device_id_type=MESH)
            copy.start()
            copies.append(copy)
        for copy in copies:
            copy.wait()
        total = x_ref[me]
        for d in range(n - 1):
            total = total + recv[d]
        part[...] = total
        o_ref[me] = total
        copies = []
        for d in range(1, n):
            peer = (me + d) % n
            copy = pltpu.make_async_remote_copy(
                part, o_ref.at[me], gsem.at[d - 1], hsem.at[d - 1],
                device_id={axis: peer}, device_id_type=MESH)
            copy.start()
            copies.append(copy)
        for copy in copies:
            copy.wait()

    return pl.pallas_call(
        kernel,
        out_shape=jax.ShapeDtypeStruct(x.shape, x.dtype),
        in_specs=[VMEM_SPEC],
        out_specs=VMEM_SPEC,
        scratch_shapes=[
            pltpu.VMEM((n - 1,) + x.shape[1:], x.dtype),
            pltpu.VMEM(x.shape[1:], x.dtype),
            pltpu.SemaphoreType.DMA((n - 1,)),
            pltpu.SemaphoreType.DMA((n - 1,)),
            pltpu.SemaphoreType.DMA((n - 1,)),
            pltpu.SemaphoreType.DMA((n - 1,)),
        ],
        compiler_params=_params(cid),
    )(x)


def _grid_barrier_signals(barrier, g, p, q):
    for dp in range(g):
        for dq in range(g):
            if dp or dq:
                pl.semaphore_signal(
                    barrier, 1, device_id={"prow": (p + dp) % g, "pcol": (q + dq) % g},
                    device_id_type=MESH)


def _permute_start(x_ref, o_ref, forward, ssem, rsem, lsem):
    g = x_ref.shape[1]
    p = lax.axis_index("prow")
    q = lax.axis_index("pcol")
    own = p == q
    slot = q if forward else p
    sends = []
    local = pltpu.make_async_copy(x_ref.at[:, p], o_ref.at[:, p], lsem)
    for dj in range(g):
        j = (p + dj) % g
        dest = {"prow": j, "pcol": p} if forward else {"prow": q, "pcol": j}
        copy = pltpu.make_async_remote_copy(
            x_ref.at[:, j], o_ref.at[:, slot], ssem.at[dj], rsem.at[slot],
            device_id=dest, device_id_type=MESH)
        if dj == 0:
            @pl.when(own)
            def _():
                local.start()

            @pl.when(jnp.logical_not(own))
            def _():
                copy.start()
        else:
            copy.start()
        sends.append(copy)

    def wait():
        for dj in range(g):
            s = (p + dj) % g
            arrival = pltpu.make_async_copy(x_ref.at[:, s], o_ref.at[:, s], rsem.at[s])
            if dj == 0:
                @pl.when(own)
                def _():
                    local.wait()

                @pl.when(jnp.logical_not(own))
                def _():
                    sends[0].wait_send()
                    arrival.wait()
            else:
                sends[dj].wait_send()
                arrival.wait()

    return wait


def _permute_scratch(g):
    return [pltpu.SemaphoreType.DMA((g,)), pltpu.SemaphoreType.DMA((g,)), pltpu.SemaphoreType.DMA(())]


def permute_rows(x, forward, cid):
    g = x.shape[1]

    def kernel(x_ref, o_ref, ssem, rsem, lsem):
        p = lax.axis_index("prow")
        q = lax.axis_index("pcol")
        barrier = pltpu.get_barrier_semaphore()
        _grid_barrier_signals(barrier, g, p, q)
        pl.semaphore_wait(barrier, g * g - 1)
        _permute_start(x_ref, o_ref, forward, ssem, rsem, lsem)()

    return pl.pallas_call(
        kernel,
        out_shape=jax.ShapeDtypeStruct(x.shape, x.dtype),
        in_specs=[VMEM_SPEC],
        out_specs=VMEM_SPEC,
        scratch_shapes=_permute_scratch(g),
        compiler_params=_params(cid),
    )(x)


def root_exchange(chunks, forest, root_in, cid):
    n = chunks.shape[0]
    g = forest.shape[1]
    axis = "layer"

    def kernel(x_ref, f_ref, r_ref, o_ref, fo_ref, ro_ref, recv, part,
               ssem, rsem, gsem, hsem, fs, fr, fl, rs, rr, rl):
        me = lax.axis_index(axis)
        p = lax.axis_index("prow")
        q = lax.axis_index("pcol")
        barrier = pltpu.get_barrier_semaphore()
        for d in range(1, n):
            pl.semaphore_signal(barrier, 1, device_id={axis: (me + d) % n}, device_id_type=MESH)
        _grid_barrier_signals(barrier, g, p, q)
        pl.semaphore_wait(barrier, n - 1 + g * g - 1)
        root_wait = _permute_start(r_ref, ro_ref, True, rs, rr, rl)
        forest_wait = _permute_start(f_ref, fo_ref, False, fs, fr, fl)
        copies = []
        for d in range(1, n):
            peer = (me + d) % n
            copy = pltpu.make_async_remote_copy(
                x_ref.at[peer], recv.at[d - 1], ssem.at[d - 1], rsem.at[d - 1],
                device_id={axis: peer}, device_id_type=MESH)
            copy.start()
            copies.append(copy)
        for copy in copies:
            copy.wait()
        total = x_ref[me]
        for d in range(n - 1):
            total = total + recv[d]
        part[...] = total
        o_ref[me] = total
        copies = []
        for d in range(1, n):
            peer = (me + d) % n
            copy = pltpu.make_async_remote_copy(
                part, o_ref.at[me], gsem.at[d - 1], hsem.at[d - 1],
                device_id={axis: peer}, device_id_type=MESH)
            copy.start()
            copies.append(copy)
        for copy in copies:
            copy.wait()
        root_wait()
        forest_wait()

    return pl.pallas_call(
        kernel,
        out_shape=(
            jax.ShapeDtypeStruct(chunks.shape, chunks.dtype),
            jax.ShapeDtypeStruct(forest.shape, forest.dtype),
            jax.ShapeDtypeStruct(root_in.shape, root_in.dtype),
        ),
        in_specs=[VMEM_SPEC] * 3,
        out_specs=(VMEM_SPEC,) * 3,
        scratch_shapes=[
            pltpu.VMEM((n - 1,) + chunks.shape[1:], chunks.dtype),
            pltpu.VMEM(chunks.shape[1:], chunks.dtype),
            pltpu.SemaphoreType.DMA((n - 1,)),
            pltpu.SemaphoreType.DMA((n - 1,)),
            pltpu.SemaphoreType.DMA((n - 1,)),
            pltpu.SemaphoreType.DMA((n - 1,)),
        ] + _permute_scratch(g) + _permute_scratch(g),
        compiler_params=_params(cid),
    )(chunks, forest, root_in)


def solve_all(local_forest, local_root, factors, pattern, inverses, root_inverse, n_layer, cid):
    levels, g, slice_rows, cols = local_forest.shape
    rows = g * slice_rows
    f32, bf16 = jnp.float32, jnp.bfloat16
    def kernel(f_ref, r_ref, w_hbm, pat_ref, inv_hbm, rinv_hbm, fo_ref, ro_ref,
               placed, placed_root, sol, root_sol, gath, tot, sb, rrecv,
               recv_a, sbuf, recv_b, tbuf, recv_1, part, full, w_ref, inv_ref, rinv_ref, load_sems,
               gs, gr, rs_s, rs_r, a_sem, b_send, b_recv, c1_send, c1_recv, hs, hr, *perm_sems):
        p = lax.axis_index("prow")
        q = lax.axis_index("pcol")
        me = lax.axis_index("layer")
        perm = [perm_sems[3 * i:3 * i + 3] for i in range(levels + 3)]
        loads = [pltpu.make_async_copy(src, dst, load_sems.at[i]) for i, (src, dst) in
                 enumerate(((inv_hbm, inv_ref), (w_hbm, w_ref), (rinv_hbm, rinv_ref)))]
        for load in loads:
            load.start()
        barrier = pltpu.get_barrier_semaphore()
        _grid_barrier_signals(barrier, g, p, q)
        for d in range(1, n_layer):
            pl.semaphore_signal(barrier, 1, device_id={"layer": (me + d) % n_layer},
                                device_id_type=MESH)
        pl.semaphore_wait(barrier, g * g - 1 + n_layer - 1)
        forest_in = _permute_start(f_ref, placed, True, *perm[0])
        root_in = _permute_start(r_ref, placed_root, True, *perm[1])
        tot[...] = jnp.zeros(tot.shape, f32)
        forest_in()
        pending = []
        outs = []
        loads[0].wait()
        for t in range(levels):
            rhs = placed[t].reshape(rows, cols).astype(f32)
            if t > 0:
                for copy in pending:
                    copy.wait()
                red = tot[t - 1, q]
                for d in range(g - 1):
                    red = red + rrecv[t - 1, d].astype(f32)
                rhs = rhs - red
            ans = jnp.dot(inv_ref[t], rhs, precision=lax.Precision.HIGHEST,
                          preferred_element_type=f32).astype(bf16)
            sol[t] = ans.reshape(g, slice_rows, cols)
            gath[t, p] = ans
            copies = []
            for d in range(1, g):
                copy = pltpu.make_async_remote_copy(
                    gath.at[t, p], gath.at[t, p], gs.at[t, d - 1], gr.at[t, d - 1],
                    device_id={"prow": (p + d) % g}, device_id_type=MESH)
                copy.start()
                copies.append(copy)
            outs.append(_permute_start(sol.at[pl.ds(t, 1)], fo_ref.at[pl.ds(t, 1)], False,
                                       *perm[3 + t]))
            for copy in copies:
                copy.wait()
            if t == 0:
                loads[1].wait()
            for target in range(t + 1, levels + 1):
                pair = pair_slot(t, target)

                def body(j, carry, t=t, target=target, pair=pair):
                    acc = tot[target - 1, j]
                    for z in range(g):
                        present = pat_ref[pair, j, z].astype(f32).astype(bf16)
                        acc = acc + jnp.dot(w_ref[pair, j, z] * present, gath[t, z],
                                            preferred_element_type=f32)
                    tot[target - 1, j] = acc
                    return carry

                lax.fori_loop(0, g, body, 0)
            if t + 1 < levels:
                pending = []
                sb[t] = tot[t].astype(bf16)
                for d in range(1, g):
                    peer = (q + d) % g
                    copy = pltpu.make_async_remote_copy(
                        sb.at[t, peer], rrecv.at[t, d - 1], rs_s.at[t, d - 1], rs_r.at[t, d - 1],
                        device_id={"pcol": peer}, device_id_type=MESH)
                    copy.start()
                    pending.append(copy)
        core = me % 2
        half = g // 2
        copy = pltpu.make_async_remote_copy(
            tot.at[levels - 1, pl.ds((1 - core) * half, half)], recv_a, a_sem.at[0], a_sem.at[1],
            device_id={"layer": me + 1 - 2 * core}, device_id_type=MESH)
        copy.start()
        copy.wait()
        sbuf[...] = tot[levels - 1, pl.ds(core * half, half)] + recv_a[...]
        holder = q // half == core
        for k in range(half):
            j = core * half + k
            off = (j - q + g) % g
            copy = pltpu.make_async_remote_copy(
                sbuf.at[k], recv_b.at[off], b_send.at[k], b_recv.at[off],
                device_id={"pcol": j}, device_id_type=MESH)

            @pl.when(j != q)
            def _(copy=copy):
                copy.start()
                copy.wait_send()

        n_h = n_layer // 2
        m = me // 2
        c_rows = rows // n_h
        mine = pl.ds(pl.multiple_of(m * c_rows, 8), c_rows)

        @pl.when(holder)
        def _():
            for off in range(1, g):
                pltpu.make_async_copy(sbuf.at[0], recv_b.at[off], b_recv.at[off]).wait()
            t_sum = sbuf[q - core * half]
            for off in range(1, g):
                t_sum = t_sum + recv_b[off]
            tbuf[...] = t_sum
            copies = []
            for dm in range(1, n_h):
                pm = (m + dm) % n_h
                copy = pltpu.make_async_remote_copy(
                    tbuf.at[pl.ds(pl.multiple_of(pm * c_rows, 8), c_rows)], recv_1.at[dm - 1],
                    c1_send.at[dm - 1], c1_recv.at[dm - 1],
                    device_id={"layer": 2 * pm + core}, device_id_type=MESH)
                copy.start()
                copies.append(copy)
            for copy in copies:
                copy.wait()
            total = tbuf[mine]
            for dm in range(n_h - 1):
                total = total + recv_1[dm]
            part[...] = total
            full[mine] = total
            copies = []
            for d in range(1, n_layer):
                copy = pltpu.make_async_remote_copy(
                    part, full.at[mine], hs.at[d - 1], hr.at[m],
                    device_id={"layer": (me + d) % n_layer}, device_id_type=MESH)
                copy.start()
                copies.append(copy)
            for copy in copies:
                copy.wait_send()

        for dm in range(n_h):
            mm = (m + dm) % n_h
            arrival = pltpu.make_async_copy(
                part, full.at[pl.ds(pl.multiple_of(mm * c_rows, 8), c_rows)], hr.at[mm])
            if dm == 0:
                @pl.when(jnp.logical_not(holder))
                def _():
                    arrival.wait()
            else:
                arrival.wait()
        root_in()
        loads[2].wait()
        side = placed_root[0].reshape(rows, cols).astype(f32) - full[...]
        answer = jnp.dot(rinv_ref[...], side, precision=lax.Precision.HIGHEST,
                         preferred_element_type=f32).astype(bf16)
        root_sol[0] = answer.reshape(g, slice_rows, cols)
        root_out = _permute_start(root_sol, ro_ref, False, *perm[2])
        for wait in outs:
            wait()
        root_out()

    return pl.pallas_call(
        kernel,
        out_shape=(
            jax.ShapeDtypeStruct(local_forest.shape, bf16),
            jax.ShapeDtypeStruct(local_root.shape, bf16),
        ),
        in_specs=[ANY_SPEC, ANY_SPEC, ANY_SPEC,
                  pl.BlockSpec(memory_space=pltpu.SMEM), ANY_SPEC, ANY_SPEC],
        out_specs=(VMEM_SPEC,) * 2,
        scratch_shapes=[
            pltpu.VMEM(local_forest.shape, bf16),
            pltpu.VMEM(local_root.shape, bf16),
            pltpu.VMEM(local_forest.shape, bf16),
            pltpu.VMEM(local_root.shape, bf16),
            pltpu.VMEM((levels, g, rows, cols), bf16),
            pltpu.VMEM((levels, g, rows, cols), f32),
            pltpu.VMEM((levels - 1, g, rows, cols), bf16),
            pltpu.VMEM((levels - 1, g - 1, rows, cols), bf16),
            pltpu.VMEM((g // 2, rows, cols), f32),
            pltpu.VMEM((g // 2, rows, cols), f32),
            pltpu.VMEM((g, rows, cols), f32),
            pltpu.VMEM((rows, cols), f32),
            pltpu.VMEM((max(n_layer // 2 - 1, 1), rows // (n_layer // 2), cols), f32),
            pltpu.VMEM((rows // (n_layer // 2), cols), f32),
            pltpu.VMEM((rows, cols), f32),
            pltpu.VMEM(factors.shape, factors.dtype),
            pltpu.VMEM(inverses.shape, f32),
            pltpu.VMEM(root_inverse.shape, f32),
            pltpu.SemaphoreType.DMA((3,)),
            pltpu.SemaphoreType.DMA((levels, g - 1)),
            pltpu.SemaphoreType.DMA((levels, g - 1)),
            pltpu.SemaphoreType.DMA((levels, g - 1)),
            pltpu.SemaphoreType.DMA((levels, g - 1)),
            pltpu.SemaphoreType.DMA((2,)),
            pltpu.SemaphoreType.DMA((g // 2,)),
            pltpu.SemaphoreType.DMA((g,)),
            pltpu.SemaphoreType.DMA((max(n_layer // 2 - 1, 1),)),
            pltpu.SemaphoreType.DMA((max(n_layer // 2 - 1, 1),)),
            pltpu.SemaphoreType.DMA((n_layer - 1,)),
            pltpu.SemaphoreType.DMA((n_layer // 2,)),
        ] + _permute_scratch(g) * (levels + 3),
        compiler_params=_params(cid),
    )(local_forest, local_root, factors, pattern, inverses, root_inverse)


def shards(subtree_right_hand, root_rhs, blocks, pattern, forest_inverse, root_inverse):
    grid_size = lax.axis_size("prow")
    n_layer = lax.axis_size("layer")
    super_rows = blocks.shape[-1]
    rhs_cols = subtree_right_hand.shape[-1]
    slice_rows = super_rows // grid_size
    local_forest = subtree_right_hand.reshape(3, grid_size, slice_rows, rhs_cols)
    local_root = root_rhs.reshape(1, grid_size, slice_rows, rhs_cols)
    factors = blocks.reshape(6, grid_size, grid_size, super_rows, super_rows)
    present = pattern.reshape(6, grid_size, grid_size)
    inverses = forest_inverse.reshape(3, super_rows, super_rows)
    forest_back, root_back = solve_all(
        local_forest, local_root, factors, present, inverses,
        root_inverse.reshape(super_rows, super_rows), n_layer, 10)
    forest_out = forest_back.reshape(1, 3 * super_rows, rhs_cols)
    root_out = root_back.reshape(super_rows, rhs_cols)
    return (forest_out, root_out)


def solution(mesh):
    placed = (
        P("layer", ("prow", "pcol"), None),
        P(("prow", "pcol"), None),
        P("layer", None, "prow", "pcol", None, None, None, None),
        P("layer", None, "prow", "pcol", None, None),
        P("layer", None, "prow", "pcol", None, None),
        P("prow", "pcol", None, None),
    )
    return jax.shard_map(
        shards,
        mesh=mesh,
        in_specs=placed,
        out_specs=(P("layer", ("prow", "pcol"), None), P(("prow", "pcol"), None)),
        check_vma=False,
    )
```

```python
import jax
import jax.numpy as jnp
from jax import lax
from jax.experimental import pallas as pl
from jax.experimental.pallas import tpu as pltpu
from jax.sharding import PartitionSpec as P

MESH = pl.DeviceIdType.MESH
VMEM_SPEC = pl.BlockSpec(memory_space=pltpu.VMEM)
ANY_SPEC = pl.BlockSpec(memory_space=pl.ANY)


def pair_slot(source, target):
    return (0, 3, 5)[source] + target - source - 1


def _barrier(axis, n, me):
    barrier = pltpu.get_barrier_semaphore()
    for d in range(1, n):
        pl.semaphore_signal(barrier, 1, device_id={axis: (me + d) % n}, device_id_type=MESH)
    pl.semaphore_wait(barrier, n - 1)


def _params(cid):
    return pltpu.CompilerParams(collective_id=cid, has_side_effects=True)


def reduce_scatter(x, own_part, axis, cid, wire):
    n = x.shape[0]

    def kernel(x_ref, own_ref, o_ref, recv, ssem, rsem):
        me = lax.axis_index(axis)
        _barrier(axis, n, me)
        copies = []
        for d in range(1, n):
            peer = (me + d) % n
            copy = pltpu.make_async_remote_copy(
                x_ref.at[peer], recv.at[d - 1], ssem.at[d - 1], rsem.at[d - 1],
                device_id={axis: peer}, device_id_type=MESH)
            copy.start()
            copies.append(copy)
        for copy in copies:
            copy.wait()
        total = own_ref[...]
        for d in range(n - 1):
            total = total + recv[d].astype(jnp.float32)
        o_ref[...] = total

    return pl.pallas_call(
        kernel,
        out_shape=jax.ShapeDtypeStruct(x.shape[1:], jnp.float32),
        in_specs=[VMEM_SPEC, VMEM_SPEC],
        out_specs=VMEM_SPEC,
        scratch_shapes=[
            pltpu.VMEM((n - 1,) + x.shape[1:], wire),
            pltpu.SemaphoreType.DMA((n - 1,)),
            pltpu.SemaphoreType.DMA((n - 1,)),
        ],
        compiler_params=_params(cid),
    )(x, own_part)


def all_gather(x, axis, n, cid):
    def kernel(x_ref, o_ref, ssem, rsem):
        me = lax.axis_index(axis)
        _barrier(axis, n, me)
        copies = []
        for d in range(1, n):
            peer = (me + d) % n
            copy = pltpu.make_async_remote_copy(
                x_ref, o_ref.at[me], ssem.at[d - 1], rsem.at[d - 1],
                device_id={axis: peer}, device_id_type=MESH)
            copy.start()
            copies.append(copy)
        o_ref[me] = x_ref[...]
        for copy in copies:
            copy.wait()

    return pl.pallas_call(
        kernel,
        out_shape=jax.ShapeDtypeStruct((n,) + x.shape, x.dtype),
        in_specs=[VMEM_SPEC],
        out_specs=VMEM_SPEC,
        scratch_shapes=[
            pltpu.SemaphoreType.DMA((n - 1,)),
            pltpu.SemaphoreType.DMA((n - 1,)),
        ],
        compiler_params=_params(cid),
    )(x)


def all_reduce(x, axis, cid):
    n = x.shape[0]

    def kernel(x_ref, o_ref, recv, part, ssem, rsem, gsem, hsem):
        me = lax.axis_index(axis)
        _barrier(axis, n, me)
        copies = []
        for d in range(1, n):
            peer = (me + d) % n
            copy = pltpu.make_async_remote_copy(
                x_ref.at[peer], recv.at[d - 1], ssem.at[d - 1], rsem.at[d - 1],
                device_id={axis: peer}, device_id_type=MESH)
            copy.start()
            copies.append(copy)
        for copy in copies:
            copy.wait()
        total = x_ref[me]
        for d in range(n - 1):
            total = total + recv[d]
        part[...] = total
        o_ref[me] = total
        copies = []
        for d in range(1, n):
            peer = (me + d) % n
            copy = pltpu.make_async_remote_copy(
                part, o_ref.at[me], gsem.at[d - 1], hsem.at[d - 1],
                device_id={axis: peer}, device_id_type=MESH)
            copy.start()
            copies.append(copy)
        for copy in copies:
            copy.wait()

    return pl.pallas_call(
        kernel,
        out_shape=jax.ShapeDtypeStruct(x.shape, x.dtype),
        in_specs=[VMEM_SPEC],
        out_specs=VMEM_SPEC,
        scratch_shapes=[
            pltpu.VMEM((n - 1,) + x.shape[1:], x.dtype),
            pltpu.VMEM(x.shape[1:], x.dtype),
            pltpu.SemaphoreType.DMA((n - 1,)),
            pltpu.SemaphoreType.DMA((n - 1,)),
            pltpu.SemaphoreType.DMA((n - 1,)),
            pltpu.SemaphoreType.DMA((n - 1,)),
        ],
        compiler_params=_params(cid),
    )(x)


def _grid_barrier_signals(barrier, g, p, q):
    for dp in range(g):
        for dq in range(g):
            if dp or dq:
                pl.semaphore_signal(
                    barrier, 1, device_id={"prow": (p + dp) % g, "pcol": (q + dq) % g},
                    device_id_type=MESH)


def _permute_start(x_ref, o_ref, forward, ssem, rsem, lsem):
    g = x_ref.shape[1]
    p = lax.axis_index("prow")
    q = lax.axis_index("pcol")
    own = p == q
    slot = q if forward else p
    sends = []
    local = pltpu.make_async_copy(x_ref.at[:, p], o_ref.at[:, p], lsem)
    for dj in range(g):
        j = (p + dj) % g
        dest = {"prow": j, "pcol": p} if forward else {"prow": q, "pcol": j}
        copy = pltpu.make_async_remote_copy(
            x_ref.at[:, j], o_ref.at[:, slot], ssem.at[dj], rsem.at[slot],
            device_id=dest, device_id_type=MESH)
        if dj == 0:
            @pl.when(own)
            def _():
                local.start()

            @pl.when(jnp.logical_not(own))
            def _():
                copy.start()
        else:
            copy.start()
        sends.append(copy)

    def wait():
        for dj in range(g):
            s = (p + dj) % g
            arrival = pltpu.make_async_copy(x_ref.at[:, s], o_ref.at[:, s], rsem.at[s])
            if dj == 0:
                @pl.when(own)
                def _():
                    local.wait()

                @pl.when(jnp.logical_not(own))
                def _():
                    sends[0].wait_send()
                    arrival.wait()
            else:
                sends[dj].wait_send()
                arrival.wait()

    return wait


def _permute_scratch(g):
    return [pltpu.SemaphoreType.DMA((g,)), pltpu.SemaphoreType.DMA((g,)), pltpu.SemaphoreType.DMA(())]


def permute_rows(x, forward, cid):
    g = x.shape[1]

    def kernel(x_ref, o_ref, ssem, rsem, lsem):
        p = lax.axis_index("prow")
        q = lax.axis_index("pcol")
        barrier = pltpu.get_barrier_semaphore()
        _grid_barrier_signals(barrier, g, p, q)
        pl.semaphore_wait(barrier, g * g - 1)
        _permute_start(x_ref, o_ref, forward, ssem, rsem, lsem)()

    return pl.pallas_call(
        kernel,
        out_shape=jax.ShapeDtypeStruct(x.shape, x.dtype),
        in_specs=[VMEM_SPEC],
        out_specs=VMEM_SPEC,
        scratch_shapes=_permute_scratch(g),
        compiler_params=_params(cid),
    )(x)


def root_exchange(chunks, forest, root_in, cid):
    n = chunks.shape[0]
    g = forest.shape[1]
    axis = "layer"

    def kernel(x_ref, f_ref, r_ref, o_ref, fo_ref, ro_ref, recv, part,
               ssem, rsem, gsem, hsem, fs, fr, fl, rs, rr, rl):
        me = lax.axis_index(axis)
        p = lax.axis_index("prow")
        q = lax.axis_index("pcol")
        barrier = pltpu.get_barrier_semaphore()
        for d in range(1, n):
            pl.semaphore_signal(barrier, 1, device_id={axis: (me + d) % n}, device_id_type=MESH)
        _grid_barrier_signals(barrier, g, p, q)
        pl.semaphore_wait(barrier, n - 1 + g * g - 1)
        root_wait = _permute_start(r_ref, ro_ref, True, rs, rr, rl)
        forest_wait = _permute_start(f_ref, fo_ref, False, fs, fr, fl)
        copies = []
        for d in range(1, n):
            peer = (me + d) % n
            copy = pltpu.make_async_remote_copy(
                x_ref.at[peer], recv.at[d - 1], ssem.at[d - 1], rsem.at[d - 1],
                device_id={axis: peer}, device_id_type=MESH)
            copy.start()
            copies.append(copy)
        for copy in copies:
            copy.wait()
        total = x_ref[me]
        for d in range(n - 1):
            total = total + recv[d]
        part[...] = total
        o_ref[me] = total
        copies = []
        for d in range(1, n):
            peer = (me + d) % n
            copy = pltpu.make_async_remote_copy(
                part, o_ref.at[me], gsem.at[d - 1], hsem.at[d - 1],
                device_id={axis: peer}, device_id_type=MESH)
            copy.start()
            copies.append(copy)
        for copy in copies:
            copy.wait()
        root_wait()
        forest_wait()

    return pl.pallas_call(
        kernel,
        out_shape=(
            jax.ShapeDtypeStruct(chunks.shape, chunks.dtype),
            jax.ShapeDtypeStruct(forest.shape, forest.dtype),
            jax.ShapeDtypeStruct(root_in.shape, root_in.dtype),
        ),
        in_specs=[VMEM_SPEC] * 3,
        out_specs=(VMEM_SPEC,) * 3,
        scratch_shapes=[
            pltpu.VMEM((n - 1,) + chunks.shape[1:], chunks.dtype),
            pltpu.VMEM(chunks.shape[1:], chunks.dtype),
            pltpu.SemaphoreType.DMA((n - 1,)),
            pltpu.SemaphoreType.DMA((n - 1,)),
            pltpu.SemaphoreType.DMA((n - 1,)),
            pltpu.SemaphoreType.DMA((n - 1,)),
        ] + _permute_scratch(g) + _permute_scratch(g),
        compiler_params=_params(cid),
    )(chunks, forest, root_in)


def solve_all(local_forest, local_root, factors, pattern, inverses, root_inverse, n_layer, cid):
    levels, g, slice_rows, cols = local_forest.shape
    rows = g * slice_rows
    f32, bf16 = jnp.float32, jnp.bfloat16
    def kernel(f_ref, r_ref, w_hbm, pat_ref, inv_hbm, rinv_hbm, fo_ref, ro_ref,
               placed, placed_root, sol, root_sol, gath, tot, sb, rrecv,
               recv_a, sbuf, recv_b, tbuf, recv_1, part, full, w_ref, inv_ref, rinv_ref, load_sems,
               gs, gr, rs_s, rs_r, a_sem, b_send, b_recv, c1_send, c1_recv, hs, hr, *perm_sems):
        p = lax.axis_index("prow")
        q = lax.axis_index("pcol")
        me = lax.axis_index("layer")
        perm = [perm_sems[3 * i:3 * i + 3] for i in range(levels + 4)]
        loads = [pltpu.make_async_copy(src, dst, load_sems.at[i]) for i, (src, dst) in
                 enumerate(((inv_hbm, inv_ref), (w_hbm, w_ref), (rinv_hbm, rinv_ref)))]
        for load in loads:
            load.start()
        barrier = pltpu.get_barrier_semaphore()
        _grid_barrier_signals(barrier, g, p, q)
        for d in range(1, n_layer):
            pl.semaphore_signal(barrier, 1, device_id={"layer": (me + d) % n_layer},
                                device_id_type=MESH)
        pl.semaphore_wait(barrier, g * g - 1 + n_layer - 1)
        first_in = _permute_start(f_ref.at[pl.ds(0, 1)], placed.at[pl.ds(0, 1)], True, *perm[0])
        rest_in = _permute_start(f_ref.at[pl.ds(1, levels - 1)], placed.at[pl.ds(1, levels - 1)],
                                 True, *perm[levels + 3])
        root_in = _permute_start(r_ref, placed_root, True, *perm[1])
        tot[...] = jnp.zeros(tot.shape, f32)
        first_in()
        pending = []
        outs = []
        loads[0].wait()
        for t in range(levels):
            if t == 1:
                rest_in()
            rhs = placed[t].reshape(rows, cols).astype(f32)
            if t > 0:
                for copy in pending:
                    copy.wait()
                red = tot[t - 1, q]
                for d in range(g - 1):
                    red = red + rrecv[t - 1, d].astype(f32)
                rhs = rhs - red
            ans = jnp.dot(inv_ref[t], rhs, precision=lax.Precision.HIGHEST,
                          preferred_element_type=f32).astype(bf16)
            sol[t] = ans.reshape(g, slice_rows, cols)
            gath[t, p] = ans
            copies = []
            for d in range(1, g):
                copy = pltpu.make_async_remote_copy(
                    gath.at[t, p], gath.at[t, p], gs.at[t, d - 1], gr.at[t, d - 1],
                    device_id={"prow": (p + d) % g}, device_id_type=MESH)
                copy.start()
                copies.append(copy)
            outs.append(_permute_start(sol.at[pl.ds(t, 1)], fo_ref.at[pl.ds(t, 1)], False,
                                       *perm[3 + t]))
            for copy in copies:
                copy.wait()
            if t == 0:
                loads[1].wait()
            for target in range(t + 1, levels + 1):
                pair = pair_slot(t, target)

                def body(j, carry, t=t, target=target, pair=pair):
                    acc = tot[target - 1, j]
                    for z in range(g):
                        present = pat_ref[pair, j, z].astype(f32).astype(bf16)
                        acc = acc + jnp.dot(w_ref[pair, j, z] * present, gath[t, z],
                                            preferred_element_type=f32)
                    tot[target - 1, j] = acc
                    return carry

                lax.fori_loop(0, g, body, 0)
            if t + 1 < levels:
                pending = []
                sb[t] = tot[t].astype(bf16)
                for d in range(1, g):
                    peer = (q + d) % g
                    copy = pltpu.make_async_remote_copy(
                        sb.at[t, peer], rrecv.at[t, d - 1], rs_s.at[t, d - 1], rs_r.at[t, d - 1],
                        device_id={"pcol": peer}, device_id_type=MESH)
                    copy.start()
                    pending.append(copy)
        core = me % 2
        half = g // 2
        copy = pltpu.make_async_remote_copy(
            tot.at[levels - 1, pl.ds((1 - core) * half, half)], recv_a, a_sem.at[0], a_sem.at[1],
            device_id={"layer": me + 1 - 2 * core}, device_id_type=MESH)
        copy.start()
        copy.wait()
        sbuf[...] = tot[levels - 1, pl.ds(core * half, half)] + recv_a[...]
        holder = q // half == core
        for k in range(half):
            j = core * half + k
            off = (j - q + g) % g
            copy = pltpu.make_async_remote_copy(
                sbuf.at[k], recv_b.at[off], b_send.at[k], b_recv.at[off],
                device_id={"pcol": j}, device_id_type=MESH)

            @pl.when(j != q)
            def _(copy=copy):
                copy.start()
                copy.wait_send()

        n_h = n_layer // 2
        m = me // 2
        c_rows = rows // n_h
        mine = pl.ds(pl.multiple_of(m * c_rows, 8), c_rows)

        @pl.when(holder)
        def _():
            for off in range(1, g):
                pltpu.make_async_copy(sbuf.at[0], recv_b.at[off], b_recv.at[off]).wait()
            t_sum = sbuf[q - core * half]
            for off in range(1, g):
                t_sum = t_sum + recv_b[off]
            tbuf[...] = t_sum
            copies = []
            for dm in range(1, n_h):
                pm = (m + dm) % n_h
                copy = pltpu.make_async_remote_copy(
                    tbuf.at[pl.ds(pl.multiple_of(pm * c_rows, 8), c_rows)], recv_1.at[dm - 1],
                    c1_send.at[dm - 1], c1_recv.at[dm - 1],
                    device_id={"layer": 2 * pm + core}, device_id_type=MESH)
                copy.start()
                copies.append(copy)
            for copy in copies:
                copy.wait()
            total = tbuf[mine]
            for dm in range(n_h - 1):
                total = total + recv_1[dm]
            part[...] = total
            full[mine] = total
            copies = []
            for d in range(1, n_layer):
                copy = pltpu.make_async_remote_copy(
                    part, full.at[mine], hs.at[d - 1], hr.at[m],
                    device_id={"layer": (me + d) % n_layer}, device_id_type=MESH)
                copy.start()
                copies.append(copy)
            for copy in copies:
                copy.wait_send()

        for dm in range(n_h):
            mm = (m + dm) % n_h
            arrival = pltpu.make_async_copy(
                part, full.at[pl.ds(pl.multiple_of(mm * c_rows, 8), c_rows)], hr.at[mm])
            if dm == 0:
                @pl.when(jnp.logical_not(holder))
                def _():
                    arrival.wait()
            else:
                arrival.wait()
        root_in()
        loads[2].wait()
        side = placed_root[0].reshape(rows, cols).astype(f32) - full[...]
        answer = jnp.dot(rinv_ref[...], side, precision=lax.Precision.HIGHEST,
                         preferred_element_type=f32).astype(bf16)
        root_sol[0] = answer.reshape(g, slice_rows, cols)
        root_out = _permute_start(root_sol, ro_ref, False, *perm[2])
        for wait in outs:
            wait()
        root_out()

    return pl.pallas_call(
        kernel,
        out_shape=(
            jax.ShapeDtypeStruct(local_forest.shape, bf16),
            jax.ShapeDtypeStruct(local_root.shape, bf16),
        ),
        in_specs=[ANY_SPEC, ANY_SPEC, ANY_SPEC,
                  pl.BlockSpec(memory_space=pltpu.SMEM), ANY_SPEC, ANY_SPEC],
        out_specs=(VMEM_SPEC,) * 2,
        scratch_shapes=[
            pltpu.VMEM(local_forest.shape, bf16),
            pltpu.VMEM(local_root.shape, bf16),
            pltpu.VMEM(local_forest.shape, bf16),
            pltpu.VMEM(local_root.shape, bf16),
            pltpu.VMEM((levels, g, rows, cols), bf16),
            pltpu.VMEM((levels, g, rows, cols), f32),
            pltpu.VMEM((levels - 1, g, rows, cols), bf16),
            pltpu.VMEM((levels - 1, g - 1, rows, cols), bf16),
            pltpu.VMEM((g // 2, rows, cols), f32),
            pltpu.VMEM((g // 2, rows, cols), f32),
            pltpu.VMEM((g, rows, cols), f32),
            pltpu.VMEM((rows, cols), f32),
            pltpu.VMEM((max(n_layer // 2 - 1, 1), rows // (n_layer // 2), cols), f32),
            pltpu.VMEM((rows // (n_layer // 2), cols), f32),
            pltpu.VMEM((rows, cols), f32),
            pltpu.VMEM(factors.shape, factors.dtype),
            pltpu.VMEM(inverses.shape, f32),
            pltpu.VMEM(root_inverse.shape, f32),
            pltpu.SemaphoreType.DMA((3,)),
            pltpu.SemaphoreType.DMA((levels, g - 1)),
            pltpu.SemaphoreType.DMA((levels, g - 1)),
            pltpu.SemaphoreType.DMA((levels, g - 1)),
            pltpu.SemaphoreType.DMA((levels, g - 1)),
            pltpu.SemaphoreType.DMA((2,)),
            pltpu.SemaphoreType.DMA((g // 2,)),
            pltpu.SemaphoreType.DMA((g,)),
            pltpu.SemaphoreType.DMA((max(n_layer // 2 - 1, 1),)),
            pltpu.SemaphoreType.DMA((max(n_layer // 2 - 1, 1),)),
            pltpu.SemaphoreType.DMA((n_layer - 1,)),
            pltpu.SemaphoreType.DMA((n_layer // 2,)),
        ] + _permute_scratch(g) * (levels + 4),
        compiler_params=_params(cid),
    )(local_forest, local_root, factors, pattern, inverses, root_inverse)


def shards(subtree_right_hand, root_rhs, blocks, pattern, forest_inverse, root_inverse):
    grid_size = lax.axis_size("prow")
    n_layer = lax.axis_size("layer")
    super_rows = blocks.shape[-1]
    rhs_cols = subtree_right_hand.shape[-1]
    slice_rows = super_rows // grid_size
    local_forest = subtree_right_hand.reshape(3, grid_size, slice_rows, rhs_cols)
    local_root = root_rhs.reshape(1, grid_size, slice_rows, rhs_cols)
    factors = blocks.reshape(6, grid_size, grid_size, super_rows, super_rows)
    present = pattern.reshape(6, grid_size, grid_size)
    inverses = forest_inverse.reshape(3, super_rows, super_rows)
    forest_back, root_back = solve_all(
        local_forest, local_root, factors, present, inverses,
        root_inverse.reshape(super_rows, super_rows), n_layer, 10)
    forest_out = forest_back.reshape(1, 3 * super_rows, rhs_cols)
    root_out = root_back.reshape(super_rows, rhs_cols)
    return (forest_out, root_out)


def solution(mesh):
    placed = (
        P("layer", ("prow", "pcol"), None),
        P(("prow", "pcol"), None),
        P("layer", None, "prow", "pcol", None, None, None, None),
        P("layer", None, "prow", "pcol", None, None),
        P("layer", None, "prow", "pcol", None, None),
        P("prow", "pcol", None, None),
    )
    return jax.shard_map(
        shards,
        mesh=mesh,
        in_specs=placed,
        out_specs=(P("layer", ("prow", "pcol"), None), P(("prow", "pcol"), None)),
        check_vma=False,
    )
```

```python
import jax
import jax.numpy as jnp
from jax import lax
from jax.experimental import pallas as pl
from jax.experimental.pallas import tpu as pltpu
from jax.sharding import PartitionSpec as P

MESH = pl.DeviceIdType.MESH
VMEM_SPEC = pl.BlockSpec(memory_space=pltpu.VMEM)
ANY_SPEC = pl.BlockSpec(memory_space=pl.ANY)


def pair_slot(source, target):
    return (0, 3, 5)[source] + target - source - 1


def _barrier(axis, n, me):
    barrier = pltpu.get_barrier_semaphore()
    for d in range(1, n):
        pl.semaphore_signal(barrier, 1, device_id={axis: (me + d) % n}, device_id_type=MESH)
    pl.semaphore_wait(barrier, n - 1)


def _params(cid):
    return pltpu.CompilerParams(collective_id=cid, has_side_effects=True)


def reduce_scatter(x, own_part, axis, cid, wire):
    n = x.shape[0]

    def kernel(x_ref, own_ref, o_ref, recv, ssem, rsem):
        me = lax.axis_index(axis)
        _barrier(axis, n, me)
        copies = []
        for d in range(1, n):
            peer = (me + d) % n
            copy = pltpu.make_async_remote_copy(
                x_ref.at[peer], recv.at[d - 1], ssem.at[d - 1], rsem.at[d - 1],
                device_id={axis: peer}, device_id_type=MESH)
            copy.start()
            copies.append(copy)
        for copy in copies:
            copy.wait()
        total = own_ref[...]
        for d in range(n - 1):
            total = total + recv[d].astype(jnp.float32)
        o_ref[...] = total

    return pl.pallas_call(
        kernel,
        out_shape=jax.ShapeDtypeStruct(x.shape[1:], jnp.float32),
        in_specs=[VMEM_SPEC, VMEM_SPEC],
        out_specs=VMEM_SPEC,
        scratch_shapes=[
            pltpu.VMEM((n - 1,) + x.shape[1:], wire),
            pltpu.SemaphoreType.DMA((n - 1,)),
            pltpu.SemaphoreType.DMA((n - 1,)),
        ],
        compiler_params=_params(cid),
    )(x, own_part)


def all_gather(x, axis, n, cid):
    def kernel(x_ref, o_ref, ssem, rsem):
        me = lax.axis_index(axis)
        _barrier(axis, n, me)
        copies = []
        for d in range(1, n):
            peer = (me + d) % n
            copy = pltpu.make_async_remote_copy(
                x_ref, o_ref.at[me], ssem.at[d - 1], rsem.at[d - 1],
                device_id={axis: peer}, device_id_type=MESH)
            copy.start()
            copies.append(copy)
        o_ref[me] = x_ref[...]
        for copy in copies:
            copy.wait()

    return pl.pallas_call(
        kernel,
        out_shape=jax.ShapeDtypeStruct((n,) + x.shape, x.dtype),
        in_specs=[VMEM_SPEC],
        out_specs=VMEM_SPEC,
        scratch_shapes=[
            pltpu.SemaphoreType.DMA((n - 1,)),
            pltpu.SemaphoreType.DMA((n - 1,)),
        ],
        compiler_params=_params(cid),
    )(x)


def all_reduce(x, axis, cid):
    n = x.shape[0]

    def kernel(x_ref, o_ref, recv, part, ssem, rsem, gsem, hsem):
        me = lax.axis_index(axis)
        _barrier(axis, n, me)
        copies = []
        for d in range(1, n):
            peer = (me + d) % n
            copy = pltpu.make_async_remote_copy(
                x_ref.at[peer], recv.at[d - 1], ssem.at[d - 1], rsem.at[d - 1],
                device_id={axis: peer}, device_id_type=MESH)
            copy.start()
            copies.append(copy)
        for copy in copies:
            copy.wait()
        total = x_ref[me]
        for d in range(n - 1):
            total = total + recv[d]
        part[...] = total
        o_ref[me] = total
        copies = []
        for d in range(1, n):
            peer = (me + d) % n
            copy = pltpu.make_async_remote_copy(
                part, o_ref.at[me], gsem.at[d - 1], hsem.at[d - 1],
                device_id={axis: peer}, device_id_type=MESH)
            copy.start()
            copies.append(copy)
        for copy in copies:
            copy.wait()

    return pl.pallas_call(
        kernel,
        out_shape=jax.ShapeDtypeStruct(x.shape, x.dtype),
        in_specs=[VMEM_SPEC],
        out_specs=VMEM_SPEC,
        scratch_shapes=[
            pltpu.VMEM((n - 1,) + x.shape[1:], x.dtype),
            pltpu.VMEM(x.shape[1:], x.dtype),
            pltpu.SemaphoreType.DMA((n - 1,)),
            pltpu.SemaphoreType.DMA((n - 1,)),
            pltpu.SemaphoreType.DMA((n - 1,)),
            pltpu.SemaphoreType.DMA((n - 1,)),
        ],
        compiler_params=_params(cid),
    )(x)


def _grid_barrier_signals(barrier, g, p, q):
    for dp in range(g):
        for dq in range(g):
            if dp or dq:
                pl.semaphore_signal(
                    barrier, 1, device_id={"prow": (p + dp) % g, "pcol": (q + dq) % g},
                    device_id_type=MESH)


def _permute_start(x_ref, o_ref, forward, ssem, rsem, lsem):
    g = x_ref.shape[1]
    p = lax.axis_index("prow")
    q = lax.axis_index("pcol")
    own = p == q
    slot = q if forward else p
    sends = []
    local = pltpu.make_async_copy(x_ref.at[:, p], o_ref.at[:, p], lsem)
    for dj in range(g):
        j = (p + dj) % g
        dest = {"prow": j, "pcol": p} if forward else {"prow": q, "pcol": j}
        copy = pltpu.make_async_remote_copy(
            x_ref.at[:, j], o_ref.at[:, slot], ssem.at[dj], rsem.at[slot],
            device_id=dest, device_id_type=MESH)
        if dj == 0:
            @pl.when(own)
            def _():
                local.start()

            @pl.when(jnp.logical_not(own))
            def _():
                copy.start()
        else:
            copy.start()
        sends.append(copy)

    def wait():
        for dj in range(g):
            s = (p + dj) % g
            arrival = pltpu.make_async_copy(x_ref.at[:, s], o_ref.at[:, s], rsem.at[s])
            if dj == 0:
                @pl.when(own)
                def _():
                    local.wait()

                @pl.when(jnp.logical_not(own))
                def _():
                    sends[0].wait_send()
                    arrival.wait()
            else:
                sends[dj].wait_send()
                arrival.wait()

    return wait


def _permute_scratch(g):
    return [pltpu.SemaphoreType.DMA((g,)), pltpu.SemaphoreType.DMA((g,)), pltpu.SemaphoreType.DMA(())]


def permute_rows(x, forward, cid):
    g = x.shape[1]

    def kernel(x_ref, o_ref, ssem, rsem, lsem):
        p = lax.axis_index("prow")
        q = lax.axis_index("pcol")
        barrier = pltpu.get_barrier_semaphore()
        _grid_barrier_signals(barrier, g, p, q)
        pl.semaphore_wait(barrier, g * g - 1)
        _permute_start(x_ref, o_ref, forward, ssem, rsem, lsem)()

    return pl.pallas_call(
        kernel,
        out_shape=jax.ShapeDtypeStruct(x.shape, x.dtype),
        in_specs=[VMEM_SPEC],
        out_specs=VMEM_SPEC,
        scratch_shapes=_permute_scratch(g),
        compiler_params=_params(cid),
    )(x)


def root_exchange(chunks, forest, root_in, cid):
    n = chunks.shape[0]
    g = forest.shape[1]
    axis = "layer"

    def kernel(x_ref, f_ref, r_ref, o_ref, fo_ref, ro_ref, recv, part,
               ssem, rsem, gsem, hsem, fs, fr, fl, rs, rr, rl):
        me = lax.axis_index(axis)
        p = lax.axis_index("prow")
        q = lax.axis_index("pcol")
        barrier = pltpu.get_barrier_semaphore()
        for d in range(1, n):
            pl.semaphore_signal(barrier, 1, device_id={axis: (me + d) % n}, device_id_type=MESH)
        _grid_barrier_signals(barrier, g, p, q)
        pl.semaphore_wait(barrier, n - 1 + g * g - 1)
        root_wait = _permute_start(r_ref, ro_ref, True, rs, rr, rl)
        forest_wait = _permute_start(f_ref, fo_ref, False, fs, fr, fl)
        copies = []
        for d in range(1, n):
            peer = (me + d) % n
            copy = pltpu.make_async_remote_copy(
                x_ref.at[peer], recv.at[d - 1], ssem.at[d - 1], rsem.at[d - 1],
                device_id={axis: peer}, device_id_type=MESH)
            copy.start()
            copies.append(copy)
        for copy in copies:
            copy.wait()
        total = x_ref[me]
        for d in range(n - 1):
            total = total + recv[d]
        part[...] = total
        o_ref[me] = total
        copies = []
        for d in range(1, n):
            peer = (me + d) % n
            copy = pltpu.make_async_remote_copy(
                part, o_ref.at[me], gsem.at[d - 1], hsem.at[d - 1],
                device_id={axis: peer}, device_id_type=MESH)
            copy.start()
            copies.append(copy)
        for copy in copies:
            copy.wait()
        root_wait()
        forest_wait()

    return pl.pallas_call(
        kernel,
        out_shape=(
            jax.ShapeDtypeStruct(chunks.shape, chunks.dtype),
            jax.ShapeDtypeStruct(forest.shape, forest.dtype),
            jax.ShapeDtypeStruct(root_in.shape, root_in.dtype),
        ),
        in_specs=[VMEM_SPEC] * 3,
        out_specs=(VMEM_SPEC,) * 3,
        scratch_shapes=[
            pltpu.VMEM((n - 1,) + chunks.shape[1:], chunks.dtype),
            pltpu.VMEM(chunks.shape[1:], chunks.dtype),
            pltpu.SemaphoreType.DMA((n - 1,)),
            pltpu.SemaphoreType.DMA((n - 1,)),
            pltpu.SemaphoreType.DMA((n - 1,)),
            pltpu.SemaphoreType.DMA((n - 1,)),
        ] + _permute_scratch(g) + _permute_scratch(g),
        compiler_params=_params(cid),
    )(chunks, forest, root_in)


def solve_all(local_forest, local_root, factors, pattern, inverses, root_inverse, n_layer, cid):
    levels, g, slice_rows, cols = local_forest.shape
    rows = g * slice_rows
    f32, bf16 = jnp.float32, jnp.bfloat16
    def kernel(f_ref, r_ref, w_hbm, pat_ref, inv_hbm, rinv_hbm, fo_ref, ro_ref,
               placed, placed_root, sol, root_sol, gath, tot, sb, rrecv,
               recv_a, sbuf, recv_b, tbuf, recv_1, part, full, w_ref, inv_ref, rinv_ref, load_sems,
               gs, gr, rs_s, rs_r, a_sem, b_send, b_recv, c1_send, c1_recv, hs, hr, *perm_sems):
        p = lax.axis_index("prow")
        q = lax.axis_index("pcol")
        me = lax.axis_index("layer")
        perm = [perm_sems[3 * i:3 * i + 3] for i in range(levels + 4)]
        loads = [pltpu.make_async_copy(src, dst, load_sems.at[i]) for i, (src, dst) in
                 enumerate(((inv_hbm, inv_ref), (w_hbm, w_ref), (rinv_hbm, rinv_ref)))]
        for load in loads:
            load.start()
        barrier = pltpu.get_barrier_semaphore()
        _grid_barrier_signals(barrier, g, p, q)
        for d in range(1, n_layer):
            pl.semaphore_signal(barrier, 1, device_id={"layer": (me + d) % n_layer},
                                device_id_type=MESH)
        pl.semaphore_wait(barrier, g * g - 1 + n_layer - 1)
        first_in = _permute_start(f_ref.at[pl.ds(0, 1)], placed.at[pl.ds(0, 1)], True, *perm[0])
        rest_in = _permute_start(f_ref.at[pl.ds(1, levels - 1)], placed.at[pl.ds(1, levels - 1)],
                                 True, *perm[levels + 3])
        tot[...] = jnp.zeros(tot.shape, f32)
        first_in()
        pending = []
        outs = []
        loads[0].wait()
        for t in range(levels):
            if t == 1:
                rest_in()
            rhs = placed[t].reshape(rows, cols).astype(f32)
            if t > 0:
                for copy in pending:
                    copy.wait()
                red = tot[t - 1, q]
                for d in range(g - 1):
                    red = red + rrecv[t - 1, d].astype(f32)
                rhs = rhs - red
            ans = jnp.dot(inv_ref[t], rhs, precision=lax.Precision.HIGHEST,
                          preferred_element_type=f32).astype(bf16)
            sol[t] = ans.reshape(g, slice_rows, cols)
            gath[t, p] = ans
            copies = []
            for d in range(1, g):
                copy = pltpu.make_async_remote_copy(
                    gath.at[t, p], gath.at[t, p], gs.at[t, d - 1], gr.at[t, d - 1],
                    device_id={"prow": (p + d) % g}, device_id_type=MESH)
                copy.start()
                copies.append(copy)
            outs.append(_permute_start(sol.at[pl.ds(t, 1)], fo_ref.at[pl.ds(t, 1)], False,
                                       *perm[3 + t]))
            for copy in copies:
                copy.wait()
            if t == 0:
                loads[1].wait()
            for target in range(t + 1, levels + 1):
                pair = pair_slot(t, target)

                def body(j, carry, t=t, target=target, pair=pair):
                    acc = tot[target - 1, j]
                    for z in range(g):
                        present = pat_ref[pair, j, z].astype(f32).astype(bf16)
                        acc = acc + jnp.dot(w_ref[pair, j, z] * present, gath[t, z],
                                            preferred_element_type=f32)
                    tot[target - 1, j] = acc
                    return carry

                lax.fori_loop(0, g, body, 0)
            if t == 0:
                root_in = _permute_start(r_ref, placed_root, True, *perm[1])
            if t + 1 < levels:
                pending = []
                sb[t] = tot[t].astype(bf16)
                for d in range(1, g):
                    peer = (q + d) % g
                    copy = pltpu.make_async_remote_copy(
                        sb.at[t, peer], rrecv.at[t, d - 1], rs_s.at[t, d - 1], rs_r.at[t, d - 1],
                        device_id={"pcol": peer}, device_id_type=MESH)
                    copy.start()
                    pending.append(copy)
        core = me % 2
        half = g // 2
        copy = pltpu.make_async_remote_copy(
            tot.at[levels - 1, pl.ds((1 - core) * half, half)], recv_a, a_sem.at[0], a_sem.at[1],
            device_id={"layer": me + 1 - 2 * core}, device_id_type=MESH)
        copy.start()
        copy.wait()
        sbuf[...] = tot[levels - 1, pl.ds(core * half, half)] + recv_a[...]
        holder = q // half == core
        for k in range(half):
            j = core * half + k
            off = (j - q + g) % g
            copy = pltpu.make_async_remote_copy(
                sbuf.at[k], recv_b.at[off], b_send.at[k], b_recv.at[off],
                device_id={"pcol": j}, device_id_type=MESH)

            @pl.when(j != q)
            def _(copy=copy):
                copy.start()
                copy.wait_send()

        n_h = n_layer // 2
        m = me // 2
        c_rows = rows // n_h
        mine = pl.ds(pl.multiple_of(m * c_rows, 8), c_rows)

        @pl.when(holder)
        def _():
            for off in range(1, g):
                pltpu.make_async_copy(sbuf.at[0], recv_b.at[off], b_recv.at[off]).wait()
            t_sum = sbuf[q - core * half]
            for off in range(1, g):
                t_sum = t_sum + recv_b[off]
            tbuf[...] = t_sum
            copies = []
            for dm in range(1, n_h):
                pm = (m + dm) % n_h
                copy = pltpu.make_async_remote_copy(
                    tbuf.at[pl.ds(pl.multiple_of(pm * c_rows, 8), c_rows)], recv_1.at[dm - 1],
                    c1_send.at[dm - 1], c1_recv.at[dm - 1],
                    device_id={"layer": 2 * pm + core}, device_id_type=MESH)
                copy.start()
                copies.append(copy)
            for copy in copies:
                copy.wait()
            total = tbuf[mine]
            for dm in range(n_h - 1):
                total = total + recv_1[dm]
            part[...] = total
            full[mine] = total
            copies = []
            for d in range(1, n_layer):
                copy = pltpu.make_async_remote_copy(
                    part, full.at[mine], hs.at[d - 1], hr.at[m],
                    device_id={"layer": (me + d) % n_layer}, device_id_type=MESH)
                copy.start()
                copies.append(copy)
            for copy in copies:
                copy.wait_send()

        for dm in range(n_h):
            mm = (m + dm) % n_h
            arrival = pltpu.make_async_copy(
                part, full.at[pl.ds(pl.multiple_of(mm * c_rows, 8), c_rows)], hr.at[mm])
            if dm == 0:
                @pl.when(jnp.logical_not(holder))
                def _():
                    arrival.wait()
            else:
                arrival.wait()
        root_in()
        loads[2].wait()
        side = placed_root[0].reshape(rows, cols).astype(f32) - full[...]
        answer = jnp.dot(rinv_ref[...], side, precision=lax.Precision.HIGHEST,
                         preferred_element_type=f32).astype(bf16)
        root_sol[0] = answer.reshape(g, slice_rows, cols)
        root_out = _permute_start(root_sol, ro_ref, False, *perm[2])
        for wait in outs:
            wait()
        root_out()

    return pl.pallas_call(
        kernel,
        out_shape=(
            jax.ShapeDtypeStruct(local_forest.shape, bf16),
            jax.ShapeDtypeStruct(local_root.shape, bf16),
        ),
        in_specs=[ANY_SPEC, ANY_SPEC, ANY_SPEC,
                  pl.BlockSpec(memory_space=pltpu.SMEM), ANY_SPEC, ANY_SPEC],
        out_specs=(VMEM_SPEC,) * 2,
        scratch_shapes=[
            pltpu.VMEM(local_forest.shape, bf16),
            pltpu.VMEM(local_root.shape, bf16),
            pltpu.VMEM(local_forest.shape, bf16),
            pltpu.VMEM(local_root.shape, bf16),
            pltpu.VMEM((levels, g, rows, cols), bf16),
            pltpu.VMEM((levels, g, rows, cols), f32),
            pltpu.VMEM((levels - 1, g, rows, cols), bf16),
            pltpu.VMEM((levels - 1, g - 1, rows, cols), bf16),
            pltpu.VMEM((g // 2, rows, cols), f32),
            pltpu.VMEM((g // 2, rows, cols), f32),
            pltpu.VMEM((g, rows, cols), f32),
            pltpu.VMEM((rows, cols), f32),
            pltpu.VMEM((max(n_layer // 2 - 1, 1), rows // (n_layer // 2), cols), f32),
            pltpu.VMEM((rows // (n_layer // 2), cols), f32),
            pltpu.VMEM((rows, cols), f32),
            pltpu.VMEM(factors.shape, factors.dtype),
            pltpu.VMEM(inverses.shape, f32),
            pltpu.VMEM(root_inverse.shape, f32),
            pltpu.SemaphoreType.DMA((3,)),
            pltpu.SemaphoreType.DMA((levels, g - 1)),
            pltpu.SemaphoreType.DMA((levels, g - 1)),
            pltpu.SemaphoreType.DMA((levels, g - 1)),
            pltpu.SemaphoreType.DMA((levels, g - 1)),
            pltpu.SemaphoreType.DMA((2,)),
            pltpu.SemaphoreType.DMA((g // 2,)),
            pltpu.SemaphoreType.DMA((g,)),
            pltpu.SemaphoreType.DMA((max(n_layer // 2 - 1, 1),)),
            pltpu.SemaphoreType.DMA((max(n_layer // 2 - 1, 1),)),
            pltpu.SemaphoreType.DMA((n_layer - 1,)),
            pltpu.SemaphoreType.DMA((n_layer // 2,)),
        ] + _permute_scratch(g) * (levels + 4),
        compiler_params=_params(cid),
    )(local_forest, local_root, factors, pattern, inverses, root_inverse)


def shards(subtree_right_hand, root_rhs, blocks, pattern, forest_inverse, root_inverse):
    grid_size = lax.axis_size("prow")
    n_layer = lax.axis_size("layer")
    super_rows = blocks.shape[-1]
    rhs_cols = subtree_right_hand.shape[-1]
    slice_rows = super_rows // grid_size
    local_forest = subtree_right_hand.reshape(3, grid_size, slice_rows, rhs_cols)
    local_root = root_rhs.reshape(1, grid_size, slice_rows, rhs_cols)
    factors = blocks.reshape(6, grid_size, grid_size, super_rows, super_rows)
    present = pattern.reshape(6, grid_size, grid_size)
    inverses = forest_inverse.reshape(3, super_rows, super_rows)
    forest_back, root_back = solve_all(
        local_forest, local_root, factors, present, inverses,
        root_inverse.reshape(super_rows, super_rows), n_layer, 10)
    forest_out = forest_back.reshape(1, 3 * super_rows, rhs_cols)
    root_out = root_back.reshape(super_rows, rhs_cols)
    return (forest_out, root_out)


def solution(mesh):
    placed = (
        P("layer", ("prow", "pcol"), None),
        P(("prow", "pcol"), None),
        P("layer", None, "prow", "pcol", None, None, None, None),
        P("layer", None, "prow", "pcol", None, None),
        P("layer", None, "prow", "pcol", None, None),
        P("prow", "pcol", None, None),
    )
    return jax.shard_map(
        shards,
        mesh=mesh,
        in_specs=placed,
        out_specs=(P("layer", ("prow", "pcol"), None), P(("prow", "pcol"), None)),
        check_vma=False,
    )
```

```python
import jax
import jax.numpy as jnp
from jax import lax
from jax.experimental import pallas as pl
from jax.experimental.pallas import tpu as pltpu
from jax.sharding import PartitionSpec as P

MESH = pl.DeviceIdType.MESH
VMEM_SPEC = pl.BlockSpec(memory_space=pltpu.VMEM)
ANY_SPEC = pl.BlockSpec(memory_space=pl.ANY)


def pair_slot(source, target):
    return (0, 3, 5)[source] + target - source - 1


def _barrier(axis, n, me):
    barrier = pltpu.get_barrier_semaphore()
    for d in range(1, n):
        pl.semaphore_signal(barrier, 1, device_id={axis: (me + d) % n}, device_id_type=MESH)
    pl.semaphore_wait(barrier, n - 1)


def _params(cid):
    return pltpu.CompilerParams(collective_id=cid, has_side_effects=True)


def reduce_scatter(x, own_part, axis, cid, wire):
    n = x.shape[0]

    def kernel(x_ref, own_ref, o_ref, recv, ssem, rsem):
        me = lax.axis_index(axis)
        _barrier(axis, n, me)
        copies = []
        for d in range(1, n):
            peer = (me + d) % n
            copy = pltpu.make_async_remote_copy(
                x_ref.at[peer], recv.at[d - 1], ssem.at[d - 1], rsem.at[d - 1],
                device_id={axis: peer}, device_id_type=MESH)
            copy.start()
            copies.append(copy)
        for copy in copies:
            copy.wait()
        total = own_ref[...]
        for d in range(n - 1):
            total = total + recv[d].astype(jnp.float32)
        o_ref[...] = total

    return pl.pallas_call(
        kernel,
        out_shape=jax.ShapeDtypeStruct(x.shape[1:], jnp.float32),
        in_specs=[VMEM_SPEC, VMEM_SPEC],
        out_specs=VMEM_SPEC,
        scratch_shapes=[
            pltpu.VMEM((n - 1,) + x.shape[1:], wire),
            pltpu.SemaphoreType.DMA((n - 1,)),
            pltpu.SemaphoreType.DMA((n - 1,)),
        ],
        compiler_params=_params(cid),
    )(x, own_part)


def all_gather(x, axis, n, cid):
    def kernel(x_ref, o_ref, ssem, rsem):
        me = lax.axis_index(axis)
        _barrier(axis, n, me)
        copies = []
        for d in range(1, n):
            peer = (me + d) % n
            copy = pltpu.make_async_remote_copy(
                x_ref, o_ref.at[me], ssem.at[d - 1], rsem.at[d - 1],
                device_id={axis: peer}, device_id_type=MESH)
            copy.start()
            copies.append(copy)
        o_ref[me] = x_ref[...]
        for copy in copies:
            copy.wait()

    return pl.pallas_call(
        kernel,
        out_shape=jax.ShapeDtypeStruct((n,) + x.shape, x.dtype),
        in_specs=[VMEM_SPEC],
        out_specs=VMEM_SPEC,
        scratch_shapes=[
            pltpu.SemaphoreType.DMA((n - 1,)),
            pltpu.SemaphoreType.DMA((n - 1,)),
        ],
        compiler_params=_params(cid),
    )(x)


def all_reduce(x, axis, cid):
    n = x.shape[0]

    def kernel(x_ref, o_ref, recv, part, ssem, rsem, gsem, hsem):
        me = lax.axis_index(axis)
        _barrier(axis, n, me)
        copies = []
        for d in range(1, n):
            peer = (me + d) % n
            copy = pltpu.make_async_remote_copy(
                x_ref.at[peer], recv.at[d - 1], ssem.at[d - 1], rsem.at[d - 1],
                device_id={axis: peer}, device_id_type=MESH)
            copy.start()
            copies.append(copy)
        for copy in copies:
            copy.wait()
        total = x_ref[me]
        for d in range(n - 1):
            total = total + recv[d]
        part[...] = total
        o_ref[me] = total
        copies = []
        for d in range(1, n):
            peer = (me + d) % n
            copy = pltpu.make_async_remote_copy(
                part, o_ref.at[me], gsem.at[d - 1], hsem.at[d - 1],
                device_id={axis: peer}, device_id_type=MESH)
            copy.start()
            copies.append(copy)
        for copy in copies:
            copy.wait()

    return pl.pallas_call(
        kernel,
        out_shape=jax.ShapeDtypeStruct(x.shape, x.dtype),
        in_specs=[VMEM_SPEC],
        out_specs=VMEM_SPEC,
        scratch_shapes=[
            pltpu.VMEM((n - 1,) + x.shape[1:], x.dtype),
            pltpu.VMEM(x.shape[1:], x.dtype),
            pltpu.SemaphoreType.DMA((n - 1,)),
            pltpu.SemaphoreType.DMA((n - 1,)),
            pltpu.SemaphoreType.DMA((n - 1,)),
            pltpu.SemaphoreType.DMA((n - 1,)),
        ],
        compiler_params=_params(cid),
    )(x)


def _grid_barrier_signals(barrier, g, p, q):
    for dp in range(g):
        for dq in range(g):
            if dp or dq:
                pl.semaphore_signal(
                    barrier, 1, device_id={"prow": (p + dp) % g, "pcol": (q + dq) % g},
                    device_id_type=MESH)


def _permute_start(x_ref, o_ref, forward, ssem, rsem, lsem):
    g = x_ref.shape[1]
    p = lax.axis_index("prow")
    q = lax.axis_index("pcol")
    own = p == q
    slot = q if forward else p
    sends = []
    local = pltpu.make_async_copy(x_ref.at[:, p], o_ref.at[:, p], lsem)
    for dj in range(g):
        j = (p + dj) % g
        dest = {"prow": j, "pcol": p} if forward else {"prow": q, "pcol": j}
        copy = pltpu.make_async_remote_copy(
            x_ref.at[:, j], o_ref.at[:, slot], ssem.at[dj], rsem.at[slot],
            device_id=dest, device_id_type=MESH)
        if dj == 0:
            @pl.when(own)
            def _():
                local.start()

            @pl.when(jnp.logical_not(own))
            def _():
                copy.start()
        else:
            copy.start()
        sends.append(copy)

    def wait():
        for dj in range(g):
            s = (p + dj) % g
            arrival = pltpu.make_async_copy(x_ref.at[:, s], o_ref.at[:, s], rsem.at[s])
            if dj == 0:
                @pl.when(own)
                def _():
                    local.wait()

                @pl.when(jnp.logical_not(own))
                def _():
                    sends[0].wait_send()
                    arrival.wait()
            else:
                sends[dj].wait_send()
                arrival.wait()

    return wait


def _permute_scratch(g):
    return [pltpu.SemaphoreType.DMA((g,)), pltpu.SemaphoreType.DMA((g,)), pltpu.SemaphoreType.DMA(())]


def permute_rows(x, forward, cid):
    g = x.shape[1]

    def kernel(x_ref, o_ref, ssem, rsem, lsem):
        p = lax.axis_index("prow")
        q = lax.axis_index("pcol")
        barrier = pltpu.get_barrier_semaphore()
        _grid_barrier_signals(barrier, g, p, q)
        pl.semaphore_wait(barrier, g * g - 1)
        _permute_start(x_ref, o_ref, forward, ssem, rsem, lsem)()

    return pl.pallas_call(
        kernel,
        out_shape=jax.ShapeDtypeStruct(x.shape, x.dtype),
        in_specs=[VMEM_SPEC],
        out_specs=VMEM_SPEC,
        scratch_shapes=_permute_scratch(g),
        compiler_params=_params(cid),
    )(x)


def root_exchange(chunks, forest, root_in, cid):
    n = chunks.shape[0]
    g = forest.shape[1]
    axis = "layer"

    def kernel(x_ref, f_ref, r_ref, o_ref, fo_ref, ro_ref, recv, part,
               ssem, rsem, gsem, hsem, fs, fr, fl, rs, rr, rl):
        me = lax.axis_index(axis)
        p = lax.axis_index("prow")
        q = lax.axis_index("pcol")
        barrier = pltpu.get_barrier_semaphore()
        for d in range(1, n):
            pl.semaphore_signal(barrier, 1, device_id={axis: (me + d) % n}, device_id_type=MESH)
        _grid_barrier_signals(barrier, g, p, q)
        pl.semaphore_wait(barrier, n - 1 + g * g - 1)
        root_wait = _permute_start(r_ref, ro_ref, True, rs, rr, rl)
        forest_wait = _permute_start(f_ref, fo_ref, False, fs, fr, fl)
        copies = []
        for d in range(1, n):
            peer = (me + d) % n
            copy = pltpu.make_async_remote_copy(
                x_ref.at[peer], recv.at[d - 1], ssem.at[d - 1], rsem.at[d - 1],
                device_id={axis: peer}, device_id_type=MESH)
            copy.start()
            copies.append(copy)
        for copy in copies:
            copy.wait()
        total = x_ref[me]
        for d in range(n - 1):
            total = total + recv[d]
        part[...] = total
        o_ref[me] = total
        copies = []
        for d in range(1, n):
            peer = (me + d) % n
            copy = pltpu.make_async_remote_copy(
                part, o_ref.at[me], gsem.at[d - 1], hsem.at[d - 1],
                device_id={axis: peer}, device_id_type=MESH)
            copy.start()
            copies.append(copy)
        for copy in copies:
            copy.wait()
        root_wait()
        forest_wait()

    return pl.pallas_call(
        kernel,
        out_shape=(
            jax.ShapeDtypeStruct(chunks.shape, chunks.dtype),
            jax.ShapeDtypeStruct(forest.shape, forest.dtype),
            jax.ShapeDtypeStruct(root_in.shape, root_in.dtype),
        ),
        in_specs=[VMEM_SPEC] * 3,
        out_specs=(VMEM_SPEC,) * 3,
        scratch_shapes=[
            pltpu.VMEM((n - 1,) + chunks.shape[1:], chunks.dtype),
            pltpu.VMEM(chunks.shape[1:], chunks.dtype),
            pltpu.SemaphoreType.DMA((n - 1,)),
            pltpu.SemaphoreType.DMA((n - 1,)),
            pltpu.SemaphoreType.DMA((n - 1,)),
            pltpu.SemaphoreType.DMA((n - 1,)),
        ] + _permute_scratch(g) + _permute_scratch(g),
        compiler_params=_params(cid),
    )(chunks, forest, root_in)


def solve_all(local_forest, local_root, factors, pattern, inverses, root_inverse, n_layer, cid):
    levels, g, slice_rows, cols = local_forest.shape
    rows = g * slice_rows
    f32, bf16 = jnp.float32, jnp.bfloat16
    def kernel(f_ref, r_ref, w_hbm, pat_ref, inv_hbm, rinv_hbm, fo_ref, ro_ref,
               placed, placed_root, sol, root_sol, gath, tot, sb, rrecv,
               recv_a, sbuf, recv_b, tbuf, recv_1, part, full, w_ref, inv_ref, rinv_ref, load_sems,
               gs, gr, rs_s, rs_r, a_sem, b_send, b_recv, c1_send, c1_recv, hs, hr, *perm_sems):
        p = lax.axis_index("prow")
        q = lax.axis_index("pcol")
        me = lax.axis_index("layer")
        perm = [perm_sems[3 * i:3 * i + 3] for i in range(levels + 4)]
        loads = [pltpu.make_async_copy(src, dst, load_sems.at[i]) for i, (src, dst) in
                 enumerate(((inv_hbm, inv_ref), (w_hbm, w_ref), (rinv_hbm, rinv_ref)))]
        for load in loads:
            load.start()
        barrier = pltpu.get_barrier_semaphore()
        _grid_barrier_signals(barrier, g, p, q)
        for d in range(1, n_layer):
            pl.semaphore_signal(barrier, 1, device_id={"layer": (me + d) % n_layer},
                                device_id_type=MESH)
        pl.semaphore_wait(barrier, g * g - 1 + n_layer - 1)
        first_in = _permute_start(f_ref.at[pl.ds(0, 1)], placed.at[pl.ds(0, 1)], True, *perm[0])
        rest_in = _permute_start(f_ref.at[pl.ds(1, levels - 1)], placed.at[pl.ds(1, levels - 1)],
                                 True, *perm[levels + 3])
        tot[...] = jnp.zeros(tot.shape, f32)
        first_in()
        pending = []
        outs = []
        loads[0].wait()
        for t in range(levels):
            if t == 1:
                rest_in()
            rhs = placed[t].reshape(rows, cols).astype(f32)
            if t > 0:
                for copy in pending:
                    copy.wait()
                red = tot[t - 1, q]
                for d in range(g - 1):
                    red = red + rrecv[t - 1, d].astype(f32)
                rhs = rhs - red
            ans = jnp.dot(inv_ref[t], rhs, precision=lax.Precision.HIGHEST,
                          preferred_element_type=f32).astype(bf16)
            sol[t] = ans.reshape(g, slice_rows, cols)
            gath[t, p] = ans
            copies = []
            for d in range(1, g):
                copy = pltpu.make_async_remote_copy(
                    gath.at[t, p], gath.at[t, p], gs.at[t, d - 1], gr.at[t, d - 1],
                    device_id={"prow": (p + d) % g}, device_id_type=MESH)
                copy.start()
                copies.append(copy)
            for copy in copies:
                copy.wait()
            if t == 0:
                loads[1].wait()
            for target in range(t + 1, levels + 1):
                pair = pair_slot(t, target)

                def body(j, carry, t=t, target=target, pair=pair):
                    acc = tot[target - 1, j]
                    for z in range(g):
                        present = pat_ref[pair, j, z].astype(f32).astype(bf16)
                        acc = acc + jnp.dot(w_ref[pair, j, z] * present, gath[t, z],
                                            preferred_element_type=f32)
                    tot[target - 1, j] = acc
                    return carry

                lax.fori_loop(0, g, body, 0)
            if t == 0:
                root_in = _permute_start(r_ref, placed_root, True, *perm[1])
            if t + 1 < levels:
                pending = []
                sb[t] = tot[t].astype(bf16)
                for d in range(1, g):
                    peer = (q + d) % g
                    copy = pltpu.make_async_remote_copy(
                        sb.at[t, peer], rrecv.at[t, d - 1], rs_s.at[t, d - 1], rs_r.at[t, d - 1],
                        device_id={"pcol": peer}, device_id_type=MESH)
                    copy.start()
                    pending.append(copy)
        core = me % 2
        half = g // 2
        copy = pltpu.make_async_remote_copy(
            tot.at[levels - 1, pl.ds((1 - core) * half, half)], recv_a, a_sem.at[0], a_sem.at[1],
            device_id={"layer": me + 1 - 2 * core}, device_id_type=MESH)
        copy.start()
        for t in range(levels):
            outs.append(_permute_start(sol.at[pl.ds(t, 1)], fo_ref.at[pl.ds(t, 1)], False,
                                       *perm[3 + t]))
        copy.wait()
        sbuf[...] = tot[levels - 1, pl.ds(core * half, half)] + recv_a[...]
        holder = q // half == core
        for k in range(half):
            j = core * half + k
            off = (j - q + g) % g
            copy = pltpu.make_async_remote_copy(
                sbuf.at[k], recv_b.at[off], b_send.at[k], b_recv.at[off],
                device_id={"pcol": j}, device_id_type=MESH)

            @pl.when(j != q)
            def _(copy=copy):
                copy.start()
                copy.wait_send()

        n_h = n_layer // 2
        m = me // 2
        c_rows = rows // n_h
        mine = pl.ds(pl.multiple_of(m * c_rows, 8), c_rows)

        @pl.when(holder)
        def _():
            for off in range(1, g):
                pltpu.make_async_copy(sbuf.at[0], recv_b.at[off], b_recv.at[off]).wait()
            t_sum = sbuf[q - core * half]
            for off in range(1, g):
                t_sum = t_sum + recv_b[off]
            tbuf[...] = t_sum
            copies = []
            for dm in range(1, n_h):
                pm = (m + dm) % n_h
                copy = pltpu.make_async_remote_copy(
                    tbuf.at[pl.ds(pl.multiple_of(pm * c_rows, 8), c_rows)], recv_1.at[dm - 1],
                    c1_send.at[dm - 1], c1_recv.at[dm - 1],
                    device_id={"layer": 2 * pm + core}, device_id_type=MESH)
                copy.start()
                copies.append(copy)
            for copy in copies:
                copy.wait()
            total = tbuf[mine]
            for dm in range(n_h - 1):
                total = total + recv_1[dm]
            part[...] = total
            full[mine] = total
            copies = []
            for d in range(1, n_layer):
                copy = pltpu.make_async_remote_copy(
                    part, full.at[mine], hs.at[d - 1], hr.at[m],
                    device_id={"layer": (me + d) % n_layer}, device_id_type=MESH)
                copy.start()
                copies.append(copy)
            for copy in copies:
                copy.wait_send()

        for dm in range(n_h):
            mm = (m + dm) % n_h
            arrival = pltpu.make_async_copy(
                part, full.at[pl.ds(pl.multiple_of(mm * c_rows, 8), c_rows)], hr.at[mm])
            if dm == 0:
                @pl.when(jnp.logical_not(holder))
                def _():
                    arrival.wait()
            else:
                arrival.wait()
        root_in()
        loads[2].wait()
        side = placed_root[0].reshape(rows, cols).astype(f32) - full[...]
        answer = jnp.dot(rinv_ref[...], side, precision=lax.Precision.HIGHEST,
                         preferred_element_type=f32).astype(bf16)
        root_sol[0] = answer.reshape(g, slice_rows, cols)
        root_out = _permute_start(root_sol, ro_ref, False, *perm[2])
        for wait in outs:
            wait()
        root_out()

    return pl.pallas_call(
        kernel,
        out_shape=(
            jax.ShapeDtypeStruct(local_forest.shape, bf16),
            jax.ShapeDtypeStruct(local_root.shape, bf16),
        ),
        in_specs=[ANY_SPEC, ANY_SPEC, ANY_SPEC,
                  pl.BlockSpec(memory_space=pltpu.SMEM), ANY_SPEC, ANY_SPEC],
        out_specs=(VMEM_SPEC,) * 2,
        scratch_shapes=[
            pltpu.VMEM(local_forest.shape, bf16),
            pltpu.VMEM(local_root.shape, bf16),
            pltpu.VMEM(local_forest.shape, bf16),
            pltpu.VMEM(local_root.shape, bf16),
            pltpu.VMEM((levels, g, rows, cols), bf16),
            pltpu.VMEM((levels, g, rows, cols), f32),
            pltpu.VMEM((levels - 1, g, rows, cols), bf16),
            pltpu.VMEM((levels - 1, g - 1, rows, cols), bf16),
            pltpu.VMEM((g // 2, rows, cols), f32),
            pltpu.VMEM((g // 2, rows, cols), f32),
            pltpu.VMEM((g, rows, cols), f32),
            pltpu.VMEM((rows, cols), f32),
            pltpu.VMEM((max(n_layer // 2 - 1, 1), rows // (n_layer // 2), cols), f32),
            pltpu.VMEM((rows // (n_layer // 2), cols), f32),
            pltpu.VMEM((rows, cols), f32),
            pltpu.VMEM(factors.shape, factors.dtype),
            pltpu.VMEM(inverses.shape, f32),
            pltpu.VMEM(root_inverse.shape, f32),
            pltpu.SemaphoreType.DMA((3,)),
            pltpu.SemaphoreType.DMA((levels, g - 1)),
            pltpu.SemaphoreType.DMA((levels, g - 1)),
            pltpu.SemaphoreType.DMA((levels, g - 1)),
            pltpu.SemaphoreType.DMA((levels, g - 1)),
            pltpu.SemaphoreType.DMA((2,)),
            pltpu.SemaphoreType.DMA((g // 2,)),
            pltpu.SemaphoreType.DMA((g,)),
            pltpu.SemaphoreType.DMA((max(n_layer // 2 - 1, 1),)),
            pltpu.SemaphoreType.DMA((max(n_layer // 2 - 1, 1),)),
            pltpu.SemaphoreType.DMA((n_layer - 1,)),
            pltpu.SemaphoreType.DMA((n_layer // 2,)),
        ] + _permute_scratch(g) * (levels + 4),
        compiler_params=_params(cid),
    )(local_forest, local_root, factors, pattern, inverses, root_inverse)


def shards(subtree_right_hand, root_rhs, blocks, pattern, forest_inverse, root_inverse):
    grid_size = lax.axis_size("prow")
    n_layer = lax.axis_size("layer")
    super_rows = blocks.shape[-1]
    rhs_cols = subtree_right_hand.shape[-1]
    slice_rows = super_rows // grid_size
    local_forest = subtree_right_hand.reshape(3, grid_size, slice_rows, rhs_cols)
    local_root = root_rhs.reshape(1, grid_size, slice_rows, rhs_cols)
    factors = blocks.reshape(6, grid_size, grid_size, super_rows, super_rows)
    present = pattern.reshape(6, grid_size, grid_size)
    inverses = forest_inverse.reshape(3, super_rows, super_rows)
    forest_back, root_back = solve_all(
        local_forest, local_root, factors, present, inverses,
        root_inverse.reshape(super_rows, super_rows), n_layer, 10)
    forest_out = forest_back.reshape(1, 3 * super_rows, rhs_cols)
    root_out = root_back.reshape(super_rows, rhs_cols)
    return (forest_out, root_out)


def solution(mesh):
    placed = (
        P("layer", ("prow", "pcol"), None),
        P(("prow", "pcol"), None),
        P("layer", None, "prow", "pcol", None, None, None, None),
        P("layer", None, "prow", "pcol", None, None),
        P("layer", None, "prow", "pcol", None, None),
        P("prow", "pcol", None, None),
    )
    return jax.shard_map(
        shards,
        mesh=mesh,
        in_specs=placed,
        out_specs=(P("layer", ("prow", "pcol"), None), P(("prow", "pcol"), None)),
        check_vma=False,
    )
```

```python
import jax
import jax.numpy as jnp
from jax import lax
from jax.experimental import pallas as pl
from jax.experimental.pallas import tpu as pltpu
from jax.sharding import PartitionSpec as P

MESH = pl.DeviceIdType.MESH
VMEM_SPEC = pl.BlockSpec(memory_space=pltpu.VMEM)
ANY_SPEC = pl.BlockSpec(memory_space=pl.ANY)


def pair_slot(source, target):
    return (0, 3, 5)[source] + target - source - 1


def _barrier(axis, n, me):
    barrier = pltpu.get_barrier_semaphore()
    for d in range(1, n):
        pl.semaphore_signal(barrier, 1, device_id={axis: (me + d) % n}, device_id_type=MESH)
    pl.semaphore_wait(barrier, n - 1)


def _params(cid):
    return pltpu.CompilerParams(collective_id=cid, has_side_effects=True)


def reduce_scatter(x, own_part, axis, cid, wire):
    n = x.shape[0]

    def kernel(x_ref, own_ref, o_ref, recv, ssem, rsem):
        me = lax.axis_index(axis)
        _barrier(axis, n, me)
        copies = []
        for d in range(1, n):
            peer = (me + d) % n
            copy = pltpu.make_async_remote_copy(
                x_ref.at[peer], recv.at[d - 1], ssem.at[d - 1], rsem.at[d - 1],
                device_id={axis: peer}, device_id_type=MESH)
            copy.start()
            copies.append(copy)
        for copy in copies:
            copy.wait()
        total = own_ref[...]
        for d in range(n - 1):
            total = total + recv[d].astype(jnp.float32)
        o_ref[...] = total

    return pl.pallas_call(
        kernel,
        out_shape=jax.ShapeDtypeStruct(x.shape[1:], jnp.float32),
        in_specs=[VMEM_SPEC, VMEM_SPEC],
        out_specs=VMEM_SPEC,
        scratch_shapes=[
            pltpu.VMEM((n - 1,) + x.shape[1:], wire),
            pltpu.SemaphoreType.DMA((n - 1,)),
            pltpu.SemaphoreType.DMA((n - 1,)),
        ],
        compiler_params=_params(cid),
    )(x, own_part)


def all_gather(x, axis, n, cid):
    def kernel(x_ref, o_ref, ssem, rsem):
        me = lax.axis_index(axis)
        _barrier(axis, n, me)
        copies = []
        for d in range(1, n):
            peer = (me + d) % n
            copy = pltpu.make_async_remote_copy(
                x_ref, o_ref.at[me], ssem.at[d - 1], rsem.at[d - 1],
                device_id={axis: peer}, device_id_type=MESH)
            copy.start()
            copies.append(copy)
        o_ref[me] = x_ref[...]
        for copy in copies:
            copy.wait()

    return pl.pallas_call(
        kernel,
        out_shape=jax.ShapeDtypeStruct((n,) + x.shape, x.dtype),
        in_specs=[VMEM_SPEC],
        out_specs=VMEM_SPEC,
        scratch_shapes=[
            pltpu.SemaphoreType.DMA((n - 1,)),
            pltpu.SemaphoreType.DMA((n - 1,)),
        ],
        compiler_params=_params(cid),
    )(x)


def all_reduce(x, axis, cid):
    n = x.shape[0]

    def kernel(x_ref, o_ref, recv, part, ssem, rsem, gsem, hsem):
        me = lax.axis_index(axis)
        _barrier(axis, n, me)
        copies = []
        for d in range(1, n):
            peer = (me + d) % n
            copy = pltpu.make_async_remote_copy(
                x_ref.at[peer], recv.at[d - 1], ssem.at[d - 1], rsem.at[d - 1],
                device_id={axis: peer}, device_id_type=MESH)
            copy.start()
            copies.append(copy)
        for copy in copies:
            copy.wait()
        total = x_ref[me]
        for d in range(n - 1):
            total = total + recv[d]
        part[...] = total
        o_ref[me] = total
        copies = []
        for d in range(1, n):
            peer = (me + d) % n
            copy = pltpu.make_async_remote_copy(
                part, o_ref.at[me], gsem.at[d - 1], hsem.at[d - 1],
                device_id={axis: peer}, device_id_type=MESH)
            copy.start()
            copies.append(copy)
        for copy in copies:
            copy.wait()

    return pl.pallas_call(
        kernel,
        out_shape=jax.ShapeDtypeStruct(x.shape, x.dtype),
        in_specs=[VMEM_SPEC],
        out_specs=VMEM_SPEC,
        scratch_shapes=[
            pltpu.VMEM((n - 1,) + x.shape[1:], x.dtype),
            pltpu.VMEM(x.shape[1:], x.dtype),
            pltpu.SemaphoreType.DMA((n - 1,)),
            pltpu.SemaphoreType.DMA((n - 1,)),
            pltpu.SemaphoreType.DMA((n - 1,)),
            pltpu.SemaphoreType.DMA((n - 1,)),
        ],
        compiler_params=_params(cid),
    )(x)


def _grid_barrier_signals(barrier, g, p, q):
    for dp in range(g):
        for dq in range(g):
            if dp or dq:
                pl.semaphore_signal(
                    barrier, 1, device_id={"prow": (p + dp) % g, "pcol": (q + dq) % g},
                    device_id_type=MESH)


def _permute_start(x_ref, o_ref, forward, ssem, rsem, lsem):
    g = x_ref.shape[1]
    p = lax.axis_index("prow")
    q = lax.axis_index("pcol")
    own = p == q
    slot = q if forward else p
    sends = []
    local = pltpu.make_async_copy(x_ref.at[:, p], o_ref.at[:, p], lsem)
    for dj in range(g):
        j = (p + dj) % g
        dest = {"prow": j, "pcol": p} if forward else {"prow": q, "pcol": j}
        copy = pltpu.make_async_remote_copy(
            x_ref.at[:, j], o_ref.at[:, slot], ssem.at[dj], rsem.at[slot],
            device_id=dest, device_id_type=MESH)
        if dj == 0:
            @pl.when(own)
            def _():
                local.start()

            @pl.when(jnp.logical_not(own))
            def _():
                copy.start()
        else:
            copy.start()
        sends.append(copy)

    def wait():
        for dj in range(g):
            s = (p + dj) % g
            arrival = pltpu.make_async_copy(x_ref.at[:, s], o_ref.at[:, s], rsem.at[s])
            if dj == 0:
                @pl.when(own)
                def _():
                    local.wait()

                @pl.when(jnp.logical_not(own))
                def _():
                    sends[0].wait_send()
                    arrival.wait()
            else:
                sends[dj].wait_send()
                arrival.wait()

    return wait


def _permute_scratch(g):
    return [pltpu.SemaphoreType.DMA((g,)), pltpu.SemaphoreType.DMA((g,)), pltpu.SemaphoreType.DMA(())]


def permute_rows(x, forward, cid):
    g = x.shape[1]

    def kernel(x_ref, o_ref, ssem, rsem, lsem):
        p = lax.axis_index("prow")
        q = lax.axis_index("pcol")
        barrier = pltpu.get_barrier_semaphore()
        _grid_barrier_signals(barrier, g, p, q)
        pl.semaphore_wait(barrier, g * g - 1)
        _permute_start(x_ref, o_ref, forward, ssem, rsem, lsem)()

    return pl.pallas_call(
        kernel,
        out_shape=jax.ShapeDtypeStruct(x.shape, x.dtype),
        in_specs=[VMEM_SPEC],
        out_specs=VMEM_SPEC,
        scratch_shapes=_permute_scratch(g),
        compiler_params=_params(cid),
    )(x)


def root_exchange(chunks, forest, root_in, cid):
    n = chunks.shape[0]
    g = forest.shape[1]
    axis = "layer"

    def kernel(x_ref, f_ref, r_ref, o_ref, fo_ref, ro_ref, recv, part,
               ssem, rsem, gsem, hsem, fs, fr, fl, rs, rr, rl):
        me = lax.axis_index(axis)
        p = lax.axis_index("prow")
        q = lax.axis_index("pcol")
        barrier = pltpu.get_barrier_semaphore()
        for d in range(1, n):
            pl.semaphore_signal(barrier, 1, device_id={axis: (me + d) % n}, device_id_type=MESH)
        _grid_barrier_signals(barrier, g, p, q)
        pl.semaphore_wait(barrier, n - 1 + g * g - 1)
        root_wait = _permute_start(r_ref, ro_ref, True, rs, rr, rl)
        forest_wait = _permute_start(f_ref, fo_ref, False, fs, fr, fl)
        copies = []
        for d in range(1, n):
            peer = (me + d) % n
            copy = pltpu.make_async_remote_copy(
                x_ref.at[peer], recv.at[d - 1], ssem.at[d - 1], rsem.at[d - 1],
                device_id={axis: peer}, device_id_type=MESH)
            copy.start()
            copies.append(copy)
        for copy in copies:
            copy.wait()
        total = x_ref[me]
        for d in range(n - 1):
            total = total + recv[d]
        part[...] = total
        o_ref[me] = total
        copies = []
        for d in range(1, n):
            peer = (me + d) % n
            copy = pltpu.make_async_remote_copy(
                part, o_ref.at[me], gsem.at[d - 1], hsem.at[d - 1],
                device_id={axis: peer}, device_id_type=MESH)
            copy.start()
            copies.append(copy)
        for copy in copies:
            copy.wait()
        root_wait()
        forest_wait()

    return pl.pallas_call(
        kernel,
        out_shape=(
            jax.ShapeDtypeStruct(chunks.shape, chunks.dtype),
            jax.ShapeDtypeStruct(forest.shape, forest.dtype),
            jax.ShapeDtypeStruct(root_in.shape, root_in.dtype),
        ),
        in_specs=[VMEM_SPEC] * 3,
        out_specs=(VMEM_SPEC,) * 3,
        scratch_shapes=[
            pltpu.VMEM((n - 1,) + chunks.shape[1:], chunks.dtype),
            pltpu.VMEM(chunks.shape[1:], chunks.dtype),
            pltpu.SemaphoreType.DMA((n - 1,)),
            pltpu.SemaphoreType.DMA((n - 1,)),
            pltpu.SemaphoreType.DMA((n - 1,)),
            pltpu.SemaphoreType.DMA((n - 1,)),
        ] + _permute_scratch(g) + _permute_scratch(g),
        compiler_params=_params(cid),
    )(chunks, forest, root_in)


def solve_all(local_forest, local_root, factors, pattern, inverses, root_inverse, n_layer, cid):
    levels, g, slice_rows, cols = local_forest.shape
    rows = g * slice_rows
    f32, bf16 = jnp.float32, jnp.bfloat16
    def kernel(f_ref, r_ref, w_hbm, pat_ref, inv_hbm, rinv_hbm, fo_ref, ro_ref,
               placed, placed_root, sol, root_sol, gath, tot, sb, rrecv,
               recv_a, sbuf, recv_b, tbuf, recv_1, part, full, w_ref, inv_ref, rinv_ref, load_sems,
               gs, gr, rs_s, rs_r, a_sem, b_send, b_recv, c1_send, c1_recv, hs, hr, *perm_sems):
        p = lax.axis_index("prow")
        q = lax.axis_index("pcol")
        me = lax.axis_index("layer")
        perm = [perm_sems[3 * i:3 * i + 3] for i in range(levels + 4)]
        loads = [pltpu.make_async_copy(src, dst, load_sems.at[i]) for i, (src, dst) in
                 enumerate(((inv_hbm, inv_ref), (w_hbm, w_ref), (rinv_hbm, rinv_ref)))]
        for load in loads:
            load.start()
        barrier = pltpu.get_barrier_semaphore()
        _grid_barrier_signals(barrier, g, p, q)
        for d in range(1, n_layer):
            pl.semaphore_signal(barrier, 1, device_id={"layer": (me + d) % n_layer},
                                device_id_type=MESH)
        pl.semaphore_wait(barrier, g * g - 1 + n_layer - 1)
        first_in = _permute_start(f_ref.at[pl.ds(0, 1)], placed.at[pl.ds(0, 1)], True, *perm[0])
        rest_in = _permute_start(f_ref.at[pl.ds(1, levels - 1)], placed.at[pl.ds(1, levels - 1)],
                                 True, *perm[levels + 3])
        tot[...] = jnp.zeros(tot.shape, f32)
        first_in()
        pending = []
        outs = []
        loads[0].wait()
        for t in range(levels):
            if t == 1:
                rest_in()
            rhs = placed[t].reshape(rows, cols).astype(f32)
            if t > 0:
                for copy in pending:
                    copy.wait()
                red = tot[t - 1, q]
                for d in range(g - 1):
                    red = red + rrecv[t - 1, d].astype(f32)
                rhs = rhs - red
            ans = jnp.dot(inv_ref[t], rhs, precision=lax.Precision.HIGHEST,
                          preferred_element_type=f32).astype(bf16)
            sol[t] = ans.reshape(g, slice_rows, cols)
            gath[t, p] = ans
            copies = []
            for d in range(1, g):
                copy = pltpu.make_async_remote_copy(
                    gath.at[t, p], gath.at[t, p], gs.at[t, d - 1], gr.at[t, d - 1],
                    device_id={"prow": (p + d) % g}, device_id_type=MESH)
                copy.start()
                copies.append(copy)
            outs.append(_permute_start(sol.at[pl.ds(t, 1)], fo_ref.at[pl.ds(t, 1)], False,
                                       *perm[3 + t]))
            for copy in copies:
                copy.wait()
            if t == 0:
                loads[1].wait()
            for target in range(t + 1, levels + 1):
                pair = pair_slot(t, target)

                def body(j, carry, t=t, target=target, pair=pair):
                    acc = tot[target - 1, j]
                    for z in range(g):
                        present = pat_ref[pair, j, z].astype(f32).astype(bf16)
                        acc = acc + jnp.dot(w_ref[pair, j, z] * present, gath[t, z],
                                            preferred_element_type=f32)
                    tot[target - 1, j] = acc
                    return carry

                lax.fori_loop(0, g, body, 0)
            if t == 0:
                root_in = _permute_start(r_ref, placed_root, True, *perm[1])
            if t + 1 < levels:
                pending = []
                sb[t] = tot[t].astype(bf16)
                for d in range(1, g):
                    peer = (q + d) % g
                    copy = pltpu.make_async_remote_copy(
                        sb.at[t, peer], rrecv.at[t, d - 1], rs_s.at[t, d - 1], rs_r.at[t, d - 1],
                        device_id={"pcol": peer}, device_id_type=MESH)
                    copy.start()
                    pending.append(copy)
        core = me % 2
        half = g // 2
        copy = pltpu.make_async_remote_copy(
            tot.at[levels - 1, pl.ds((1 - core) * half, half)], recv_a, a_sem.at[0], a_sem.at[1],
            device_id={"layer": me + 1 - 2 * core}, device_id_type=MESH)
        copy.start()
        copy.wait()
        sbuf[...] = tot[levels - 1, pl.ds(core * half, half)] + recv_a[...]
        holder = q // half == core
        for k in range(half):
            j = core * half + k
            off = (j - q + g) % g
            copy = pltpu.make_async_remote_copy(
                sbuf.at[k], recv_b.at[off], b_send.at[k], b_recv.at[off],
                device_id={"pcol": j}, device_id_type=MESH)

            @pl.when(j != q)
            def _(copy=copy):
                copy.start()
                copy.wait_send()

        n_h = n_layer // 2
        m = me // 2
        c_rows = rows // n_h
        mine = pl.ds(pl.multiple_of(m * c_rows, 8), c_rows)

        @pl.when(holder)
        def _():
            for off in range(1, g):
                pltpu.make_async_copy(sbuf.at[0], recv_b.at[off], b_recv.at[off]).wait()
            t_sum = sbuf[q - core * half]
            for off in range(1, g):
                t_sum = t_sum + recv_b[off]
            tbuf[...] = t_sum
            copies = []
            for dm in range(1, n_h):
                pm = (m + dm) % n_h
                copy = pltpu.make_async_remote_copy(
                    tbuf.at[pl.ds(pl.multiple_of(pm * c_rows, 8), c_rows)], recv_1.at[dm - 1],
                    c1_send.at[dm - 1], c1_recv.at[dm - 1],
                    device_id={"layer": 2 * pm + core}, device_id_type=MESH)
                copy.start()
                copies.append(copy)
            for copy in copies:
                copy.wait()
            total = tbuf[mine]
            for dm in range(n_h - 1):
                total = total + recv_1[dm]
            part[...] = total
            full[mine] = total
            copies = []
            for dm in range(1, n_h):
                pm = (m + dm) % n_h
                copy = pltpu.make_async_remote_copy(
                    part, full.at[mine], hs.at[dm - 1], hr.at[m],
                    device_id={"layer": 2 * pm + core}, device_id_type=MESH)
                copy.start()
                copies.append(copy)
            for copy in copies:
                copy.wait_send()
            for dm in range(1, n_h):
                mm = (m + dm) % n_h
                pltpu.make_async_copy(
                    part, full.at[pl.ds(pl.multiple_of(mm * c_rows, 8), c_rows)], hr.at[mm]).wait()
            copy = pltpu.make_async_remote_copy(
                full, full, hs.at[n_layer - 2], hr.at[n_h],
                device_id={"layer": me + 1 - 2 * core}, device_id_type=MESH)
            copy.start()
            copy.wait_send()

        @pl.when(jnp.logical_not(holder))
        def _():
            pltpu.make_async_copy(full, full, hr.at[n_h]).wait()
        root_in()
        loads[2].wait()
        side = placed_root[0].reshape(rows, cols).astype(f32) - full[...]
        answer = jnp.dot(rinv_ref[...], side, precision=lax.Precision.HIGHEST,
                         preferred_element_type=f32).astype(bf16)
        root_sol[0] = answer.reshape(g, slice_rows, cols)
        root_out = _permute_start(root_sol, ro_ref, False, *perm[2])
        for wait in outs:
            wait()
        root_out()

    return pl.pallas_call(
        kernel,
        out_shape=(
            jax.ShapeDtypeStruct(local_forest.shape, bf16),
            jax.ShapeDtypeStruct(local_root.shape, bf16),
        ),
        in_specs=[ANY_SPEC, ANY_SPEC, ANY_SPEC,
                  pl.BlockSpec(memory_space=pltpu.SMEM), ANY_SPEC, ANY_SPEC],
        out_specs=(VMEM_SPEC,) * 2,
        scratch_shapes=[
            pltpu.VMEM(local_forest.shape, bf16),
            pltpu.VMEM(local_root.shape, bf16),
            pltpu.VMEM(local_forest.shape, bf16),
            pltpu.VMEM(local_root.shape, bf16),
            pltpu.VMEM((levels, g, rows, cols), bf16),
            pltpu.VMEM((levels, g, rows, cols), f32),
            pltpu.VMEM((levels - 1, g, rows, cols), bf16),
            pltpu.VMEM((levels - 1, g - 1, rows, cols), bf16),
            pltpu.VMEM((g // 2, rows, cols), f32),
            pltpu.VMEM((g // 2, rows, cols), f32),
            pltpu.VMEM((g, rows, cols), f32),
            pltpu.VMEM((rows, cols), f32),
            pltpu.VMEM((max(n_layer // 2 - 1, 1), rows // (n_layer // 2), cols), f32),
            pltpu.VMEM((rows // (n_layer // 2), cols), f32),
            pltpu.VMEM((rows, cols), f32),
            pltpu.VMEM(factors.shape, factors.dtype),
            pltpu.VMEM(inverses.shape, f32),
            pltpu.VMEM(root_inverse.shape, f32),
            pltpu.SemaphoreType.DMA((3,)),
            pltpu.SemaphoreType.DMA((levels, g - 1)),
            pltpu.SemaphoreType.DMA((levels, g - 1)),
            pltpu.SemaphoreType.DMA((levels, g - 1)),
            pltpu.SemaphoreType.DMA((levels, g - 1)),
            pltpu.SemaphoreType.DMA((2,)),
            pltpu.SemaphoreType.DMA((g // 2,)),
            pltpu.SemaphoreType.DMA((g,)),
            pltpu.SemaphoreType.DMA((max(n_layer // 2 - 1, 1),)),
            pltpu.SemaphoreType.DMA((max(n_layer // 2 - 1, 1),)),
            pltpu.SemaphoreType.DMA((n_layer - 1,)),
            pltpu.SemaphoreType.DMA((n_layer // 2 + 1,)),
        ] + _permute_scratch(g) * (levels + 4),
        compiler_params=_params(cid),
    )(local_forest, local_root, factors, pattern, inverses, root_inverse)


def shards(subtree_right_hand, root_rhs, blocks, pattern, forest_inverse, root_inverse):
    grid_size = lax.axis_size("prow")
    n_layer = lax.axis_size("layer")
    super_rows = blocks.shape[-1]
    rhs_cols = subtree_right_hand.shape[-1]
    slice_rows = super_rows // grid_size
    local_forest = subtree_right_hand.reshape(3, grid_size, slice_rows, rhs_cols)
    local_root = root_rhs.reshape(1, grid_size, slice_rows, rhs_cols)
    factors = blocks.reshape(6, grid_size, grid_size, super_rows, super_rows)
    present = pattern.reshape(6, grid_size, grid_size)
    inverses = forest_inverse.reshape(3, super_rows, super_rows)
    forest_back, root_back = solve_all(
        local_forest, local_root, factors, present, inverses,
        root_inverse.reshape(super_rows, super_rows), n_layer, 10)
    forest_out = forest_back.reshape(1, 3 * super_rows, rhs_cols)
    root_out = root_back.reshape(super_rows, rhs_cols)
    return (forest_out, root_out)


def solution(mesh):
    placed = (
        P("layer", ("prow", "pcol"), None),
        P(("prow", "pcol"), None),
        P("layer", None, "prow", "pcol", None, None, None, None),
        P("layer", None, "prow", "pcol", None, None),
        P("layer", None, "prow", "pcol", None, None),
        P("prow", "pcol", None, None),
    )
    return jax.shard_map(
        shards,
        mesh=mesh,
        in_specs=placed,
        out_specs=(P("layer", ("prow", "pcol"), None), P(("prow", "pcol"), None)),
        check_vma=False,
    )
```

```python
import jax
import jax.numpy as jnp
from jax import lax
from jax.experimental import pallas as pl
from jax.experimental.pallas import tpu as pltpu
from jax.sharding import PartitionSpec as P

MESH = pl.DeviceIdType.MESH
VMEM_SPEC = pl.BlockSpec(memory_space=pltpu.VMEM)
ANY_SPEC = pl.BlockSpec(memory_space=pl.ANY)


def pair_slot(source, target):
    return (0, 3, 5)[source] + target - source - 1


def _barrier(axis, n, me):
    barrier = pltpu.get_barrier_semaphore()
    for d in range(1, n):
        pl.semaphore_signal(barrier, 1, device_id={axis: (me + d) % n}, device_id_type=MESH)
    pl.semaphore_wait(barrier, n - 1)


def _params(cid):
    return pltpu.CompilerParams(collective_id=cid, has_side_effects=True)


def reduce_scatter(x, own_part, axis, cid, wire):
    n = x.shape[0]

    def kernel(x_ref, own_ref, o_ref, recv, ssem, rsem):
        me = lax.axis_index(axis)
        _barrier(axis, n, me)
        copies = []
        for d in range(1, n):
            peer = (me + d) % n
            copy = pltpu.make_async_remote_copy(
                x_ref.at[peer], recv.at[d - 1], ssem.at[d - 1], rsem.at[d - 1],
                device_id={axis: peer}, device_id_type=MESH)
            copy.start()
            copies.append(copy)
        for copy in copies:
            copy.wait()
        total = own_ref[...]
        for d in range(n - 1):
            total = total + recv[d].astype(jnp.float32)
        o_ref[...] = total

    return pl.pallas_call(
        kernel,
        out_shape=jax.ShapeDtypeStruct(x.shape[1:], jnp.float32),
        in_specs=[VMEM_SPEC, VMEM_SPEC],
        out_specs=VMEM_SPEC,
        scratch_shapes=[
            pltpu.VMEM((n - 1,) + x.shape[1:], wire),
            pltpu.SemaphoreType.DMA((n - 1,)),
            pltpu.SemaphoreType.DMA((n - 1,)),
        ],
        compiler_params=_params(cid),
    )(x, own_part)


def all_gather(x, axis, n, cid):
    def kernel(x_ref, o_ref, ssem, rsem):
        me = lax.axis_index(axis)
        _barrier(axis, n, me)
        copies = []
        for d in range(1, n):
            peer = (me + d) % n
            copy = pltpu.make_async_remote_copy(
                x_ref, o_ref.at[me], ssem.at[d - 1], rsem.at[d - 1],
                device_id={axis: peer}, device_id_type=MESH)
            copy.start()
            copies.append(copy)
        o_ref[me] = x_ref[...]
        for copy in copies:
            copy.wait()

    return pl.pallas_call(
        kernel,
        out_shape=jax.ShapeDtypeStruct((n,) + x.shape, x.dtype),
        in_specs=[VMEM_SPEC],
        out_specs=VMEM_SPEC,
        scratch_shapes=[
            pltpu.SemaphoreType.DMA((n - 1,)),
            pltpu.SemaphoreType.DMA((n - 1,)),
        ],
        compiler_params=_params(cid),
    )(x)


def all_reduce(x, axis, cid):
    n = x.shape[0]

    def kernel(x_ref, o_ref, recv, part, ssem, rsem, gsem, hsem):
        me = lax.axis_index(axis)
        _barrier(axis, n, me)
        copies = []
        for d in range(1, n):
            peer = (me + d) % n
            copy = pltpu.make_async_remote_copy(
                x_ref.at[peer], recv.at[d - 1], ssem.at[d - 1], rsem.at[d - 1],
                device_id={axis: peer}, device_id_type=MESH)
            copy.start()
            copies.append(copy)
        for copy in copies:
            copy.wait()
        total = x_ref[me]
        for d in range(n - 1):
            total = total + recv[d]
        part[...] = total
        o_ref[me] = total
        copies = []
        for d in range(1, n):
            peer = (me + d) % n
            copy = pltpu.make_async_remote_copy(
                part, o_ref.at[me], gsem.at[d - 1], hsem.at[d - 1],
                device_id={axis: peer}, device_id_type=MESH)
            copy.start()
            copies.append(copy)
        for copy in copies:
            copy.wait()

    return pl.pallas_call(
        kernel,
        out_shape=jax.ShapeDtypeStruct(x.shape, x.dtype),
        in_specs=[VMEM_SPEC],
        out_specs=VMEM_SPEC,
        scratch_shapes=[
            pltpu.VMEM((n - 1,) + x.shape[1:], x.dtype),
            pltpu.VMEM(x.shape[1:], x.dtype),
            pltpu.SemaphoreType.DMA((n - 1,)),
            pltpu.SemaphoreType.DMA((n - 1,)),
            pltpu.SemaphoreType.DMA((n - 1,)),
            pltpu.SemaphoreType.DMA((n - 1,)),
        ],
        compiler_params=_params(cid),
    )(x)


def _grid_barrier_signals(barrier, g, p, q):
    for dp in range(g):
        for dq in range(g):
            if dp or dq:
                pl.semaphore_signal(
                    barrier, 1, device_id={"prow": (p + dp) % g, "pcol": (q + dq) % g},
                    device_id_type=MESH)


def _permute_start(x_ref, o_ref, forward, ssem, rsem, lsem):
    g = x_ref.shape[1]
    p = lax.axis_index("prow")
    q = lax.axis_index("pcol")
    own = p == q
    slot = q if forward else p
    sends = []
    local = pltpu.make_async_copy(x_ref.at[:, p], o_ref.at[:, p], lsem)
    for dj in range(g):
        j = (p + dj) % g
        dest = {"prow": j, "pcol": p} if forward else {"prow": q, "pcol": j}
        copy = pltpu.make_async_remote_copy(
            x_ref.at[:, j], o_ref.at[:, slot], ssem.at[dj], rsem.at[slot],
            device_id=dest, device_id_type=MESH)
        if dj == 0:
            @pl.when(own)
            def _():
                local.start()

            @pl.when(jnp.logical_not(own))
            def _():
                copy.start()
        else:
            copy.start()
        sends.append(copy)

    def wait():
        for dj in range(g):
            s = (p + dj) % g
            arrival = pltpu.make_async_copy(x_ref.at[:, s], o_ref.at[:, s], rsem.at[s])
            if dj == 0:
                @pl.when(own)
                def _():
                    local.wait()

                @pl.when(jnp.logical_not(own))
                def _():
                    sends[0].wait_send()
                    arrival.wait()
            else:
                sends[dj].wait_send()
                arrival.wait()

    return wait


def _permute_scratch(g):
    return [pltpu.SemaphoreType.DMA((g,)), pltpu.SemaphoreType.DMA((g,)), pltpu.SemaphoreType.DMA(())]


def permute_rows(x, forward, cid):
    g = x.shape[1]

    def kernel(x_ref, o_ref, ssem, rsem, lsem):
        p = lax.axis_index("prow")
        q = lax.axis_index("pcol")
        barrier = pltpu.get_barrier_semaphore()
        _grid_barrier_signals(barrier, g, p, q)
        pl.semaphore_wait(barrier, g * g - 1)
        _permute_start(x_ref, o_ref, forward, ssem, rsem, lsem)()

    return pl.pallas_call(
        kernel,
        out_shape=jax.ShapeDtypeStruct(x.shape, x.dtype),
        in_specs=[VMEM_SPEC],
        out_specs=VMEM_SPEC,
        scratch_shapes=_permute_scratch(g),
        compiler_params=_params(cid),
    )(x)


def root_exchange(chunks, forest, root_in, cid):
    n = chunks.shape[0]
    g = forest.shape[1]
    axis = "layer"

    def kernel(x_ref, f_ref, r_ref, o_ref, fo_ref, ro_ref, recv, part,
               ssem, rsem, gsem, hsem, fs, fr, fl, rs, rr, rl):
        me = lax.axis_index(axis)
        p = lax.axis_index("prow")
        q = lax.axis_index("pcol")
        barrier = pltpu.get_barrier_semaphore()
        for d in range(1, n):
            pl.semaphore_signal(barrier, 1, device_id={axis: (me + d) % n}, device_id_type=MESH)
        _grid_barrier_signals(barrier, g, p, q)
        pl.semaphore_wait(barrier, n - 1 + g * g - 1)
        root_wait = _permute_start(r_ref, ro_ref, True, rs, rr, rl)
        forest_wait = _permute_start(f_ref, fo_ref, False, fs, fr, fl)
        copies = []
        for d in range(1, n):
            peer = (me + d) % n
            copy = pltpu.make_async_remote_copy(
                x_ref.at[peer], recv.at[d - 1], ssem.at[d - 1], rsem.at[d - 1],
                device_id={axis: peer}, device_id_type=MESH)
            copy.start()
            copies.append(copy)
        for copy in copies:
            copy.wait()
        total = x_ref[me]
        for d in range(n - 1):
            total = total + recv[d]
        part[...] = total
        o_ref[me] = total
        copies = []
        for d in range(1, n):
            peer = (me + d) % n
            copy = pltpu.make_async_remote_copy(
                part, o_ref.at[me], gsem.at[d - 1], hsem.at[d - 1],
                device_id={axis: peer}, device_id_type=MESH)
            copy.start()
            copies.append(copy)
        for copy in copies:
            copy.wait()
        root_wait()
        forest_wait()

    return pl.pallas_call(
        kernel,
        out_shape=(
            jax.ShapeDtypeStruct(chunks.shape, chunks.dtype),
            jax.ShapeDtypeStruct(forest.shape, forest.dtype),
            jax.ShapeDtypeStruct(root_in.shape, root_in.dtype),
        ),
        in_specs=[VMEM_SPEC] * 3,
        out_specs=(VMEM_SPEC,) * 3,
        scratch_shapes=[
            pltpu.VMEM((n - 1,) + chunks.shape[1:], chunks.dtype),
            pltpu.VMEM(chunks.shape[1:], chunks.dtype),
            pltpu.SemaphoreType.DMA((n - 1,)),
            pltpu.SemaphoreType.DMA((n - 1,)),
            pltpu.SemaphoreType.DMA((n - 1,)),
            pltpu.SemaphoreType.DMA((n - 1,)),
        ] + _permute_scratch(g) + _permute_scratch(g),
        compiler_params=_params(cid),
    )(chunks, forest, root_in)


def solve_all(local_forest, local_root, factors, pattern, inverses, root_inverse, n_layer, cid):
    levels, g, slice_rows, cols = local_forest.shape
    rows = g * slice_rows
    f32, bf16 = jnp.float32, jnp.bfloat16
    def kernel(f_ref, r_ref, w_hbm, pat_ref, inv_hbm, rinv_hbm, fo_ref, ro_ref,
               placed, placed_root, sol, root_sol, gath, tot, sb, rrecv,
               recv_a, sbuf, recv_b, tbuf, recv_1, part, full, w_ref, inv_ref, rinv_ref, load_sems,
               gs, gr, rs_s, rs_r, a_sem, b_send, b_recv, c1_send, c1_recv, hs, hr, *perm_sems):
        p = lax.axis_index("prow")
        q = lax.axis_index("pcol")
        me = lax.axis_index("layer")
        perm = [perm_sems[3 * i:3 * i + 3] for i in range(levels + 4)]
        loads = [pltpu.make_async_copy(src, dst, load_sems.at[i]) for i, (src, dst) in
                 enumerate(((inv_hbm, inv_ref), (w_hbm, w_ref), (rinv_hbm, rinv_ref)))]
        for load in loads:
            load.start()
        barrier = pltpu.get_barrier_semaphore()
        _grid_barrier_signals(barrier, g, p, q)
        for d in range(1, n_layer):
            pl.semaphore_signal(barrier, 1, device_id={"layer": (me + d) % n_layer},
                                device_id_type=MESH)
        pl.semaphore_wait(barrier, g * g - 1 + n_layer - 1)
        first_in = _permute_start(f_ref.at[pl.ds(0, 1)], placed.at[pl.ds(0, 1)], True, *perm[0])
        rest_in = _permute_start(f_ref.at[pl.ds(1, levels - 1)], placed.at[pl.ds(1, levels - 1)],
                                 True, *perm[levels + 3])
        tot[...] = jnp.zeros(tot.shape, f32)
        first_in()
        pending = []
        outs = []
        loads[0].wait()
        for t in range(levels):
            if t == 1:
                rest_in()
            rhs = placed[t].reshape(rows, cols).astype(f32)
            if t > 0:
                for copy in pending:
                    copy.wait()
                red = tot[t - 1, q]
                for d in range(g - 1):
                    red = red + rrecv[t - 1, d].astype(f32)
                rhs = rhs - red
            ans = jnp.dot(inv_ref[t], rhs, precision=lax.Precision.HIGHEST,
                          preferred_element_type=f32).astype(bf16)
            sol[t] = ans.reshape(g, slice_rows, cols)
            gath[t, p] = ans
            copies = []
            for d in range(1, g):
                copy = pltpu.make_async_remote_copy(
                    gath.at[t, p], gath.at[t, p], gs.at[t, d - 1], gr.at[t, d - 1],
                    device_id={"prow": (p + d) % g}, device_id_type=MESH)
                copy.start()
                copies.append(copy)
            outs.append(_permute_start(sol.at[pl.ds(t, 1)], fo_ref.at[pl.ds(t, 1)], False,
                                       *perm[3 + t]))
            for copy in copies:
                copy.wait()
            if t == 0:
                loads[1].wait()
            for target in range(t + 1, levels + 1):
                pair = pair_slot(t, target)

                def body(j, carry, t=t, target=target, pair=pair):
                    acc = tot[target - 1, j]
                    for z in range(g):
                        present = pat_ref[pair, j, z].astype(f32).astype(bf16)
                        acc = acc + jnp.dot(w_ref[pair, j, z] * present, gath[t, z],
                                            preferred_element_type=f32)
                    tot[target - 1, j] = acc
                    return carry

                lax.fori_loop(0, g, body, 0)
                if target == t + 1 and target < levels:
                    pending = []
                    sb[t] = tot[t].astype(bf16)
                    for d in range(1, g):
                        peer = (q + d) % g
                        copy = pltpu.make_async_remote_copy(
                            sb.at[t, peer], rrecv.at[t, d - 1], rs_s.at[t, d - 1],
                            rs_r.at[t, d - 1], device_id={"pcol": peer}, device_id_type=MESH)
                        copy.start()
                        pending.append(copy)
                if t == 0 and target == t + 1:
                    root_in = _permute_start(r_ref, placed_root, True, *perm[1])
        core = me % 2
        half = g // 2
        copy = pltpu.make_async_remote_copy(
            tot.at[levels - 1, pl.ds((1 - core) * half, half)], recv_a, a_sem.at[0], a_sem.at[1],
            device_id={"layer": me + 1 - 2 * core}, device_id_type=MESH)
        copy.start()
        copy.wait()
        sbuf[...] = tot[levels - 1, pl.ds(core * half, half)] + recv_a[...]
        holder = q // half == core
        for k in range(half):
            j = core * half + k
            off = (j - q + g) % g
            copy = pltpu.make_async_remote_copy(
                sbuf.at[k], recv_b.at[off], b_send.at[k], b_recv.at[off],
                device_id={"pcol": j}, device_id_type=MESH)

            @pl.when(j != q)
            def _(copy=copy):
                copy.start()
                copy.wait_send()

        n_h = n_layer // 2
        m = me // 2
        c_rows = rows // n_h
        mine = pl.ds(pl.multiple_of(m * c_rows, 8), c_rows)

        @pl.when(holder)
        def _():
            for off in range(1, g):
                pltpu.make_async_copy(sbuf.at[0], recv_b.at[off], b_recv.at[off]).wait()
            t_sum = sbuf[q - core * half]
            for off in range(1, g):
                t_sum = t_sum + recv_b[off]
            tbuf[...] = t_sum
            copies = []
            for dm in range(1, n_h):
                pm = (m + dm) % n_h
                copy = pltpu.make_async_remote_copy(
                    tbuf.at[pl.ds(pl.multiple_of(pm * c_rows, 8), c_rows)], recv_1.at[dm - 1],
                    c1_send.at[dm - 1], c1_recv.at[dm - 1],
                    device_id={"layer": 2 * pm + core}, device_id_type=MESH)
                copy.start()
                copies.append(copy)
            for copy in copies:
                copy.wait()
            total = tbuf[mine]
            for dm in range(n_h - 1):
                total = total + recv_1[dm]
            part[...] = total
            full[mine] = total
            copies = []
            for dm in range(1, n_h):
                pm = (m + dm) % n_h
                copy = pltpu.make_async_remote_copy(
                    part, full.at[mine], hs.at[dm - 1], hr.at[m],
                    device_id={"layer": 2 * pm + core}, device_id_type=MESH)
                copy.start()
                copies.append(copy)
            for copy in copies:
                copy.wait_send()
            for dm in range(1, n_h):
                mm = (m + dm) % n_h
                pltpu.make_async_copy(
                    part, full.at[pl.ds(pl.multiple_of(mm * c_rows, 8), c_rows)], hr.at[mm]).wait()
            copy = pltpu.make_async_remote_copy(
                full, full, hs.at[n_layer - 2], hr.at[n_h],
                device_id={"layer": me + 1 - 2 * core}, device_id_type=MESH)
            copy.start()
            copy.wait_send()

        @pl.when(jnp.logical_not(holder))
        def _():
            pltpu.make_async_copy(full, full, hr.at[n_h]).wait()
        root_in()
        loads[2].wait()
        side = placed_root[0].reshape(rows, cols).astype(f32) - full[...]
        answer = jnp.dot(rinv_ref[...], side, precision=lax.Precision.HIGHEST,
                         preferred_element_type=f32).astype(bf16)
        root_sol[0] = answer.reshape(g, slice_rows, cols)
        root_out = _permute_start(root_sol, ro_ref, False, *perm[2])
        for wait in outs:
            wait()
        root_out()

    return pl.pallas_call(
        kernel,
        out_shape=(
            jax.ShapeDtypeStruct(local_forest.shape, bf16),
            jax.ShapeDtypeStruct(local_root.shape, bf16),
        ),
        in_specs=[ANY_SPEC, ANY_SPEC, ANY_SPEC,
                  pl.BlockSpec(memory_space=pltpu.SMEM), ANY_SPEC, ANY_SPEC],
        out_specs=(VMEM_SPEC,) * 2,
        scratch_shapes=[
            pltpu.VMEM(local_forest.shape, bf16),
            pltpu.VMEM(local_root.shape, bf16),
            pltpu.VMEM(local_forest.shape, bf16),
            pltpu.VMEM(local_root.shape, bf16),
            pltpu.VMEM((levels, g, rows, cols), bf16),
            pltpu.VMEM((levels, g, rows, cols), f32),
            pltpu.VMEM((levels - 1, g, rows, cols), bf16),
            pltpu.VMEM((levels - 1, g - 1, rows, cols), bf16),
            pltpu.VMEM((g // 2, rows, cols), f32),
            pltpu.VMEM((g // 2, rows, cols), f32),
            pltpu.VMEM((g, rows, cols), f32),
            pltpu.VMEM((rows, cols), f32),
            pltpu.VMEM((max(n_layer // 2 - 1, 1), rows // (n_layer // 2), cols), f32),
            pltpu.VMEM((rows // (n_layer // 2), cols), f32),
            pltpu.VMEM((rows, cols), f32),
            pltpu.VMEM(factors.shape, factors.dtype),
            pltpu.VMEM(inverses.shape, f32),
            pltpu.VMEM(root_inverse.shape, f32),
            pltpu.SemaphoreType.DMA((3,)),
            pltpu.SemaphoreType.DMA((levels, g - 1)),
            pltpu.SemaphoreType.DMA((levels, g - 1)),
            pltpu.SemaphoreType.DMA((levels, g - 1)),
            pltpu.SemaphoreType.DMA((levels, g - 1)),
            pltpu.SemaphoreType.DMA((2,)),
            pltpu.SemaphoreType.DMA((g // 2,)),
            pltpu.SemaphoreType.DMA((g,)),
            pltpu.SemaphoreType.DMA((max(n_layer // 2 - 1, 1),)),
            pltpu.SemaphoreType.DMA((max(n_layer // 2 - 1, 1),)),
            pltpu.SemaphoreType.DMA((n_layer - 1,)),
            pltpu.SemaphoreType.DMA((n_layer // 2 + 1,)),
        ] + _permute_scratch(g) * (levels + 4),
        compiler_params=_params(cid),
    )(local_forest, local_root, factors, pattern, inverses, root_inverse)


def shards(subtree_right_hand, root_rhs, blocks, pattern, forest_inverse, root_inverse):
    grid_size = lax.axis_size("prow")
    n_layer = lax.axis_size("layer")
    super_rows = blocks.shape[-1]
    rhs_cols = subtree_right_hand.shape[-1]
    slice_rows = super_rows // grid_size
    local_forest = subtree_right_hand.reshape(3, grid_size, slice_rows, rhs_cols)
    local_root = root_rhs.reshape(1, grid_size, slice_rows, rhs_cols)
    factors = blocks.reshape(6, grid_size, grid_size, super_rows, super_rows)
    present = pattern.reshape(6, grid_size, grid_size)
    inverses = forest_inverse.reshape(3, super_rows, super_rows)
    forest_back, root_back = solve_all(
        local_forest, local_root, factors, present, inverses,
        root_inverse.reshape(super_rows, super_rows), n_layer, 10)
    forest_out = forest_back.reshape(1, 3 * super_rows, rhs_cols)
    root_out = root_back.reshape(super_rows, rhs_cols)
    return (forest_out, root_out)


def solution(mesh):
    placed = (
        P("layer", ("prow", "pcol"), None),
        P(("prow", "pcol"), None),
        P("layer", None, "prow", "pcol", None, None, None, None),
        P("layer", None, "prow", "pcol", None, None),
        P("layer", None, "prow", "pcol", None, None),
        P("prow", "pcol", None, None),
    )
    return jax.shard_map(
        shards,
        mesh=mesh,
        in_specs=placed,
        out_specs=(P("layer", ("prow", "pcol"), None), P(("prow", "pcol"), None)),
        check_vma=False,
    )
```

```python
import jax
import jax.numpy as jnp
from jax import lax
from jax.experimental import pallas as pl
from jax.experimental.pallas import tpu as pltpu
from jax.sharding import PartitionSpec as P

MESH = pl.DeviceIdType.MESH
VMEM_SPEC = pl.BlockSpec(memory_space=pltpu.VMEM)
ANY_SPEC = pl.BlockSpec(memory_space=pl.ANY)


def pair_slot(source, target):
    return (0, 3, 5)[source] + target - source - 1


def _barrier(axis, n, me):
    barrier = pltpu.get_barrier_semaphore()
    for d in range(1, n):
        pl.semaphore_signal(barrier, 1, device_id={axis: (me + d) % n}, device_id_type=MESH)
    pl.semaphore_wait(barrier, n - 1)


def _params(cid):
    return pltpu.CompilerParams(collective_id=cid, has_side_effects=True)


def reduce_scatter(x, own_part, axis, cid, wire):
    n = x.shape[0]

    def kernel(x_ref, own_ref, o_ref, recv, ssem, rsem):
        me = lax.axis_index(axis)
        _barrier(axis, n, me)
        copies = []
        for d in range(1, n):
            peer = (me + d) % n
            copy = pltpu.make_async_remote_copy(
                x_ref.at[peer], recv.at[d - 1], ssem.at[d - 1], rsem.at[d - 1],
                device_id={axis: peer}, device_id_type=MESH)
            copy.start()
            copies.append(copy)
        for copy in copies:
            copy.wait()
        total = own_ref[...]
        for d in range(n - 1):
            total = total + recv[d].astype(jnp.float32)
        o_ref[...] = total

    return pl.pallas_call(
        kernel,
        out_shape=jax.ShapeDtypeStruct(x.shape[1:], jnp.float32),
        in_specs=[VMEM_SPEC, VMEM_SPEC],
        out_specs=VMEM_SPEC,
        scratch_shapes=[
            pltpu.VMEM((n - 1,) + x.shape[1:], wire),
            pltpu.SemaphoreType.DMA((n - 1,)),
            pltpu.SemaphoreType.DMA((n - 1,)),
        ],
        compiler_params=_params(cid),
    )(x, own_part)


def all_gather(x, axis, n, cid):
    def kernel(x_ref, o_ref, ssem, rsem):
        me = lax.axis_index(axis)
        _barrier(axis, n, me)
        copies = []
        for d in range(1, n):
            peer = (me + d) % n
            copy = pltpu.make_async_remote_copy(
                x_ref, o_ref.at[me], ssem.at[d - 1], rsem.at[d - 1],
                device_id={axis: peer}, device_id_type=MESH)
            copy.start()
            copies.append(copy)
        o_ref[me] = x_ref[...]
        for copy in copies:
            copy.wait()

    return pl.pallas_call(
        kernel,
        out_shape=jax.ShapeDtypeStruct((n,) + x.shape, x.dtype),
        in_specs=[VMEM_SPEC],
        out_specs=VMEM_SPEC,
        scratch_shapes=[
            pltpu.SemaphoreType.DMA((n - 1,)),
            pltpu.SemaphoreType.DMA((n - 1,)),
        ],
        compiler_params=_params(cid),
    )(x)


def all_reduce(x, axis, cid):
    n = x.shape[0]

    def kernel(x_ref, o_ref, recv, part, ssem, rsem, gsem, hsem):
        me = lax.axis_index(axis)
        _barrier(axis, n, me)
        copies = []
        for d in range(1, n):
            peer = (me + d) % n
            copy = pltpu.make_async_remote_copy(
                x_ref.at[peer], recv.at[d - 1], ssem.at[d - 1], rsem.at[d - 1],
                device_id={axis: peer}, device_id_type=MESH)
            copy.start()
            copies.append(copy)
        for copy in copies:
            copy.wait()
        total = x_ref[me]
        for d in range(n - 1):
            total = total + recv[d]
        part[...] = total
        o_ref[me] = total
        copies = []
        for d in range(1, n):
            peer = (me + d) % n
            copy = pltpu.make_async_remote_copy(
                part, o_ref.at[me], gsem.at[d - 1], hsem.at[d - 1],
                device_id={axis: peer}, device_id_type=MESH)
            copy.start()
            copies.append(copy)
        for copy in copies:
            copy.wait()

    return pl.pallas_call(
        kernel,
        out_shape=jax.ShapeDtypeStruct(x.shape, x.dtype),
        in_specs=[VMEM_SPEC],
        out_specs=VMEM_SPEC,
        scratch_shapes=[
            pltpu.VMEM((n - 1,) + x.shape[1:], x.dtype),
            pltpu.VMEM(x.shape[1:], x.dtype),
            pltpu.SemaphoreType.DMA((n - 1,)),
            pltpu.SemaphoreType.DMA((n - 1,)),
            pltpu.SemaphoreType.DMA((n - 1,)),
            pltpu.SemaphoreType.DMA((n - 1,)),
        ],
        compiler_params=_params(cid),
    )(x)


def _grid_barrier_signals(barrier, g, p, q):
    for dp in range(g):
        for dq in range(g):
            if dp or dq:
                pl.semaphore_signal(
                    barrier, 1, device_id={"prow": (p + dp) % g, "pcol": (q + dq) % g},
                    device_id_type=MESH)


def _permute_start(x_ref, o_ref, forward, ssem, rsem, lsem):
    g = x_ref.shape[1]
    p = lax.axis_index("prow")
    q = lax.axis_index("pcol")
    own = p == q
    slot = q if forward else p
    sends = []
    local = pltpu.make_async_copy(x_ref.at[:, p], o_ref.at[:, p], lsem)
    for dj in range(g):
        j = (p + dj) % g
        dest = {"prow": j, "pcol": p} if forward else {"prow": q, "pcol": j}
        copy = pltpu.make_async_remote_copy(
            x_ref.at[:, j], o_ref.at[:, slot], ssem.at[dj], rsem.at[slot],
            device_id=dest, device_id_type=MESH)
        if dj == 0:
            @pl.when(own)
            def _():
                local.start()

            @pl.when(jnp.logical_not(own))
            def _():
                copy.start()
        else:
            copy.start()
        sends.append(copy)

    def wait():
        for dj in range(g):
            s = (p + dj) % g
            arrival = pltpu.make_async_copy(x_ref.at[:, s], o_ref.at[:, s], rsem.at[s])
            if dj == 0:
                @pl.when(own)
                def _():
                    local.wait()

                @pl.when(jnp.logical_not(own))
                def _():
                    sends[0].wait_send()
                    arrival.wait()
            else:
                sends[dj].wait_send()
                arrival.wait()

    return wait


def _permute_scratch(g):
    return [pltpu.SemaphoreType.DMA((g,)), pltpu.SemaphoreType.DMA((g,)), pltpu.SemaphoreType.DMA(())]


def permute_rows(x, forward, cid):
    g = x.shape[1]

    def kernel(x_ref, o_ref, ssem, rsem, lsem):
        p = lax.axis_index("prow")
        q = lax.axis_index("pcol")
        barrier = pltpu.get_barrier_semaphore()
        _grid_barrier_signals(barrier, g, p, q)
        pl.semaphore_wait(barrier, g * g - 1)
        _permute_start(x_ref, o_ref, forward, ssem, rsem, lsem)()

    return pl.pallas_call(
        kernel,
        out_shape=jax.ShapeDtypeStruct(x.shape, x.dtype),
        in_specs=[VMEM_SPEC],
        out_specs=VMEM_SPEC,
        scratch_shapes=_permute_scratch(g),
        compiler_params=_params(cid),
    )(x)


def root_exchange(chunks, forest, root_in, cid):
    n = chunks.shape[0]
    g = forest.shape[1]
    axis = "layer"

    def kernel(x_ref, f_ref, r_ref, o_ref, fo_ref, ro_ref, recv, part,
               ssem, rsem, gsem, hsem, fs, fr, fl, rs, rr, rl):
        me = lax.axis_index(axis)
        p = lax.axis_index("prow")
        q = lax.axis_index("pcol")
        barrier = pltpu.get_barrier_semaphore()
        for d in range(1, n):
            pl.semaphore_signal(barrier, 1, device_id={axis: (me + d) % n}, device_id_type=MESH)
        _grid_barrier_signals(barrier, g, p, q)
        pl.semaphore_wait(barrier, n - 1 + g * g - 1)
        root_wait = _permute_start(r_ref, ro_ref, True, rs, rr, rl)
        forest_wait = _permute_start(f_ref, fo_ref, False, fs, fr, fl)
        copies = []
        for d in range(1, n):
            peer = (me + d) % n
            copy = pltpu.make_async_remote_copy(
                x_ref.at[peer], recv.at[d - 1], ssem.at[d - 1], rsem.at[d - 1],
                device_id={axis: peer}, device_id_type=MESH)
            copy.start()
            copies.append(copy)
        for copy in copies:
            copy.wait()
        total = x_ref[me]
        for d in range(n - 1):
            total = total + recv[d]
        part[...] = total
        o_ref[me] = total
        copies = []
        for d in range(1, n):
            peer = (me + d) % n
            copy = pltpu.make_async_remote_copy(
                part, o_ref.at[me], gsem.at[d - 1], hsem.at[d - 1],
                device_id={axis: peer}, device_id_type=MESH)
            copy.start()
            copies.append(copy)
        for copy in copies:
            copy.wait()
        root_wait()
        forest_wait()

    return pl.pallas_call(
        kernel,
        out_shape=(
            jax.ShapeDtypeStruct(chunks.shape, chunks.dtype),
            jax.ShapeDtypeStruct(forest.shape, forest.dtype),
            jax.ShapeDtypeStruct(root_in.shape, root_in.dtype),
        ),
        in_specs=[VMEM_SPEC] * 3,
        out_specs=(VMEM_SPEC,) * 3,
        scratch_shapes=[
            pltpu.VMEM((n - 1,) + chunks.shape[1:], chunks.dtype),
            pltpu.VMEM(chunks.shape[1:], chunks.dtype),
            pltpu.SemaphoreType.DMA((n - 1,)),
            pltpu.SemaphoreType.DMA((n - 1,)),
            pltpu.SemaphoreType.DMA((n - 1,)),
            pltpu.SemaphoreType.DMA((n - 1,)),
        ] + _permute_scratch(g) + _permute_scratch(g),
        compiler_params=_params(cid),
    )(chunks, forest, root_in)


def solve_all(local_forest, local_root, factors, pattern, inverses, root_inverse, n_layer, cid):
    levels, g, slice_rows, cols = local_forest.shape
    rows = g * slice_rows
    f32, bf16 = jnp.float32, jnp.bfloat16
    def kernel(f_ref, r_ref, w_hbm, pat_ref, inv_hbm, rinv_hbm, fo_ref, ro_ref,
               placed, placed_root, sol, root_sol, gath, tot, sb, rrecv,
               recv_a, sbuf, recv_b, tbuf, recv_1, part, full, w_ref, inv_ref, rinv_ref, load_sems,
               gs, gr, rs_s, rs_r, a_sem, b_send, b_recv, c1_send, c1_recv, hs, hr, *perm_sems):
        p = lax.axis_index("prow")
        q = lax.axis_index("pcol")
        me = lax.axis_index("layer")
        perm = [perm_sems[3 * i:3 * i + 3] for i in range(levels + 4)]
        loads = [pltpu.make_async_copy(src, dst, load_sems.at[i]) for i, (src, dst) in
                 enumerate(((inv_hbm, inv_ref), (w_hbm, w_ref), (rinv_hbm, rinv_ref)))]
        for load in loads:
            load.start()
        barrier = pltpu.get_barrier_semaphore()
        _grid_barrier_signals(barrier, g, p, q)
        for d in range(1, n_layer):
            pl.semaphore_signal(barrier, 1, device_id={"layer": (me + d) % n_layer},
                                device_id_type=MESH)
        pl.semaphore_wait(barrier, g * g - 1 + n_layer - 1)
        first_in = _permute_start(f_ref.at[pl.ds(0, 1)], placed.at[pl.ds(0, 1)], True, *perm[0])
        rest_in = _permute_start(f_ref.at[pl.ds(1, levels - 1)], placed.at[pl.ds(1, levels - 1)],
                                 True, *perm[levels + 3])
        tot[...] = jnp.zeros(tot.shape, f32)
        first_in()
        pending = []
        outs = []
        loads[0].wait()
        for t in range(levels):
            if t == 1:
                rest_in()
            rhs = placed[t].reshape(rows, cols).astype(f32)
            if t > 0:
                for copy in pending:
                    copy.wait()
                red = tot[t - 1, q]
                for d in range(g - 1):
                    red = red + rrecv[t - 1, d].astype(f32)
                rhs = rhs - red
            ans = jnp.dot(inv_ref[t], rhs, precision=lax.Precision.HIGHEST,
                          preferred_element_type=f32).astype(bf16)
            sol[t] = ans.reshape(g, slice_rows, cols)
            gath[t, p] = ans
            copies = []
            for d in range(1, g):
                copy = pltpu.make_async_remote_copy(
                    gath.at[t, p], gath.at[t, p], gs.at[t, d - 1], gr.at[t, d - 1],
                    device_id={"prow": (p + d) % g}, device_id_type=MESH)
                copy.start()
                copies.append(copy)
            outs.append(_permute_start(sol.at[pl.ds(t, 1)], fo_ref.at[pl.ds(t, 1)], False,
                                       *perm[3 + t]))
            for copy in copies:
                copy.wait()
            if t == 0:
                loads[1].wait()
            for target in range(t + 1, levels + 1):
                pair = pair_slot(t, target)

                def body(j, carry, t=t, target=target, pair=pair):
                    acc = tot[target - 1, j]
                    for z in range(g):
                        present = pat_ref[pair, j, z].astype(f32).astype(bf16)
                        acc = acc + jnp.dot(w_ref[pair, j, z] * present, gath[t, z],
                                            preferred_element_type=f32)
                    tot[target - 1, j] = acc
                    return carry

                lax.fori_loop(0, g, body, 0)
                if target == t + 1 and target < levels:
                    pending = []
                    sb[t] = tot[t].astype(bf16)
                    for d in range(1, g):
                        peer = (q + d) % g
                        copy = pltpu.make_async_remote_copy(
                            sb.at[t, peer], rrecv.at[t, d - 1], rs_s.at[t, d - 1],
                            rs_r.at[t, d - 1], device_id={"pcol": peer}, device_id_type=MESH)
                        copy.start()
                        pending.append(copy)
                if t == 0 and target == t + 1:
                    root_in = _permute_start(r_ref, placed_root, True, *perm[1])
        core = me % 2
        half = g // 2
        exchanges = []
        for k in range(half):
            copy = pltpu.make_async_remote_copy(
                tot.at[levels - 1, (1 - core) * half + k], recv_a.at[k],
                a_sem.at[2 * k], a_sem.at[2 * k + 1],
                device_id={"layer": me + 1 - 2 * core}, device_id_type=MESH)
            copy.start()
            exchanges.append(copy)
        holder = q // half == core
        sends = []
        for k in range(half):
            exchanges[k].wait()
            sbuf[k] = tot[levels - 1, core * half + k] + recv_a[k]
            j = core * half + k
            off = (j - q + g) % g
            copy = pltpu.make_async_remote_copy(
                sbuf.at[k], recv_b.at[off], b_send.at[k], b_recv.at[off],
                device_id={"pcol": j}, device_id_type=MESH)

            @pl.when(j != q)
            def _(copy=copy):
                copy.start()

            sends.append((copy, j))
        for copy, j in sends:
            @pl.when(j != q)
            def _(copy=copy):
                copy.wait_send()

        n_h = n_layer // 2
        m = me // 2
        c_rows = rows // n_h
        mine = pl.ds(pl.multiple_of(m * c_rows, 8), c_rows)

        @pl.when(holder)
        def _():
            for off in range(1, g):
                pltpu.make_async_copy(sbuf.at[0], recv_b.at[off], b_recv.at[off]).wait()
            t_sum = sbuf[q - core * half]
            for off in range(1, g):
                t_sum = t_sum + recv_b[off]
            tbuf[...] = t_sum
            copies = []
            for dm in range(1, n_h):
                pm = (m + dm) % n_h
                copy = pltpu.make_async_remote_copy(
                    tbuf.at[pl.ds(pl.multiple_of(pm * c_rows, 8), c_rows)], recv_1.at[dm - 1],
                    c1_send.at[dm - 1], c1_recv.at[dm - 1],
                    device_id={"layer": 2 * pm + core}, device_id_type=MESH)
                copy.start()
                copies.append(copy)
            for copy in copies:
                copy.wait()
            total = tbuf[mine]
            for dm in range(n_h - 1):
                total = total + recv_1[dm]
            part[...] = total
            full[mine] = total
            copies = []
            for dm in range(1, n_h):
                pm = (m + dm) % n_h
                copy = pltpu.make_async_remote_copy(
                    part, full.at[mine], hs.at[dm - 1], hr.at[m],
                    device_id={"layer": 2 * pm + core}, device_id_type=MESH)
                copy.start()
                copies.append(copy)
            for copy in copies:
                copy.wait_send()
            for dm in range(1, n_h):
                mm = (m + dm) % n_h
                pltpu.make_async_copy(
                    part, full.at[pl.ds(pl.multiple_of(mm * c_rows, 8), c_rows)], hr.at[mm]).wait()
            copy = pltpu.make_async_remote_copy(
                full, full, hs.at[n_layer - 2], hr.at[n_h],
                device_id={"layer": me + 1 - 2 * core}, device_id_type=MESH)
            copy.start()
            copy.wait_send()

        @pl.when(jnp.logical_not(holder))
        def _():
            pltpu.make_async_copy(full, full, hr.at[n_h]).wait()
        root_in()
        loads[2].wait()
        side = placed_root[0].reshape(rows, cols).astype(f32) - full[...]
        answer = jnp.dot(rinv_ref[...], side, precision=lax.Precision.HIGHEST,
                         preferred_element_type=f32).astype(bf16)
        root_sol[0] = answer.reshape(g, slice_rows, cols)
        root_out = _permute_start(root_sol, ro_ref, False, *perm[2])
        for wait in outs:
            wait()
        root_out()

    return pl.pallas_call(
        kernel,
        out_shape=(
            jax.ShapeDtypeStruct(local_forest.shape, bf16),
            jax.ShapeDtypeStruct(local_root.shape, bf16),
        ),
        in_specs=[ANY_SPEC, ANY_SPEC, ANY_SPEC,
                  pl.BlockSpec(memory_space=pltpu.SMEM), ANY_SPEC, ANY_SPEC],
        out_specs=(VMEM_SPEC,) * 2,
        scratch_shapes=[
            pltpu.VMEM(local_forest.shape, bf16),
            pltpu.VMEM(local_root.shape, bf16),
            pltpu.VMEM(local_forest.shape, bf16),
            pltpu.VMEM(local_root.shape, bf16),
            pltpu.VMEM((levels, g, rows, cols), bf16),
            pltpu.VMEM((levels, g, rows, cols), f32),
            pltpu.VMEM((levels - 1, g, rows, cols), bf16),
            pltpu.VMEM((levels - 1, g - 1, rows, cols), bf16),
            pltpu.VMEM((g // 2, rows, cols), f32),
            pltpu.VMEM((g // 2, rows, cols), f32),
            pltpu.VMEM((g, rows, cols), f32),
            pltpu.VMEM((rows, cols), f32),
            pltpu.VMEM((max(n_layer // 2 - 1, 1), rows // (n_layer // 2), cols), f32),
            pltpu.VMEM((rows // (n_layer // 2), cols), f32),
            pltpu.VMEM((rows, cols), f32),
            pltpu.VMEM(factors.shape, factors.dtype),
            pltpu.VMEM(inverses.shape, f32),
            pltpu.VMEM(root_inverse.shape, f32),
            pltpu.SemaphoreType.DMA((3,)),
            pltpu.SemaphoreType.DMA((levels, g - 1)),
            pltpu.SemaphoreType.DMA((levels, g - 1)),
            pltpu.SemaphoreType.DMA((levels, g - 1)),
            pltpu.SemaphoreType.DMA((levels, g - 1)),
            pltpu.SemaphoreType.DMA((g,)),
            pltpu.SemaphoreType.DMA((g // 2,)),
            pltpu.SemaphoreType.DMA((g,)),
            pltpu.SemaphoreType.DMA((max(n_layer // 2 - 1, 1),)),
            pltpu.SemaphoreType.DMA((max(n_layer // 2 - 1, 1),)),
            pltpu.SemaphoreType.DMA((n_layer - 1,)),
            pltpu.SemaphoreType.DMA((n_layer // 2 + 1,)),
        ] + _permute_scratch(g) * (levels + 4),
        compiler_params=_params(cid),
    )(local_forest, local_root, factors, pattern, inverses, root_inverse)


def shards(subtree_right_hand, root_rhs, blocks, pattern, forest_inverse, root_inverse):
    grid_size = lax.axis_size("prow")
    n_layer = lax.axis_size("layer")
    super_rows = blocks.shape[-1]
    rhs_cols = subtree_right_hand.shape[-1]
    slice_rows = super_rows // grid_size
    local_forest = subtree_right_hand.reshape(3, grid_size, slice_rows, rhs_cols)
    local_root = root_rhs.reshape(1, grid_size, slice_rows, rhs_cols)
    factors = blocks.reshape(6, grid_size, grid_size, super_rows, super_rows)
    present = pattern.reshape(6, grid_size, grid_size)
    inverses = forest_inverse.reshape(3, super_rows, super_rows)
    forest_back, root_back = solve_all(
        local_forest, local_root, factors, present, inverses,
        root_inverse.reshape(super_rows, super_rows), n_layer, 10)
    forest_out = forest_back.reshape(1, 3 * super_rows, rhs_cols)
    root_out = root_back.reshape(super_rows, rhs_cols)
    return (forest_out, root_out)


def solution(mesh):
    placed = (
        P("layer", ("prow", "pcol"), None),
        P(("prow", "pcol"), None),
        P("layer", None, "prow", "pcol", None, None, None, None),
        P("layer", None, "prow", "pcol", None, None),
        P("layer", None, "prow", "pcol", None, None),
        P("prow", "pcol", None, None),
    )
    return jax.shard_map(
        shards,
        mesh=mesh,
        in_specs=placed,
        out_specs=(P("layer", ("prow", "pcol"), None), P(("prow", "pcol"), None)),
        check_vma=False,
    )
```

```python
import jax
import jax.numpy as jnp
from jax import lax
from jax.experimental import pallas as pl
from jax.experimental.pallas import tpu as pltpu
from jax.sharding import PartitionSpec as P

MESH = pl.DeviceIdType.MESH
VMEM_SPEC = pl.BlockSpec(memory_space=pltpu.VMEM)
ANY_SPEC = pl.BlockSpec(memory_space=pl.ANY)


def pair_slot(source, target):
    return (0, 3, 5)[source] + target - source - 1


def _barrier(axis, n, me):
    barrier = pltpu.get_barrier_semaphore()
    for d in range(1, n):
        pl.semaphore_signal(barrier, 1, device_id={axis: (me + d) % n}, device_id_type=MESH)
    pl.semaphore_wait(barrier, n - 1)


def _params(cid):
    return pltpu.CompilerParams(collective_id=cid, has_side_effects=True)


def reduce_scatter(x, own_part, axis, cid, wire):
    n = x.shape[0]

    def kernel(x_ref, own_ref, o_ref, recv, ssem, rsem):
        me = lax.axis_index(axis)
        _barrier(axis, n, me)
        copies = []
        for d in range(1, n):
            peer = (me + d) % n
            copy = pltpu.make_async_remote_copy(
                x_ref.at[peer], recv.at[d - 1], ssem.at[d - 1], rsem.at[d - 1],
                device_id={axis: peer}, device_id_type=MESH)
            copy.start()
            copies.append(copy)
        for copy in copies:
            copy.wait()
        total = own_ref[...]
        for d in range(n - 1):
            total = total + recv[d].astype(jnp.float32)
        o_ref[...] = total

    return pl.pallas_call(
        kernel,
        out_shape=jax.ShapeDtypeStruct(x.shape[1:], jnp.float32),
        in_specs=[VMEM_SPEC, VMEM_SPEC],
        out_specs=VMEM_SPEC,
        scratch_shapes=[
            pltpu.VMEM((n - 1,) + x.shape[1:], wire),
            pltpu.SemaphoreType.DMA((n - 1,)),
            pltpu.SemaphoreType.DMA((n - 1,)),
        ],
        compiler_params=_params(cid),
    )(x, own_part)


def all_gather(x, axis, n, cid):
    def kernel(x_ref, o_ref, ssem, rsem):
        me = lax.axis_index(axis)
        _barrier(axis, n, me)
        copies = []
        for d in range(1, n):
            peer = (me + d) % n
            copy = pltpu.make_async_remote_copy(
                x_ref, o_ref.at[me], ssem.at[d - 1], rsem.at[d - 1],
                device_id={axis: peer}, device_id_type=MESH)
            copy.start()
            copies.append(copy)
        o_ref[me] = x_ref[...]
        for copy in copies:
            copy.wait()

    return pl.pallas_call(
        kernel,
        out_shape=jax.ShapeDtypeStruct((n,) + x.shape, x.dtype),
        in_specs=[VMEM_SPEC],
        out_specs=VMEM_SPEC,
        scratch_shapes=[
            pltpu.SemaphoreType.DMA((n - 1,)),
            pltpu.SemaphoreType.DMA((n - 1,)),
        ],
        compiler_params=_params(cid),
    )(x)


def all_reduce(x, axis, cid):
    n = x.shape[0]

    def kernel(x_ref, o_ref, recv, part, ssem, rsem, gsem, hsem):
        me = lax.axis_index(axis)
        _barrier(axis, n, me)
        copies = []
        for d in range(1, n):
            peer = (me + d) % n
            copy = pltpu.make_async_remote_copy(
                x_ref.at[peer], recv.at[d - 1], ssem.at[d - 1], rsem.at[d - 1],
                device_id={axis: peer}, device_id_type=MESH)
            copy.start()
            copies.append(copy)
        for copy in copies:
            copy.wait()
        total = x_ref[me]
        for d in range(n - 1):
            total = total + recv[d]
        part[...] = total
        o_ref[me] = total
        copies = []
        for d in range(1, n):
            peer = (me + d) % n
            copy = pltpu.make_async_remote_copy(
                part, o_ref.at[me], gsem.at[d - 1], hsem.at[d - 1],
                device_id={axis: peer}, device_id_type=MESH)
            copy.start()
            copies.append(copy)
        for copy in copies:
            copy.wait()

    return pl.pallas_call(
        kernel,
        out_shape=jax.ShapeDtypeStruct(x.shape, x.dtype),
        in_specs=[VMEM_SPEC],
        out_specs=VMEM_SPEC,
        scratch_shapes=[
            pltpu.VMEM((n - 1,) + x.shape[1:], x.dtype),
            pltpu.VMEM(x.shape[1:], x.dtype),
            pltpu.SemaphoreType.DMA((n - 1,)),
            pltpu.SemaphoreType.DMA((n - 1,)),
            pltpu.SemaphoreType.DMA((n - 1,)),
            pltpu.SemaphoreType.DMA((n - 1,)),
        ],
        compiler_params=_params(cid),
    )(x)


def _grid_barrier_signals(barrier, g, p, q):
    for dp in range(g):
        for dq in range(g):
            if dp or dq:
                pl.semaphore_signal(
                    barrier, 1, device_id={"prow": (p + dp) % g, "pcol": (q + dq) % g},
                    device_id_type=MESH)


def _permute_start(x_ref, o_ref, forward, ssem, rsem, lsem):
    g = x_ref.shape[1]
    p = lax.axis_index("prow")
    q = lax.axis_index("pcol")
    own = p == q
    slot = q if forward else p
    sends = []
    local = pltpu.make_async_copy(x_ref.at[:, p], o_ref.at[:, p], lsem)
    for dj in range(g):
        j = (p + dj) % g
        dest = {"prow": j, "pcol": p} if forward else {"prow": q, "pcol": j}
        copy = pltpu.make_async_remote_copy(
            x_ref.at[:, j], o_ref.at[:, slot], ssem.at[dj], rsem.at[slot],
            device_id=dest, device_id_type=MESH)
        if dj == 0:
            @pl.when(own)
            def _():
                local.start()

            @pl.when(jnp.logical_not(own))
            def _():
                copy.start()
        else:
            copy.start()
        sends.append(copy)

    def wait():
        for dj in range(g):
            s = (p + dj) % g
            arrival = pltpu.make_async_copy(x_ref.at[:, s], o_ref.at[:, s], rsem.at[s])
            if dj == 0:
                @pl.when(own)
                def _():
                    local.wait()

                @pl.when(jnp.logical_not(own))
                def _():
                    sends[0].wait_send()
                    arrival.wait()
            else:
                sends[dj].wait_send()
                arrival.wait()

    return wait


def _permute_scratch(g):
    return [pltpu.SemaphoreType.DMA((g,)), pltpu.SemaphoreType.DMA((g,)), pltpu.SemaphoreType.DMA(())]


def permute_rows(x, forward, cid):
    g = x.shape[1]

    def kernel(x_ref, o_ref, ssem, rsem, lsem):
        p = lax.axis_index("prow")
        q = lax.axis_index("pcol")
        barrier = pltpu.get_barrier_semaphore()
        _grid_barrier_signals(barrier, g, p, q)
        pl.semaphore_wait(barrier, g * g - 1)
        _permute_start(x_ref, o_ref, forward, ssem, rsem, lsem)()

    return pl.pallas_call(
        kernel,
        out_shape=jax.ShapeDtypeStruct(x.shape, x.dtype),
        in_specs=[VMEM_SPEC],
        out_specs=VMEM_SPEC,
        scratch_shapes=_permute_scratch(g),
        compiler_params=_params(cid),
    )(x)


def root_exchange(chunks, forest, root_in, cid):
    n = chunks.shape[0]
    g = forest.shape[1]
    axis = "layer"

    def kernel(x_ref, f_ref, r_ref, o_ref, fo_ref, ro_ref, recv, part,
               ssem, rsem, gsem, hsem, fs, fr, fl, rs, rr, rl):
        me = lax.axis_index(axis)
        p = lax.axis_index("prow")
        q = lax.axis_index("pcol")
        barrier = pltpu.get_barrier_semaphore()
        for d in range(1, n):
            pl.semaphore_signal(barrier, 1, device_id={axis: (me + d) % n}, device_id_type=MESH)
        _grid_barrier_signals(barrier, g, p, q)
        pl.semaphore_wait(barrier, n - 1 + g * g - 1)
        root_wait = _permute_start(r_ref, ro_ref, True, rs, rr, rl)
        forest_wait = _permute_start(f_ref, fo_ref, False, fs, fr, fl)
        copies = []
        for d in range(1, n):
            peer = (me + d) % n
            copy = pltpu.make_async_remote_copy(
                x_ref.at[peer], recv.at[d - 1], ssem.at[d - 1], rsem.at[d - 1],
                device_id={axis: peer}, device_id_type=MESH)
            copy.start()
            copies.append(copy)
        for copy in copies:
            copy.wait()
        total = x_ref[me]
        for d in range(n - 1):
            total = total + recv[d]
        part[...] = total
        o_ref[me] = total
        copies = []
        for d in range(1, n):
            peer = (me + d) % n
            copy = pltpu.make_async_remote_copy(
                part, o_ref.at[me], gsem.at[d - 1], hsem.at[d - 1],
                device_id={axis: peer}, device_id_type=MESH)
            copy.start()
            copies.append(copy)
        for copy in copies:
            copy.wait()
        root_wait()
        forest_wait()

    return pl.pallas_call(
        kernel,
        out_shape=(
            jax.ShapeDtypeStruct(chunks.shape, chunks.dtype),
            jax.ShapeDtypeStruct(forest.shape, forest.dtype),
            jax.ShapeDtypeStruct(root_in.shape, root_in.dtype),
        ),
        in_specs=[VMEM_SPEC] * 3,
        out_specs=(VMEM_SPEC,) * 3,
        scratch_shapes=[
            pltpu.VMEM((n - 1,) + chunks.shape[1:], chunks.dtype),
            pltpu.VMEM(chunks.shape[1:], chunks.dtype),
            pltpu.SemaphoreType.DMA((n - 1,)),
            pltpu.SemaphoreType.DMA((n - 1,)),
            pltpu.SemaphoreType.DMA((n - 1,)),
            pltpu.SemaphoreType.DMA((n - 1,)),
        ] + _permute_scratch(g) + _permute_scratch(g),
        compiler_params=_params(cid),
    )(chunks, forest, root_in)


def solve_all(local_forest, local_root, factors, pattern, inverses, root_inverse, n_layer, cid):
    levels, g, slice_rows, cols = local_forest.shape
    rows = g * slice_rows
    f32, bf16 = jnp.float32, jnp.bfloat16
    def kernel(f_ref, r_ref, w_hbm, pat_ref, inv_hbm, rinv_hbm, fo_ref, ro_ref,
               placed, placed_root, sol, root_sol, gath, tot, sb, rrecv,
               recv_a, sbuf, recv_b, tbuf, recv_1, part, full, w_ref, inv_ref, rinv_ref, load_sems,
               gs, gr, rs_s, rs_r, a_sem, b_send, b_recv, c1_send, c1_recv, hs, hr, *perm_sems):
        p = lax.axis_index("prow")
        q = lax.axis_index("pcol")
        me = lax.axis_index("layer")
        perm = [perm_sems[3 * i:3 * i + 3] for i in range(levels + 4)]
        loads = [pltpu.make_async_copy(src, dst, load_sems.at[i]) for i, (src, dst) in
                 enumerate(((inv_hbm, inv_ref), (w_hbm, w_ref), (rinv_hbm, rinv_ref)))]
        for load in loads:
            load.start()
        barrier = pltpu.get_barrier_semaphore()
        _grid_barrier_signals(barrier, g, p, q)
        for d in range(1, n_layer):
            pl.semaphore_signal(barrier, 1, device_id={"layer": (me + d) % n_layer},
                                device_id_type=MESH)
        pl.semaphore_wait(barrier, g * g - 1 + n_layer - 1)
        first_in = _permute_start(f_ref.at[pl.ds(0, 1)], placed.at[pl.ds(0, 1)], True, *perm[0])
        rest_in = _permute_start(f_ref.at[pl.ds(1, levels - 1)], placed.at[pl.ds(1, levels - 1)],
                                 True, *perm[levels + 3])
        tot[...] = jnp.zeros(tot.shape, f32)
        first_in()
        pending = []
        outs = []
        loads[0].wait()
        for t in range(levels):
            if t == 1:
                rest_in()
            rhs = placed[t].reshape(rows, cols).astype(f32)
            if t > 0:
                for copy in pending:
                    copy.wait()
                red = tot[t - 1, q]
                for d in range(g - 1):
                    red = red + rrecv[t - 1, d].astype(f32)
                rhs = rhs - red
            ans = jnp.dot(inv_ref[t], rhs, precision=lax.Precision.HIGHEST,
                          preferred_element_type=f32).astype(bf16)
            sol[t] = ans.reshape(g, slice_rows, cols)
            gath[t, p] = ans
            copies = []
            for d in range(1, g):
                copy = pltpu.make_async_remote_copy(
                    gath.at[t, p], gath.at[t, p], gs.at[t, d - 1], gr.at[t, d - 1],
                    device_id={"prow": (p + d) % g}, device_id_type=MESH)
                copy.start()
                copies.append(copy)
            outs.append(_permute_start(sol.at[pl.ds(t, 1)], fo_ref.at[pl.ds(t, 1)], False,
                                       *perm[3 + t]))
            for copy in copies:
                copy.wait()
            if t == 0:
                loads[1].wait()
            for target in range(t + 1, levels + 1):
                pair = pair_slot(t, target)

                def body(j, carry, t=t, target=target, pair=pair):
                    acc = tot[target - 1, j]
                    for z in range(g):
                        present = pat_ref[pair, j, z].astype(f32).astype(bf16)
                        acc = acc + jnp.dot(w_ref[pair, j, z] * present, gath[t, z],
                                            preferred_element_type=f32)
                    tot[target - 1, j] = acc
                    return carry

                lax.fori_loop(0, g, body, 0)
                if target == t + 1 and target < levels:
                    pending = []
                    for d in range(1, g):
                        peer = (q + d) % g
                        sb[t, peer] = tot[t, peer].astype(bf16)
                        copy = pltpu.make_async_remote_copy(
                            sb.at[t, peer], rrecv.at[t, d - 1], rs_s.at[t, d - 1],
                            rs_r.at[t, d - 1], device_id={"pcol": peer}, device_id_type=MESH)
                        copy.start()
                        pending.append(copy)
                if t == 0 and target == t + 1:
                    root_in = _permute_start(r_ref, placed_root, True, *perm[1])
        core = me % 2
        half = g // 2
        exchanges = []
        for k in range(half):
            copy = pltpu.make_async_remote_copy(
                tot.at[levels - 1, (1 - core) * half + k], recv_a.at[k],
                a_sem.at[2 * k], a_sem.at[2 * k + 1],
                device_id={"layer": me + 1 - 2 * core}, device_id_type=MESH)
            copy.start()
            exchanges.append(copy)
        holder = q // half == core
        sends = []
        for k in range(half):
            exchanges[k].wait()
            sbuf[k] = tot[levels - 1, core * half + k] + recv_a[k]
            j = core * half + k
            off = (j - q + g) % g
            copy = pltpu.make_async_remote_copy(
                sbuf.at[k], recv_b.at[off], b_send.at[k], b_recv.at[off],
                device_id={"pcol": j}, device_id_type=MESH)

            @pl.when(j != q)
            def _(copy=copy):
                copy.start()

            sends.append((copy, j))
        for copy, j in sends:
            @pl.when(j != q)
            def _(copy=copy):
                copy.wait_send()

        n_h = n_layer // 2
        m = me // 2
        c_rows = rows // n_h
        mine = pl.ds(pl.multiple_of(m * c_rows, 8), c_rows)

        @pl.when(holder)
        def _():
            for off in range(1, g):
                pltpu.make_async_copy(sbuf.at[0], recv_b.at[off], b_recv.at[off]).wait()
            t_sum = sbuf[q - core * half]
            for off in range(1, g):
                t_sum = t_sum + recv_b[off]
            tbuf[...] = t_sum
            copies = []
            for dm in range(1, n_h):
                pm = (m + dm) % n_h
                copy = pltpu.make_async_remote_copy(
                    tbuf.at[pl.ds(pl.multiple_of(pm * c_rows, 8), c_rows)], recv_1.at[dm - 1],
                    c1_send.at[dm - 1], c1_recv.at[dm - 1],
                    device_id={"layer": 2 * pm + core}, device_id_type=MESH)
                copy.start()
                copies.append(copy)
            for copy in copies:
                copy.wait()
            total = tbuf[mine]
            for dm in range(n_h - 1):
                total = total + recv_1[dm]
            part[...] = total
            full[mine] = total
            copies = []
            for dm in range(1, n_h):
                pm = (m + dm) % n_h
                copy = pltpu.make_async_remote_copy(
                    part, full.at[mine], hs.at[dm - 1], hr.at[m],
                    device_id={"layer": 2 * pm + core}, device_id_type=MESH)
                copy.start()
                copies.append(copy)
            for copy in copies:
                copy.wait_send()
            for dm in range(1, n_h):
                mm = (m + dm) % n_h
                pltpu.make_async_copy(
                    part, full.at[pl.ds(pl.multiple_of(mm * c_rows, 8), c_rows)], hr.at[mm]).wait()
            copy = pltpu.make_async_remote_copy(
                full, full, hs.at[n_layer - 2], hr.at[n_h],
                device_id={"layer": me + 1 - 2 * core}, device_id_type=MESH)
            copy.start()
            copy.wait_send()

        @pl.when(jnp.logical_not(holder))
        def _():
            pltpu.make_async_copy(full, full, hr.at[n_h]).wait()
        root_in()
        loads[2].wait()
        side = placed_root[0].reshape(rows, cols).astype(f32) - full[...]
        answer = jnp.dot(rinv_ref[...], side, precision=lax.Precision.HIGHEST,
                         preferred_element_type=f32).astype(bf16)
        root_sol[0] = answer.reshape(g, slice_rows, cols)
        root_out = _permute_start(root_sol, ro_ref, False, *perm[2])
        for wait in outs:
            wait()
        root_out()

    return pl.pallas_call(
        kernel,
        out_shape=(
            jax.ShapeDtypeStruct(local_forest.shape, bf16),
            jax.ShapeDtypeStruct(local_root.shape, bf16),
        ),
        in_specs=[ANY_SPEC, ANY_SPEC, ANY_SPEC,
                  pl.BlockSpec(memory_space=pltpu.SMEM), ANY_SPEC, ANY_SPEC],
        out_specs=(VMEM_SPEC,) * 2,
        scratch_shapes=[
            pltpu.VMEM(local_forest.shape, bf16),
            pltpu.VMEM(local_root.shape, bf16),
            pltpu.VMEM(local_forest.shape, bf16),
            pltpu.VMEM(local_root.shape, bf16),
            pltpu.VMEM((levels, g, rows, cols), bf16),
            pltpu.VMEM((levels, g, rows, cols), f32),
            pltpu.VMEM((levels - 1, g, rows, cols), bf16),
            pltpu.VMEM((levels - 1, g - 1, rows, cols), bf16),
            pltpu.VMEM((g // 2, rows, cols), f32),
            pltpu.VMEM((g // 2, rows, cols), f32),
            pltpu.VMEM((g, rows, cols), f32),
            pltpu.VMEM((rows, cols), f32),
            pltpu.VMEM((max(n_layer // 2 - 1, 1), rows // (n_layer // 2), cols), f32),
            pltpu.VMEM((rows // (n_layer // 2), cols), f32),
            pltpu.VMEM((rows, cols), f32),
            pltpu.VMEM(factors.shape, factors.dtype),
            pltpu.VMEM(inverses.shape, f32),
            pltpu.VMEM(root_inverse.shape, f32),
            pltpu.SemaphoreType.DMA((3,)),
            pltpu.SemaphoreType.DMA((levels, g - 1)),
            pltpu.SemaphoreType.DMA((levels, g - 1)),
            pltpu.SemaphoreType.DMA((levels, g - 1)),
            pltpu.SemaphoreType.DMA((levels, g - 1)),
            pltpu.SemaphoreType.DMA((g,)),
            pltpu.SemaphoreType.DMA((g // 2,)),
            pltpu.SemaphoreType.DMA((g,)),
            pltpu.SemaphoreType.DMA((max(n_layer // 2 - 1, 1),)),
            pltpu.SemaphoreType.DMA((max(n_layer // 2 - 1, 1),)),
            pltpu.SemaphoreType.DMA((n_layer - 1,)),
            pltpu.SemaphoreType.DMA((n_layer // 2 + 1,)),
        ] + _permute_scratch(g) * (levels + 4),
        compiler_params=_params(cid),
    )(local_forest, local_root, factors, pattern, inverses, root_inverse)


def shards(subtree_right_hand, root_rhs, blocks, pattern, forest_inverse, root_inverse):
    grid_size = lax.axis_size("prow")
    n_layer = lax.axis_size("layer")
    super_rows = blocks.shape[-1]
    rhs_cols = subtree_right_hand.shape[-1]
    slice_rows = super_rows // grid_size
    local_forest = subtree_right_hand.reshape(3, grid_size, slice_rows, rhs_cols)
    local_root = root_rhs.reshape(1, grid_size, slice_rows, rhs_cols)
    factors = blocks.reshape(6, grid_size, grid_size, super_rows, super_rows)
    present = pattern.reshape(6, grid_size, grid_size)
    inverses = forest_inverse.reshape(3, super_rows, super_rows)
    forest_back, root_back = solve_all(
        local_forest, local_root, factors, present, inverses,
        root_inverse.reshape(super_rows, super_rows), n_layer, 10)
    forest_out = forest_back.reshape(1, 3 * super_rows, rhs_cols)
    root_out = root_back.reshape(super_rows, rhs_cols)
    return (forest_out, root_out)


def solution(mesh):
    placed = (
        P("layer", ("prow", "pcol"), None),
        P(("prow", "pcol"), None),
        P("layer", None, "prow", "pcol", None, None, None, None),
        P("layer", None, "prow", "pcol", None, None),
        P("layer", None, "prow", "pcol", None, None),
        P("prow", "pcol", None, None),
    )
    return jax.shard_map(
        shards,
        mesh=mesh,
        in_specs=placed,
        out_specs=(P("layer", ("prow", "pcol"), None), P(("prow", "pcol"), None)),
        check_vma=False,
    )
```
